128 devices in a mesh: ctx: 16 (over z, y_lo, core), ch: 8 (over y_hi, x).
Axes of the slice: x: 4, y: 4 (y_hi: 2, y_lo: 2; y = y_hi * 2 + y_lo), z: 4, core: 2. Of those that a mesh axis runs over, the one named last changes fastest.
Arguments:
- tokens: bfloat16 [2048, 8192], P('ctx', 'ch'), may hold values from -6 to 6
- w_in: bfloat16 [8192, 3, 4096], P('ctx', None, 'ch'), may hold values from -0.0625 to 0.0625
- short_filter: float32 [3, 3, 4096], P(None, None, 'ch'), may hold values from -3 to 3
- decay_rate: float32 [256, 16], P('ch'), may hold values from 0.00024414062 to 0.1
- residue: float32 [256, 16], P('ch'), may hold values from -1.5 to 1.5
- skip: float32 [4096], P('ch'), may hold values from -6 to 6
Outputs:
- block_out: bfloat16 [2048, 4096], P('ctx', 'ch')
The draws below stay inside these ranges and needn't reach their ends.
All inputs are finite; a program needn't handle non-finite values.
Results may differ from the reference program's by a relative error of at most 0.011.
Values may be sent and summed in bfloat16 or wider, within the bound.
A program may use at most 128 MiB of HBM per device.

```python
import math
import jax
import jax.numpy as jnp
from jax import lax

D = 8192
CH = 4096
GROUP = 16
ORDER = 16
SEQ = 2048
FILTERS = 256


def levels(stream_key, extent, shards, low, high):
    gain = 1.0
    for position, parts in shards:
        heights = jax.random.uniform(jax.random.fold_in(jax.random.fold_in(stream_key, 6), position), (parts,), jnp.float32, low / len(shards), high / len(shards))
        gain = gain * jnp.repeat(jnp.exp(heights), extent[position] // parts).reshape((-1,) + (1,) * (len(extent) - 1 - position))
    return gain


def gaussian(stream_key, dims, spread, bound, cuts=(), dtype=jnp.bfloat16):
    array = spread * jax.random.normal(stream_key, dims, jnp.float32)
    if cuts:
        array = array * levels(stream_key, dims, cuts, -0.22, 0.18)
    return jnp.clip(array, -bound, bound).astype(dtype)


def setup_inputs(seed: int = 0) -> dict:
    key_list = jax.random.split(jax.random.key(seed), 7)
    tokens = gaussian(key_list[0], (SEQ, D), 1.0, 6.0, ((0, 16), (1, 8)))
    w_in = gaussian(key_list[1], (D, 3, CH), D ** -0.5, 0.0625, ((0, 16), (2, 8)))
    short_filter = gaussian(key_list[2], (3, 3, CH), 0.6, 3.0, ((2, 8),), jnp.float32)
    decay_rate = jnp.clip(jnp.exp(math.log(0.1) - 6.015181 * jax.random.uniform(key_list[3], (FILTERS, ORDER), jnp.float32) ** levels(key_list[3], (FILTERS, ORDER), ((0, 8),), -0.2, 0.2)), 0.00024414062, 0.1)
    residue = gaussian(key_list[4], (FILTERS, ORDER), 0.25, 1.5, ((0, 8),), jnp.float32)
    skip = gaussian(key_list[5], (CH,), 1.0, 6.0, ((0, 8),), jnp.float32)
    return dict(tokens=tokens, w_in=w_in, short_filter=short_filter, decay_rate=decay_rate, residue=residue, skip=skip)


def reference(tokens, w_in, short_filter, decay_rate, residue, skip):
    flat_weight = w_in.reshape(D, 3 * CH).astype(jnp.float32)
    projected = jnp.dot(tokens.astype(jnp.float32), flat_weight, precision=lax.Precision.HIGHEST)
    rounded = lax.optimization_barrier(projected.astype(jnp.bfloat16))
    proj_all = rounded.astype(jnp.float32).reshape(SEQ, 3, CH)
    padded_rows = jnp.concatenate([jnp.zeros((2, 3, CH), jnp.float32), proj_all], axis=0)
    short_mixed = short_filter[0] * padded_rows[2:] + short_filter[1] * padded_rows[1:-1] + short_filter[2] * padded_rows[:-2]
    query_part = short_mixed[:, 0]
    key_part = short_mixed[:, 1]
    value_part = short_mixed[:, 2]
    gated_input = (key_part * value_part).astype(jnp.bfloat16).astype(jnp.float32)
    pole_weight = residue * jnp.sqrt(2.0 * decay_rate)
    lag_index = jnp.arange(SEQ).astype(jnp.float32)
    filter_rows = jnp.einsum('fr,frl->fl', pole_weight, jnp.exp(-decay_rate[:, :, None] * lag_index[None, None, :]), precision=lax.Precision.HIGHEST)
    per_channel = jnp.repeat(filter_rows, GROUP, axis=0).T
    fft_len = 2 * SEQ
    long_out = jnp.fft.irfft(jnp.fft.rfft(gated_input, fft_len, axis=0) * jnp.fft.rfft(per_channel, fft_len, axis=0), fft_len, axis=0)[:SEQ]
    return (query_part * (long_out + skip * gated_input)).astype(jnp.bfloat16)
```

```python
import jax
import jax.numpy as jnp
from jax import lax
from jax.sharding import Mesh
from jax.sharding import PartitionSpec as P

GROUP = 16
HIGH = lax.Precision.HIGHEST


def split_bf16(x):
    hi = x.astype(jnp.bfloat16)
    lo = (x - hi.astype(jnp.float32)).astype(jnp.bfloat16)
    return hi, lo


def dot_split(spec, weight, data):
    hi, lo = split_bf16(weight)
    return jnp.einsum(spec, hi, data, preferred_element_type=jnp.float32) + jnp.einsum(
        spec, lo, data, preferred_element_type=jnp.float32
    )


def local(tokens, w_in, short_filter, decay_rate, residue, skip):
    n_chip = lax.axis_size("p")
    block_len = tokens.shape[0]
    local_width = w_in.shape[2]
    group_count = local_width // GROUP
    chip = lax.axis_index("p")
    core = lax.axis_index("c")
    col = lax.axis_index("ch")

    pairs = [(p * n_chip + m, m * n_chip + p) for p in range(n_chip) for m in range(n_chip)]
    moved = lax.ppermute(tokens, ("p", "ch"), pairs)
    tok_t = lax.all_gather(moved, "ch", axis=0, tiled=False)
    w_chip = lax.all_gather(w_in, "c", axis=0, tiled=True)
    flat_w = w_chip.reshape(w_chip.shape[0], -1)

    tail = tok_t[:, block_len - 2 :]
    partner_tail = lax.ppermute(tail, "c", [(0, 1), (1, 0)])
    shifted_tail = jnp.concatenate([jnp.zeros_like(partner_tail[:1]), partner_tail[:-1]], axis=0)
    prior = jnp.where(core == 1, partner_tail, shifted_tail)
    tok_ext = jnp.concatenate([prior, tok_t], axis=1)
    n_blk, ext_len = tok_ext.shape[0], tok_ext.shape[1]
    partial = jnp.dot(
        tok_ext.reshape(n_blk * ext_len, -1), flat_w, preferred_element_type=jnp.float32
    ).reshape(n_blk, ext_len, -1)
    proj = lax.psum_scatter(partial, "p", scatter_dimension=0, tiled=False)
    first = jnp.logical_and(chip == 0, core == 0)
    row_id = lax.broadcasted_iota(jnp.int32, proj.shape, 0)
    proj = jnp.where(jnp.logical_and(first, row_id < 2), 0.0, proj)
    proj = proj.astype(jnp.bfloat16).astype(jnp.float32).reshape(ext_len, 3, local_width)
    mixed = (
        short_filter[0] * proj[2:]
        + short_filter[1] * proj[1:-1]
        + short_filter[2] * proj[:-2]
    )
    query = mixed[:, 0]
    gated = (mixed[:, 1] * mixed[:, 2]).astype(jnp.bfloat16)
    x = gated.reshape(block_len, group_count, GROUP)

    pole_weight = residue * jnp.sqrt(2.0 * decay_rate)
    pos = jnp.arange(block_len, dtype=jnp.float32)
    lam = decay_rate[:, None, :]
    a_mat = pole_weight[:, None, :] * jnp.exp(-lam * pos[None, :, None])
    b_mat = jnp.exp(lam * pos[None, :, None])
    toep = jnp.einsum("gtr,gsr->gts", a_mat, b_mat, precision=HIGH)
    causal = pos[:, None] >= pos[None, :]
    toep = jnp.where(causal[None], toep, 0.0)
    near = dot_split("gts,sgc->tgc", toep, x)

    e_mat = jnp.exp(-lam * (block_len - 1 - pos)[None, :, None])
    s_loc = dot_split("gsr,sgc->grc", e_mat, x)
    s_all = lax.all_gather(s_loc, ("p", "c"), axis=0, tiled=False)
    me = chip * lax.axis_size("c") + core
    k_idx = jnp.arange(s_all.shape[0])
    gap = (me - 1 - k_idx).astype(jnp.float32)
    decay = jnp.where(
        gap[:, None, None] >= 0.0,
        jnp.exp(-decay_rate[None] * (block_len * jnp.maximum(gap, 0.0))[:, None, None]),
        0.0,
    )
    s_in = jnp.einsum("kgr,kgrc->grc", decay, s_all, precision=HIGH)
    f_mat = pole_weight[:, None, :] * jnp.exp(-lam * (pos + 1.0)[None, :, None])
    far = jnp.einsum("gtr,grc->tgc", f_mat, s_in, precision=HIGH)
    long_out = (near + far).reshape(block_len, local_width)
    out = query * (long_out + skip * gated.astype(jnp.float32))
    return out.astype(jnp.bfloat16)


def solution(mesh):
    n_ctx, n_ch = mesh.devices.shape
    sub = Mesh(mesh.devices.reshape(n_ctx // 2, 2, n_ch), ("p", "c", "ch"))
    ctx = ("p", "c")
    return jax.shard_map(
        local,
        mesh=sub,
        in_specs=(
            P(ctx, "ch"),
            P(ctx, None, "ch"),
            P(None, None, "ch"),
            P("ch", None),
            P("ch", None),
            P("ch"),
        ),
        out_specs=P(ctx, "ch"),
        check_vma=False,
    )
```

```python
import jax
import jax.numpy as jnp
from jax import lax
from jax.sharding import Mesh
from jax.sharding import PartitionSpec as P

GROUP = 16
HIGH = lax.Precision.HIGHEST


def split_bf16(x):
    hi = x.astype(jnp.bfloat16)
    lo = (x - hi.astype(jnp.float32)).astype(jnp.bfloat16)
    return hi, lo


def dot_split(spec, weight, data):
    hi, lo = split_bf16(weight)
    return jnp.einsum(spec, hi, data, preferred_element_type=jnp.float32) + jnp.einsum(
        spec, lo, data, preferred_element_type=jnp.float32
    )


def local(tokens, w_in, short_filter, decay_rate, residue, skip):
    n_chip = lax.axis_size("p")
    block_len = tokens.shape[0]
    local_width = w_in.shape[2]
    group_count = local_width // GROUP
    chip = lax.axis_index("p")
    core = lax.axis_index("c")
    col = lax.axis_index("ch")

    n_col = lax.axis_size("ch")
    pieces = []
    for k in range(n_col):
        pairs = [(p * n_col + m, m * n_col + (p + k) % n_col) for p in range(n_chip) for m in range(n_col)]
        pieces.append(lax.ppermute(tokens, ("p", "ch"), pairs))
    stacked = jnp.stack(pieces)
    src = (col - jnp.arange(n_col)) % n_col
    order = jnp.argsort(src)
    tok_t = jnp.take(stacked, order, axis=0)
    w_flat = w_in.reshape(w_in.shape[0], -1)
    w_other = lax.ppermute(w_flat, "c", [(0, 1), (1, 0)])
    flat_w = jnp.where(
        core == 0,
        jnp.concatenate([w_flat, w_other], axis=0),
        jnp.concatenate([w_other, w_flat], axis=0),
    )

    tail = tok_t[:, block_len - 2 :]
    partner_tail = lax.ppermute(tail, "c", [(0, 1), (1, 0)])
    shifted_tail = jnp.concatenate([jnp.zeros_like(partner_tail[:1]), partner_tail[:-1]], axis=0)
    prior = jnp.where(core == 1, partner_tail, shifted_tail)
    tok_ext = jnp.concatenate([prior, tok_t], axis=1)
    n_blk, ext_len = tok_ext.shape[0], tok_ext.shape[1]
    partial = jnp.dot(
        tok_ext.reshape(n_blk * ext_len, -1), flat_w, preferred_element_type=jnp.float32
    ).reshape(n_blk, ext_len, -1)
    proj = lax.psum_scatter(
        partial.astype(jnp.bfloat16), "p", scatter_dimension=0, tiled=False
    ).astype(jnp.float32)
    first = jnp.logical_and(chip == 0, core == 0)
    row_id = lax.broadcasted_iota(jnp.int32, proj.shape, 0)
    proj = jnp.where(jnp.logical_and(first, row_id < 2), 0.0, proj)
    proj = proj.astype(jnp.bfloat16).astype(jnp.float32).reshape(ext_len, 3, local_width)
    mixed = (
        short_filter[0] * proj[2:]
        + short_filter[1] * proj[1:-1]
        + short_filter[2] * proj[:-2]
    )
    query = mixed[:, 0]
    gated = (mixed[:, 1] * mixed[:, 2]).astype(jnp.bfloat16)
    x = gated.reshape(block_len, group_count, GROUP)

    pole_weight = residue * jnp.sqrt(2.0 * decay_rate)
    pos = jnp.arange(block_len, dtype=jnp.float32)
    lam = decay_rate[:, None, :]
    a_mat = pole_weight[:, None, :] * jnp.exp(-lam * pos[None, :, None])
    b_mat = jnp.exp(lam * pos[None, :, None])
    toep = jnp.einsum("gtr,gsr->gts", a_mat, b_mat, precision=HIGH)
    causal = pos[:, None] >= pos[None, :]
    toep = jnp.where(causal[None], toep, 0.0)
    near = dot_split("gts,sgc->tgc", toep, x)

    e_mat = jnp.exp(-lam * (block_len - 1 - pos)[None, :, None])
    s_loc = dot_split("gsr,sgc->grc", e_mat, x)
    n_ctx = n_chip * lax.axis_size("c")
    me = chip * lax.axis_size("c") + core
    s_flat = s_loc.reshape(group_count, -1)
    s_in = jnp.zeros_like(s_flat)
    for k in range(1, n_ctx):
        pairs = [(i, i + k) for i in range(n_ctx - k)]
        got = lax.ppermute(s_flat, ("p", "c"), pairs)
        fac = jnp.exp(-decay_rate * (block_len * (k - 1.0)))
        fac = jnp.where(me >= k, fac, 0.0)
        s_in = s_in + (fac[:, :, None] * got.reshape(s_loc.shape)).reshape(s_flat.shape)
    s_in = s_in.reshape(s_loc.shape)
    f_mat = pole_weight[:, None, :] * jnp.exp(-lam * (pos + 1.0)[None, :, None])
    far = jnp.einsum("gtr,grc->tgc", f_mat, s_in, precision=HIGH)
    long_out = (near + far).reshape(block_len, local_width)
    out = query * (long_out + skip * gated.astype(jnp.float32))
    return out.astype(jnp.bfloat16)


def solution(mesh):
    n_ctx, n_ch = mesh.devices.shape
    sub = Mesh(mesh.devices.reshape(n_ctx // 2, 2, n_ch), ("p", "c", "ch"))
    ctx = ("p", "c")
    return jax.shard_map(
        local,
        mesh=sub,
        in_specs=(
            P(ctx, "ch"),
            P(ctx, None, "ch"),
            P(None, None, "ch"),
            P("ch", None),
            P("ch", None),
            P("ch"),
        ),
        out_specs=P(ctx, "ch"),
        check_vma=False,
    )
```

```python
import jax
import jax.numpy as jnp
from jax import lax
from jax.experimental import pallas as pl
from jax.experimental.pallas import tpu as pltpu
from jax.sharding import Mesh
from jax.sharding import PartitionSpec as P

GROUP = 16
HIGH = lax.Precision.HIGHEST


def split_bf16(x):
    hi = x.astype(jnp.bfloat16)
    lo = (x - hi.astype(jnp.float32)).astype(jnp.bfloat16)
    return hi, lo


def dot_split(spec, weight, data):
    hi, lo = split_bf16(weight)
    return jnp.einsum(spec, hi, data, preferred_element_type=jnp.float32) + jnp.einsum(
        spec, lo, data, preferred_element_type=jnp.float32
    )


def ring_chip(r, n):
    hi = r // (n // 2)
    return 2 * (r + hi * (n - 1 - 2 * r)) + hi


def ring_pos(p, n):
    z, y = p // 2, p % 2
    return z + y * (n - 1 - 2 * z)


def rs_kernel(part_ref, out_ref, sbuf, rbuf, send_sem, recv_sem):
    n = part_ref.shape[0]
    chip = lax.axis_index("p")
    core = lax.axis_index("c")
    col = lax.axis_index("ch")
    r = ring_pos(chip, n)
    d = 1 - 2 * core
    nxt = ring_chip((r + d + n) % n, n)
    prv = ring_chip((r - d + n) % n, n)
    mesh_id = pl.DeviceIdType.MESH
    barrier = pltpu.get_barrier_semaphore()
    for nb in (nxt, prv):
        pl.semaphore_signal(barrier, 1, device_id=(nb, core, col), device_id_type=mesh_id)
    pl.semaphore_wait(barrier, 2)
    copies = []
    for s in range(n - 1):
        q = ring_chip((r - d * (1 + s) + 2 * n) % n, n)
        if s == 0:
            sbuf[0] = part_ref[q].astype(sbuf.dtype)
        else:
            copies[s - 1].wait_recv()
            sbuf[s] = (rbuf[s - 1].astype(jnp.float32) + part_ref[q]).astype(sbuf.dtype)
        copy = pltpu.make_async_remote_copy(
            src_ref=sbuf.at[s],
            dst_ref=rbuf.at[s],
            send_sem=send_sem.at[s],
            recv_sem=recv_sem.at[s],
            device_id=(nxt, core, col),
            device_id_type=mesh_id,
        )
        copy.start()
        copies.append(copy)
    copies[-1].wait_recv()
    out_ref[...] = (rbuf[n - 2].astype(jnp.float32) + part_ref[chip]).astype(out_ref.dtype)
    for copy in copies:
        copy.wait_send()


def ring_reduce_scatter(partial):
    n, rows, width = partial.shape
    return pl.pallas_call(
        rs_kernel,
        out_shape=jax.ShapeDtypeStruct((rows, width), jnp.bfloat16),
        in_specs=[pl.BlockSpec(memory_space=pltpu.VMEM)],
        out_specs=pl.BlockSpec(memory_space=pltpu.VMEM),
        scratch_shapes=[
            pltpu.VMEM((n - 1, rows, width), jnp.bfloat16),
            pltpu.VMEM((n - 1, rows, width), jnp.bfloat16),
            pltpu.SemaphoreType.DMA((n - 1,)),
            pltpu.SemaphoreType.DMA((n - 1,)),
        ],
        compiler_params=pltpu.CompilerParams(
            collective_id=0, has_side_effects=True, vmem_limit_bytes=48 * 1024 * 1024
        ),
    )(partial)


def local(tokens, w_in, short_filter, decay_rate, residue, skip):
    n_chip = lax.axis_size("p")
    block_len = tokens.shape[0]
    local_width = w_in.shape[2]
    group_count = local_width // GROUP
    chip = lax.axis_index("p")
    core = lax.axis_index("c")
    col = lax.axis_index("ch")

    n_col = lax.axis_size("ch")
    pieces = []
    for k in range(n_col):
        pairs = [(p * n_col + m, m * n_col + (p + k) % n_col) for p in range(n_chip) for m in range(n_col)]
        pieces.append(lax.ppermute(tokens, ("p", "ch"), pairs))
    stacked = jnp.stack(pieces)
    src = (col - jnp.arange(n_col)) % n_col
    order = jnp.argsort(src)
    tok_t = jnp.take(stacked, order, axis=0)
    w_flat = w_in.reshape(w_in.shape[0], -1)
    w_other = lax.ppermute(w_flat, "c", [(0, 1), (1, 0)])
    flat_w = jnp.where(
        core == 0,
        jnp.concatenate([w_flat, w_other], axis=0),
        jnp.concatenate([w_other, w_flat], axis=0),
    )

    tail = tok_t[:, block_len - 2 :]
    partner_tail = lax.ppermute(tail, "c", [(0, 1), (1, 0)])
    shifted_tail = jnp.concatenate([jnp.zeros_like(partner_tail[:1]), partner_tail[:-1]], axis=0)
    prior = jnp.where(core == 1, partner_tail, shifted_tail)
    tok_ext = jnp.concatenate([prior, tok_t], axis=1)
    n_blk, ext_len = tok_ext.shape[0], tok_ext.shape[1]
    partial = jnp.dot(
        tok_ext.reshape(n_blk * ext_len, -1), flat_w, preferred_element_type=jnp.float32
    ).reshape(n_blk, ext_len, -1)
    proj = ring_reduce_scatter(partial).astype(jnp.float32)
    first = jnp.logical_and(chip == 0, core == 0)
    row_id = lax.broadcasted_iota(jnp.int32, proj.shape, 0)
    proj = jnp.where(jnp.logical_and(first, row_id < 2), 0.0, proj)
    proj = proj.astype(jnp.bfloat16).astype(jnp.float32).reshape(ext_len, 3, local_width)
    mixed = (
        short_filter[0] * proj[2:]
        + short_filter[1] * proj[1:-1]
        + short_filter[2] * proj[:-2]
    )
    query = mixed[:, 0]
    gated = (mixed[:, 1] * mixed[:, 2]).astype(jnp.bfloat16)
    x = gated.reshape(block_len, group_count, GROUP)

    pole_weight = residue * jnp.sqrt(2.0 * decay_rate)
    pos = jnp.arange(block_len, dtype=jnp.float32)
    lam = decay_rate[:, None, :]
    a_mat = pole_weight[:, None, :] * jnp.exp(-lam * pos[None, :, None])
    b_mat = jnp.exp(lam * pos[None, :, None])
    toep = jnp.einsum("gtr,gsr->gts", a_mat, b_mat, precision=HIGH)
    causal = pos[:, None] >= pos[None, :]
    toep = jnp.where(causal[None], toep, 0.0)
    near = dot_split("gts,sgc->tgc", toep, x)

    e_mat = jnp.exp(-lam * (block_len - 1 - pos)[None, :, None])
    s_loc = dot_split("gsr,sgc->grc", e_mat, x)
    n_ctx = n_chip * lax.axis_size("c")
    me = chip * lax.axis_size("c") + core
    s_flat = s_loc.reshape(group_count, -1)
    s_in = jnp.zeros_like(s_flat)
    for k in range(1, n_ctx):
        pairs = [(i, i + k) for i in range(n_ctx - k)]
        got = lax.ppermute(s_flat, ("p", "c"), pairs)
        fac = jnp.exp(-decay_rate * (block_len * (k - 1.0)))
        fac = jnp.where(me >= k, fac, 0.0)
        s_in = s_in + (fac[:, :, None] * got.reshape(s_loc.shape)).reshape(s_flat.shape)
    s_in = s_in.reshape(s_loc.shape)
    f_mat = pole_weight[:, None, :] * jnp.exp(-lam * (pos + 1.0)[None, :, None])
    far = jnp.einsum("gtr,grc->tgc", f_mat, s_in, precision=HIGH)
    long_out = (near + far).reshape(block_len, local_width)
    out = query * (long_out + skip * gated.astype(jnp.float32))
    return out.astype(jnp.bfloat16)


def solution(mesh):
    n_ctx, n_ch = mesh.devices.shape
    sub = Mesh(mesh.devices.reshape(n_ctx // 2, 2, n_ch), ("p", "c", "ch"))
    ctx = ("p", "c")
    return jax.shard_map(
        local,
        mesh=sub,
        in_specs=(
            P(ctx, "ch"),
            P(ctx, None, "ch"),
            P(None, None, "ch"),
            P("ch", None),
            P("ch", None),
            P("ch"),
        ),
        out_specs=P(ctx, "ch"),
        check_vma=False,
    )
```

```python
import jax
import jax.numpy as jnp
from jax import lax
from jax.experimental import pallas as pl
from jax.experimental.pallas import tpu as pltpu
from jax.sharding import Mesh
from jax.sharding import PartitionSpec as P

GROUP = 16
HIGH = lax.Precision.HIGHEST


def split_bf16(x):
    hi = x.astype(jnp.bfloat16)
    lo = (x - hi.astype(jnp.float32)).astype(jnp.bfloat16)
    return hi, lo


def dot_split(spec, weight, data):
    hi, lo = split_bf16(weight)
    return jnp.einsum(spec, hi, data, preferred_element_type=jnp.float32) + jnp.einsum(
        spec, lo, data, preferred_element_type=jnp.float32
    )


def ring_chip(r, n):
    hi = r // (n // 2)
    return 2 * (r + hi * (n - 1 - 2 * r)) + hi


def ring_pos(p, n):
    z, y = p // 2, p % 2
    return z + y * (n - 1 - 2 * z)


def rs_kernel(part_ref, out_ref, sbuf, rbuf, send_sem, recv_sem):
    n = part_ref.shape[0]
    chip = lax.axis_index("p")
    core = lax.axis_index("c")
    col = lax.axis_index("ch")
    r = ring_pos(chip, n)
    d = 1 - 2 * core
    nxt = ring_chip((r + d + n) % n, n)
    prv = ring_chip((r - d + n) % n, n)
    mesh_id = pl.DeviceIdType.MESH
    barrier = pltpu.get_barrier_semaphore()
    for nb in (nxt, prv):
        pl.semaphore_signal(barrier, 1, device_id=(nb, core, col), device_id_type=mesh_id)
    pl.semaphore_wait(barrier, 2)
    copies = []
    for s in range(n - 1):
        q = ring_chip((r - d * (1 + s) + 2 * n) % n, n)
        if s == 0:
            sbuf[0] = part_ref[q].astype(sbuf.dtype)
        else:
            copies[s - 1].wait_recv()
            sbuf[s] = (rbuf[s - 1].astype(jnp.float32) + part_ref[q]).astype(sbuf.dtype)
        copy = pltpu.make_async_remote_copy(
            src_ref=sbuf.at[s],
            dst_ref=rbuf.at[s],
            send_sem=send_sem.at[s],
            recv_sem=recv_sem.at[s],
            device_id=(nxt, core, col),
            device_id_type=mesh_id,
        )
        copy.start()
        copies.append(copy)
    copies[-1].wait_recv()
    out_ref[...] = (rbuf[n - 2].astype(jnp.float32) + part_ref[chip]).astype(out_ref.dtype)
    for copy in copies:
        copy.wait_send()


def ring_reduce_scatter(partial):
    n, rows, width = partial.shape
    return pl.pallas_call(
        rs_kernel,
        out_shape=jax.ShapeDtypeStruct((rows, width), jnp.bfloat16),
        in_specs=[pl.BlockSpec(memory_space=pltpu.VMEM)],
        out_specs=pl.BlockSpec(memory_space=pltpu.VMEM),
        scratch_shapes=[
            pltpu.VMEM((n - 1, rows, width), jnp.bfloat16),
            pltpu.VMEM((n - 1, rows, width), jnp.bfloat16),
            pltpu.SemaphoreType.DMA((n - 1,)),
            pltpu.SemaphoreType.DMA((n - 1,)),
        ],
        compiler_params=pltpu.CompilerParams(
            collective_id=0, has_side_effects=True, vmem_limit_bytes=48 * 1024 * 1024
        ),
    )(partial)


def tok_kernel(src_ref, out_ref, send_sem, recv_sem):
    n = out_ref.shape[0]
    chip = lax.axis_index("p")
    core = lax.axis_index("c")
    col = lax.axis_index("ch")
    mesh_id = pl.DeviceIdType.MESH
    diag = chip == col
    barrier = pltpu.get_barrier_semaphore()
    for k in range(n):
        dest = (col, core, (chip + k) % n)
        srce = ((chip + k) % n, core, chip)
        if k == 0:
            @pl.when(jnp.logical_not(diag))
            def _():
                pl.semaphore_signal(barrier, 1, device_id=dest, device_id_type=mesh_id)
                pl.semaphore_signal(barrier, 1, device_id=srce, device_id_type=mesh_id)
        else:
            pl.semaphore_signal(barrier, 1, device_id=dest, device_id_type=mesh_id)
            pl.semaphore_signal(barrier, 1, device_id=srce, device_id_type=mesh_id)
    pl.semaphore_wait(barrier, 2 * n - 2 * diag.astype(jnp.int32))
    copies = []
    for k in range(n):
        copy = pltpu.make_async_remote_copy(
            src_ref=src_ref,
            dst_ref=out_ref.at[chip],
            send_sem=send_sem.at[k],
            recv_sem=recv_sem.at[chip],
            device_id=(col, core, (chip + k) % n),
            device_id_type=mesh_id,
        )
        if k == 0:
            own = pltpu.make_async_copy(src_ref, out_ref.at[chip], recv_sem.at[chip])

            @pl.when(diag)
            def _():
                own.start()

            @pl.when(jnp.logical_not(diag))
            def _():
                copy.start()
        else:
            copy.start()
        copies.append(copy)
    for j in range(n):
        pltpu.make_async_copy(src_ref, out_ref.at[j], recv_sem.at[j]).wait()
    for k in range(n):
        if k == 0:
            @pl.when(jnp.logical_not(diag))
            def _():
                copies[0].wait_send()
        else:
            copies[k].wait_send()


def spread_tokens(tokens, n):
    rows, width = tokens.shape
    return pl.pallas_call(
        tok_kernel,
        out_shape=jax.ShapeDtypeStruct((n, rows, width), tokens.dtype),
        in_specs=[pl.BlockSpec(memory_space=pltpu.VMEM)],
        out_specs=pl.BlockSpec(memory_space=pltpu.VMEM),
        scratch_shapes=[pltpu.SemaphoreType.DMA((n,)), pltpu.SemaphoreType.DMA((n,))],
        compiler_params=pltpu.CompilerParams(collective_id=1, has_side_effects=True),
    )(tokens)


def state_kernel(src_ref, out_ref, send_sem, recv_sem):
    n = out_ref.shape[0]
    n_core = lax.axis_size("c")
    me = lax.axis_index("p") * n_core + lax.axis_index("c")
    col = lax.axis_index("ch")
    mesh_id = pl.DeviceIdType.MESH
    barrier = pltpu.get_barrier_semaphore()
    for k in range(1, n):
        other = (me + k) % n
        pl.semaphore_signal(
            barrier, 1, device_id=(other // n_core, other % n_core, col), device_id_type=mesh_id
        )
    for j in range(n):
        @pl.when(j >= me)
        def _():
            out_ref[j] = jnp.zeros(out_ref.shape[1:], out_ref.dtype)
    pl.semaphore_wait(barrier, n - 1)
    copies = []
    for k in range(1, n):
        other = me + k
        copy = pltpu.make_async_remote_copy(
            src_ref=src_ref,
            dst_ref=out_ref.at[me],
            send_sem=send_sem.at[k],
            recv_sem=recv_sem.at[me],
            device_id=(other // n_core, other % n_core, col),
            device_id_type=mesh_id,
        )

        @pl.when(other < n)
        def _():
            copy.start()

        copies.append((other, copy))
    for j in range(n):
        @pl.when(j < me)
        def _():
            pltpu.make_async_copy(src_ref, out_ref.at[j], recv_sem.at[j]).wait()
    for other, copy in copies:
        @pl.when(other < n)
        def _():
            copy.wait_send()


def gather_earlier(state, n):
    return pl.pallas_call(
        state_kernel,
        out_shape=jax.ShapeDtypeStruct((n,) + state.shape, state.dtype),
        in_specs=[pl.BlockSpec(memory_space=pltpu.VMEM)],
        out_specs=pl.BlockSpec(memory_space=pltpu.VMEM),
        scratch_shapes=[pltpu.SemaphoreType.DMA((n,)), pltpu.SemaphoreType.DMA((n,))],
        compiler_params=pltpu.CompilerParams(collective_id=2, has_side_effects=True),
    )(state)


def local(tokens, w_in, short_filter, decay_rate, residue, skip):
    n_chip = lax.axis_size("p")
    block_len = tokens.shape[0]
    local_width = w_in.shape[2]
    group_count = local_width // GROUP
    chip = lax.axis_index("p")
    core = lax.axis_index("c")
    col = lax.axis_index("ch")

    n_col = lax.axis_size("ch")
    tok_t = spread_tokens(tokens, n_col)
    w_flat = w_in.reshape(w_in.shape[0], -1)
    w_other = lax.ppermute(w_flat, "c", [(0, 1), (1, 0)])
    flat_w = jnp.where(
        core == 0,
        jnp.concatenate([w_flat, w_other], axis=0),
        jnp.concatenate([w_other, w_flat], axis=0),
    )

    tail = tok_t[:, block_len - 2 :]
    partner_tail = lax.ppermute(tail, "c", [(0, 1), (1, 0)])
    shifted_tail = jnp.concatenate([jnp.zeros_like(partner_tail[:1]), partner_tail[:-1]], axis=0)
    prior = jnp.where(core == 1, partner_tail, shifted_tail)
    tok_ext = jnp.concatenate([prior, tok_t], axis=1)
    n_blk, ext_len = tok_ext.shape[0], tok_ext.shape[1]
    partial = jnp.dot(
        tok_ext.reshape(n_blk * ext_len, -1), flat_w, preferred_element_type=jnp.float32
    ).reshape(n_blk, ext_len, -1)
    proj = ring_reduce_scatter(partial).astype(jnp.float32)
    first = jnp.logical_and(chip == 0, core == 0)
    row_id = lax.broadcasted_iota(jnp.int32, proj.shape, 0)
    proj = jnp.where(jnp.logical_and(first, row_id < 2), 0.0, proj)
    proj = proj.astype(jnp.bfloat16).astype(jnp.float32).reshape(ext_len, 3, local_width)
    mixed = (
        short_filter[0] * proj[2:]
        + short_filter[1] * proj[1:-1]
        + short_filter[2] * proj[:-2]
    )
    query = mixed[:, 0]
    gated = (mixed[:, 1] * mixed[:, 2]).astype(jnp.bfloat16)
    x = gated.reshape(block_len, group_count, GROUP)

    pole_weight = residue * jnp.sqrt(2.0 * decay_rate)
    pos = jnp.arange(block_len, dtype=jnp.float32)
    lam = decay_rate[:, None, :]
    a_mat = pole_weight[:, None, :] * jnp.exp(-lam * pos[None, :, None])
    b_mat = jnp.exp(lam * pos[None, :, None])
    toep = jnp.einsum("gtr,gsr->gts", a_mat, b_mat, precision=HIGH)
    causal = pos[:, None] >= pos[None, :]
    toep = jnp.where(causal[None], toep, 0.0)
    near = dot_split("gts,sgc->tgc", toep, x)

    e_mat = jnp.exp(-lam * (block_len - 1 - pos)[None, :, None])
    s_loc = dot_split("gsr,sgc->grc", e_mat, x)
    n_ctx = n_chip * lax.axis_size("c")
    me = chip * lax.axis_size("c") + core
    s_flat = s_loc.reshape(group_count, -1)
    s_all = gather_earlier(s_flat, n_ctx).reshape((n_ctx,) + s_loc.shape)
    gap = (me - 1 - jnp.arange(n_ctx)).astype(jnp.float32)
    fac = jnp.exp(-decay_rate[None] * (block_len * jnp.maximum(gap, 0.0))[:, None, None])
    fac = jnp.where(gap[:, None, None] >= 0.0, fac, 0.0)
    s_in = jnp.sum(fac[..., None] * s_all, axis=0)
    f_mat = pole_weight[:, None, :] * jnp.exp(-lam * (pos + 1.0)[None, :, None])
    far = jnp.einsum("gtr,grc->tgc", f_mat, s_in, precision=HIGH)
    long_out = (near + far).reshape(block_len, local_width)
    out = query * (long_out + skip * gated.astype(jnp.float32))
    return out.astype(jnp.bfloat16)


def solution(mesh):
    n_ctx, n_ch = mesh.devices.shape
    sub = Mesh(mesh.devices.reshape(n_ctx // 2, 2, n_ch), ("p", "c", "ch"))
    ctx = ("p", "c")
    return jax.shard_map(
        local,
        mesh=sub,
        in_specs=(
            P(ctx, "ch"),
            P(ctx, None, "ch"),
            P(None, None, "ch"),
            P("ch", None),
            P("ch", None),
            P("ch"),
        ),
        out_specs=P(ctx, "ch"),
        check_vma=False,
    )
```

```python
import jax
import jax.numpy as jnp
from jax import lax
from jax.experimental import pallas as pl
from jax.experimental.pallas import tpu as pltpu
from jax.sharding import Mesh
from jax.sharding import PartitionSpec as P

GROUP = 16
HIGH = lax.Precision.HIGHEST


def split_bf16(x):
    hi = x.astype(jnp.bfloat16)
    lo = (x - hi.astype(jnp.float32)).astype(jnp.bfloat16)
    return hi, lo


def dot_split(spec, weight, data):
    hi, lo = split_bf16(weight)
    return jnp.einsum(spec, hi, data, preferred_element_type=jnp.float32) + jnp.einsum(
        spec, lo, data, preferred_element_type=jnp.float32
    )


def ring_chip(r, n):
    hi = r // (n // 2)
    return 2 * (r + hi * (n - 1 - 2 * r)) + hi


def ring_pos(p, n):
    z, y = p // 2, p % 2
    return z + y * (n - 1 - 2 * z)


def rs_kernel(part_ref, out_ref, sbuf, rbuf, send_sem, recv_sem):
    n, _, width = part_ref.shape
    half = width // 2
    chip = lax.axis_index("p")
    core = lax.axis_index("c")
    col = lax.axis_index("ch")
    r = ring_pos(chip, n)
    nxt = ring_chip((r + 1) % n, n)
    prv = ring_chip((r - 1 + n) % n, n)
    mesh_id = pl.DeviceIdType.MESH
    barrier = pltpu.get_barrier_semaphore()
    for nb in (nxt, prv):
        pl.semaphore_signal(barrier, 1, device_id=(nb, core, col), device_id_type=mesh_id)
    pl.semaphore_wait(barrier, 2)
    copies = [[], []]
    for s in range(n - 1):
        for h, (d, dest) in enumerate(((1, nxt), (-1, prv))):
            cols = pl.ds(h * half, half)
            q = ring_chip((r - d * (1 + s) + 2 * n) % n, n)
            if s == 0:
                sbuf[h, 0] = part_ref[q, :, cols].astype(sbuf.dtype)
            else:
                copies[h][s - 1].wait_recv()
                sbuf[h, s] = (rbuf[h, s - 1].astype(jnp.float32) + part_ref[q, :, cols]).astype(
                    sbuf.dtype
                )
            copy = pltpu.make_async_remote_copy(
                src_ref=sbuf.at[h, s],
                dst_ref=rbuf.at[h, s],
                send_sem=send_sem.at[h, s],
                recv_sem=recv_sem.at[h, s],
                device_id=(dest, core, col),
                device_id_type=mesh_id,
            )
            copy.start()
            copies[h].append(copy)
    for h in range(2):
        cols = pl.ds(h * half, half)
        copies[h][-1].wait_recv()
        out_ref[:, cols] = (rbuf[h, n - 2].astype(jnp.float32) + part_ref[chip, :, cols]).astype(
            out_ref.dtype
        )
    for h in range(2):
        for copy in copies[h]:
            copy.wait_send()


def ring_reduce_scatter(partial):
    n, rows, width = partial.shape
    return pl.pallas_call(
        rs_kernel,
        out_shape=jax.ShapeDtypeStruct((rows, width), jnp.bfloat16),
        in_specs=[pl.BlockSpec(memory_space=pltpu.VMEM)],
        out_specs=pl.BlockSpec(memory_space=pltpu.VMEM),
        scratch_shapes=[
            pltpu.VMEM((2, n - 1, rows, width // 2), jnp.bfloat16),
            pltpu.VMEM((2, n - 1, rows, width // 2), jnp.bfloat16),
            pltpu.SemaphoreType.DMA((2, n - 1)),
            pltpu.SemaphoreType.DMA((2, n - 1)),
        ],
        compiler_params=pltpu.CompilerParams(
            collective_id=0, has_side_effects=True, vmem_limit_bytes=48 * 1024 * 1024
        ),
    )(partial)


def tok_kernel(src_ref, out_ref, send_sem, recv_sem):
    n = out_ref.shape[0]
    chip = lax.axis_index("p")
    core = lax.axis_index("c")
    col = lax.axis_index("ch")
    mesh_id = pl.DeviceIdType.MESH
    diag = chip == col
    barrier = pltpu.get_barrier_semaphore()
    for k in range(n):
        dest = (col, core, (chip + k) % n)
        srce = ((chip + k) % n, core, chip)
        if k == 0:
            @pl.when(jnp.logical_not(diag))
            def _():
                pl.semaphore_signal(barrier, 1, device_id=dest, device_id_type=mesh_id)
                pl.semaphore_signal(barrier, 1, device_id=srce, device_id_type=mesh_id)
        else:
            pl.semaphore_signal(barrier, 1, device_id=dest, device_id_type=mesh_id)
            pl.semaphore_signal(barrier, 1, device_id=srce, device_id_type=mesh_id)
    pl.semaphore_wait(barrier, 2 * n - 2 * diag.astype(jnp.int32))
    copies = []
    for k in range(n):
        copy = pltpu.make_async_remote_copy(
            src_ref=src_ref,
            dst_ref=out_ref.at[chip],
            send_sem=send_sem.at[k],
            recv_sem=recv_sem.at[chip],
            device_id=(col, core, (chip + k) % n),
            device_id_type=mesh_id,
        )
        if k == 0:
            own = pltpu.make_async_copy(src_ref, out_ref.at[chip], recv_sem.at[chip])

            @pl.when(diag)
            def _():
                own.start()

            @pl.when(jnp.logical_not(diag))
            def _():
                copy.start()
        else:
            copy.start()
        copies.append(copy)
    for j in range(n):
        pltpu.make_async_copy(src_ref, out_ref.at[j], recv_sem.at[j]).wait()
    for k in range(n):
        if k == 0:
            @pl.when(jnp.logical_not(diag))
            def _():
                copies[0].wait_send()
        else:
            copies[k].wait_send()


def spread_tokens(tokens, n):
    rows, width = tokens.shape
    return pl.pallas_call(
        tok_kernel,
        out_shape=jax.ShapeDtypeStruct((n, rows, width), tokens.dtype),
        in_specs=[pl.BlockSpec(memory_space=pltpu.VMEM)],
        out_specs=pl.BlockSpec(memory_space=pltpu.VMEM),
        scratch_shapes=[pltpu.SemaphoreType.DMA((n,)), pltpu.SemaphoreType.DMA((n,))],
        compiler_params=pltpu.CompilerParams(collective_id=1, has_side_effects=True),
    )(tokens)


def state_kernel(src_ref, out_ref, send_sem, recv_sem):
    n = out_ref.shape[0]
    n_core = lax.axis_size("c")
    me = lax.axis_index("p") * n_core + lax.axis_index("c")
    col = lax.axis_index("ch")
    mesh_id = pl.DeviceIdType.MESH
    barrier = pltpu.get_barrier_semaphore()
    for k in range(1, n):
        other = (me + k) % n
        pl.semaphore_signal(
            barrier, 1, device_id=(other // n_core, other % n_core, col), device_id_type=mesh_id
        )
    for j in range(n):
        @pl.when(j >= me)
        def _():
            out_ref[j] = jnp.zeros(out_ref.shape[1:], out_ref.dtype)
    pl.semaphore_wait(barrier, n - 1)
    copies = []
    for k in range(1, n):
        other = me + k
        copy = pltpu.make_async_remote_copy(
            src_ref=src_ref,
            dst_ref=out_ref.at[me],
            send_sem=send_sem.at[k],
            recv_sem=recv_sem.at[me],
            device_id=(other // n_core, other % n_core, col),
            device_id_type=mesh_id,
        )

        @pl.when(other < n)
        def _():
            copy.start()

        copies.append((other, copy))
    for j in range(n):
        @pl.when(j < me)
        def _():
            pltpu.make_async_copy(src_ref, out_ref.at[j], recv_sem.at[j]).wait()
    for other, copy in copies:
        @pl.when(other < n)
        def _():
            copy.wait_send()


def gather_earlier(state, n):
    return pl.pallas_call(
        state_kernel,
        out_shape=jax.ShapeDtypeStruct((n,) + state.shape, state.dtype),
        in_specs=[pl.BlockSpec(memory_space=pltpu.VMEM)],
        out_specs=pl.BlockSpec(memory_space=pltpu.VMEM),
        scratch_shapes=[pltpu.SemaphoreType.DMA((n,)), pltpu.SemaphoreType.DMA((n,))],
        compiler_params=pltpu.CompilerParams(collective_id=2, has_side_effects=True),
    )(state)


def local(tokens, w_in, short_filter, decay_rate, residue, skip):
    n_chip = lax.axis_size("p")
    block_len = tokens.shape[0]
    local_width = w_in.shape[2]
    group_count = local_width // GROUP
    chip = lax.axis_index("p")
    core = lax.axis_index("c")
    col = lax.axis_index("ch")

    n_col = lax.axis_size("ch")
    tok_t = spread_tokens(tokens, n_col)
    w_flat = w_in.reshape(w_in.shape[0], -1)
    w_other = lax.ppermute(w_flat, "c", [(0, 1), (1, 0)])
    flat_w = jnp.where(
        core == 0,
        jnp.concatenate([w_flat, w_other], axis=0),
        jnp.concatenate([w_other, w_flat], axis=0),
    )

    tail = tok_t[:, block_len - 2 :]
    partner_tail = lax.ppermute(tail, "c", [(0, 1), (1, 0)])
    shifted_tail = jnp.concatenate([jnp.zeros_like(partner_tail[:1]), partner_tail[:-1]], axis=0)
    prior = jnp.where(core == 1, partner_tail, shifted_tail)
    tok_ext = jnp.concatenate([prior, tok_t], axis=1)
    n_blk, ext_len = tok_ext.shape[0], tok_ext.shape[1]
    partial = jnp.dot(
        tok_ext.reshape(n_blk * ext_len, -1), flat_w, preferred_element_type=jnp.float32
    ).reshape(n_blk, ext_len, -1)
    proj = ring_reduce_scatter(partial).astype(jnp.float32)
    first = jnp.logical_and(chip == 0, core == 0)
    row_id = lax.broadcasted_iota(jnp.int32, proj.shape, 0)
    proj = jnp.where(jnp.logical_and(first, row_id < 2), 0.0, proj)
    proj = proj.astype(jnp.bfloat16).astype(jnp.float32).reshape(ext_len, 3, local_width)
    mixed = (
        short_filter[0] * proj[2:]
        + short_filter[1] * proj[1:-1]
        + short_filter[2] * proj[:-2]
    )
    query = mixed[:, 0]
    gated = (mixed[:, 1] * mixed[:, 2]).astype(jnp.bfloat16)
    x = gated.reshape(block_len, group_count, GROUP)

    pole_weight = residue * jnp.sqrt(2.0 * decay_rate)
    pos = jnp.arange(block_len, dtype=jnp.float32)
    lam = decay_rate[:, None, :]
    a_mat = pole_weight[:, None, :] * jnp.exp(-lam * pos[None, :, None])
    b_mat = jnp.exp(lam * pos[None, :, None])
    toep = jnp.einsum("gtr,gsr->gts", a_mat, b_mat, precision=HIGH)
    causal = pos[:, None] >= pos[None, :]
    toep = jnp.where(causal[None], toep, 0.0)
    near = dot_split("gts,sgc->tgc", toep, x)

    e_mat = jnp.exp(-lam * (block_len - 1 - pos)[None, :, None])
    s_loc = dot_split("gsr,sgc->grc", e_mat, x)
    n_ctx = n_chip * lax.axis_size("c")
    me = chip * lax.axis_size("c") + core
    s_flat = s_loc.reshape(group_count, -1)
    s_all = gather_earlier(s_flat, n_ctx).reshape((n_ctx,) + s_loc.shape)
    gap = (me - 1 - jnp.arange(n_ctx)).astype(jnp.float32)
    fac = jnp.exp(-decay_rate[None] * (block_len * jnp.maximum(gap, 0.0))[:, None, None])
    fac = jnp.where(gap[:, None, None] >= 0.0, fac, 0.0)
    s_in = jnp.sum(fac[..., None] * s_all, axis=0)
    f_mat = pole_weight[:, None, :] * jnp.exp(-lam * (pos + 1.0)[None, :, None])
    far = jnp.einsum("gtr,grc->tgc", f_mat, s_in, precision=HIGH)
    long_out = (near + far).reshape(block_len, local_width)
    out = query * (long_out + skip * gated.astype(jnp.float32))
    return out.astype(jnp.bfloat16)


def solution(mesh):
    n_ctx, n_ch = mesh.devices.shape
    sub = Mesh(mesh.devices.reshape(n_ctx // 2, 2, n_ch), ("p", "c", "ch"))
    ctx = ("p", "c")
    return jax.shard_map(
        local,
        mesh=sub,
        in_specs=(
            P(ctx, "ch"),
            P(ctx, None, "ch"),
            P(None, None, "ch"),
            P("ch", None),
            P("ch", None),
            P("ch"),
        ),
        out_specs=P(ctx, "ch"),
        check_vma=False,
    )
```

```python
import jax
import jax.numpy as jnp
from jax import lax
from jax.experimental import pallas as pl
from jax.experimental.pallas import tpu as pltpu
from jax.sharding import Mesh
from jax.sharding import PartitionSpec as P

GROUP = 16
HIGH = lax.Precision.HIGHEST


def split_bf16(x):
    hi = x.astype(jnp.bfloat16)
    lo = (x - hi.astype(jnp.float32)).astype(jnp.bfloat16)
    return hi, lo


def dot_split(spec, weight, data):
    hi, lo = split_bf16(weight)
    return jnp.einsum(spec, hi, data, preferred_element_type=jnp.float32) + jnp.einsum(
        spec, lo, data, preferred_element_type=jnp.float32
    )


def ring_chip(r, n):
    hi = r // (n // 2)
    return 2 * (r + hi * (n - 1 - 2 * r)) + hi


def ring_pos(p, n):
    z, y = p // 2, p % 2
    return z + y * (n - 1 - 2 * z)


def rs_kernel(part_ref, out_ref, sbuf, rbuf, send_sem, recv_sem):
    n, _, width = part_ref.shape
    n_ring = sbuf.shape[0]
    chunk = width // n_ring
    chip = lax.axis_index("p")
    core = lax.axis_index("c")
    col = lax.axis_index("ch")
    r = ring_pos(chip, n)
    nxt = ring_chip((r + 1) % n, n)
    prv = ring_chip((r - 1 + n) % n, n)
    mesh_id = pl.DeviceIdType.MESH
    barrier = pltpu.get_barrier_semaphore()
    for nb in (nxt, prv):
        pl.semaphore_signal(barrier, 1, device_id=(nb, core, col), device_id_type=mesh_id)
    pl.semaphore_wait(barrier, 2)
    copies = [[] for _ in range(n_ring)]
    order = [h * (n_ring // 2) + k for k in range(n_ring // 2) for h in range(2)]
    for s in range(n - 1):
        for ring in order:
            d, dest = (1, nxt) if ring < n_ring // 2 else (-1, prv)
            cols = pl.ds(ring * chunk, chunk)
            q = ring_chip((r - d * (1 + s) + 2 * n) % n, n)
            if s == 0:
                sbuf[ring, 0] = part_ref[q, :, cols].astype(sbuf.dtype)
            else:
                copies[ring][s - 1].wait_recv()
                sbuf[ring, s] = (
                    rbuf[ring, s - 1].astype(jnp.float32) + part_ref[q, :, cols]
                ).astype(sbuf.dtype)
            copy = pltpu.make_async_remote_copy(
                src_ref=sbuf.at[ring, s],
                dst_ref=rbuf.at[ring, s],
                send_sem=send_sem.at[ring, s],
                recv_sem=recv_sem.at[ring, s],
                device_id=(dest, core, col),
                device_id_type=mesh_id,
            )
            copy.start()
            copies[ring].append(copy)
    for ring in order:
        cols = pl.ds(ring * chunk, chunk)
        copies[ring][-1].wait_recv()
        out_ref[:, cols] = (
            rbuf[ring, n - 2].astype(jnp.float32) + part_ref[chip, :, cols]
        ).astype(out_ref.dtype)
    for ring in order:
        for copy in copies[ring]:
            copy.wait_send()


def ring_reduce_scatter(partial, n_ring=6):
    n, rows, width = partial.shape
    return pl.pallas_call(
        rs_kernel,
        out_shape=jax.ShapeDtypeStruct((rows, width), jnp.bfloat16),
        in_specs=[pl.BlockSpec(memory_space=pltpu.VMEM)],
        out_specs=pl.BlockSpec(memory_space=pltpu.VMEM),
        scratch_shapes=[
            pltpu.VMEM((n_ring, n - 1, rows, width // n_ring), jnp.bfloat16),
            pltpu.VMEM((n_ring, n - 1, rows, width // n_ring), jnp.bfloat16),
            pltpu.SemaphoreType.DMA((n_ring, n - 1)),
            pltpu.SemaphoreType.DMA((n_ring, n - 1)),
        ],
        compiler_params=pltpu.CompilerParams(
            collective_id=0, has_side_effects=True, vmem_limit_bytes=48 * 1024 * 1024
        ),
    )(partial)


def tok_kernel(src_ref, out_ref, send_sem, recv_sem):
    n = out_ref.shape[0]
    chip = lax.axis_index("p")
    core = lax.axis_index("c")
    col = lax.axis_index("ch")
    mesh_id = pl.DeviceIdType.MESH
    diag = chip == col
    barrier = pltpu.get_barrier_semaphore()
    for k in range(n):
        dest = (col, core, (chip + k) % n)
        srce = ((chip + k) % n, core, chip)
        if k == 0:
            @pl.when(jnp.logical_not(diag))
            def _():
                pl.semaphore_signal(barrier, 1, device_id=dest, device_id_type=mesh_id)
                pl.semaphore_signal(barrier, 1, device_id=srce, device_id_type=mesh_id)
        else:
            pl.semaphore_signal(barrier, 1, device_id=dest, device_id_type=mesh_id)
            pl.semaphore_signal(barrier, 1, device_id=srce, device_id_type=mesh_id)
    pl.semaphore_wait(barrier, 2 * n - 2 * diag.astype(jnp.int32))
    copies = []
    for k in range(n):
        copy = pltpu.make_async_remote_copy(
            src_ref=src_ref,
            dst_ref=out_ref.at[chip],
            send_sem=send_sem.at[k],
            recv_sem=recv_sem.at[chip],
            device_id=(col, core, (chip + k) % n),
            device_id_type=mesh_id,
        )
        if k == 0:
            own = pltpu.make_async_copy(src_ref, out_ref.at[chip], recv_sem.at[chip])

            @pl.when(diag)
            def _():
                own.start()

            @pl.when(jnp.logical_not(diag))
            def _():
                copy.start()
        else:
            copy.start()
        copies.append(copy)
    for j in range(n):
        pltpu.make_async_copy(src_ref, out_ref.at[j], recv_sem.at[j]).wait()
    for k in range(n):
        if k == 0:
            @pl.when(jnp.logical_not(diag))
            def _():
                copies[0].wait_send()
        else:
            copies[k].wait_send()


def spread_tokens(tokens, n):
    rows, width = tokens.shape
    return pl.pallas_call(
        tok_kernel,
        out_shape=jax.ShapeDtypeStruct((n, rows, width), tokens.dtype),
        in_specs=[pl.BlockSpec(memory_space=pltpu.VMEM)],
        out_specs=pl.BlockSpec(memory_space=pltpu.VMEM),
        scratch_shapes=[pltpu.SemaphoreType.DMA((n,)), pltpu.SemaphoreType.DMA((n,))],
        compiler_params=pltpu.CompilerParams(collective_id=1, has_side_effects=True),
    )(tokens)


def state_kernel(src_ref, out_ref, send_sem, recv_sem):
    n = out_ref.shape[0]
    n_core = lax.axis_size("c")
    me = lax.axis_index("p") * n_core + lax.axis_index("c")
    col = lax.axis_index("ch")
    mesh_id = pl.DeviceIdType.MESH
    barrier = pltpu.get_barrier_semaphore()
    for k in range(1, n):
        other = (me + k) % n
        pl.semaphore_signal(
            barrier, 1, device_id=(other // n_core, other % n_core, col), device_id_type=mesh_id
        )
    for j in range(n):
        @pl.when(j >= me)
        def _():
            out_ref[j] = jnp.zeros(out_ref.shape[1:], out_ref.dtype)
    pl.semaphore_wait(barrier, n - 1)
    copies = []
    for k in range(1, n):
        other = me + k
        copy = pltpu.make_async_remote_copy(
            src_ref=src_ref,
            dst_ref=out_ref.at[me],
            send_sem=send_sem.at[k],
            recv_sem=recv_sem.at[me],
            device_id=(other // n_core, other % n_core, col),
            device_id_type=mesh_id,
        )

        @pl.when(other < n)
        def _():
            copy.start()

        copies.append((other, copy))
    for j in range(n):
        @pl.when(j < me)
        def _():
            pltpu.make_async_copy(src_ref, out_ref.at[j], recv_sem.at[j]).wait()
    for other, copy in copies:
        @pl.when(other < n)
        def _():
            copy.wait_send()


def gather_earlier(state, n):
    return pl.pallas_call(
        state_kernel,
        out_shape=jax.ShapeDtypeStruct((n,) + state.shape, state.dtype),
        in_specs=[pl.BlockSpec(memory_space=pltpu.VMEM)],
        out_specs=pl.BlockSpec(memory_space=pltpu.VMEM),
        scratch_shapes=[pltpu.SemaphoreType.DMA((n,)), pltpu.SemaphoreType.DMA((n,))],
        compiler_params=pltpu.CompilerParams(collective_id=2, has_side_effects=True),
    )(state)


def local(tokens, w_in, short_filter, decay_rate, residue, skip):
    n_chip = lax.axis_size("p")
    block_len = tokens.shape[0]
    local_width = w_in.shape[2]
    group_count = local_width // GROUP
    chip = lax.axis_index("p")
    core = lax.axis_index("c")
    col = lax.axis_index("ch")

    n_col = lax.axis_size("ch")
    tok_t = spread_tokens(tokens, n_col)
    w_flat = w_in.reshape(w_in.shape[0], -1)
    w_other = lax.ppermute(w_flat, "c", [(0, 1), (1, 0)])
    flat_w = jnp.where(
        core == 0,
        jnp.concatenate([w_flat, w_other], axis=0),
        jnp.concatenate([w_other, w_flat], axis=0),
    )

    tail = tok_t[:, block_len - 2 :]
    partner_tail = lax.ppermute(tail, "c", [(0, 1), (1, 0)])
    shifted_tail = jnp.concatenate([jnp.zeros_like(partner_tail[:1]), partner_tail[:-1]], axis=0)
    prior = jnp.where(core == 1, partner_tail, shifted_tail)
    tok_ext = jnp.concatenate([prior, tok_t], axis=1)
    n_blk, ext_len = tok_ext.shape[0], tok_ext.shape[1]
    partial = jnp.dot(
        tok_ext.reshape(n_blk * ext_len, -1), flat_w, preferred_element_type=jnp.float32
    ).reshape(n_blk, ext_len, -1)
    proj = ring_reduce_scatter(partial).astype(jnp.float32)
    first = jnp.logical_and(chip == 0, core == 0)
    row_id = lax.broadcasted_iota(jnp.int32, proj.shape, 0)
    proj = jnp.where(jnp.logical_and(first, row_id < 2), 0.0, proj)
    proj = proj.astype(jnp.bfloat16).astype(jnp.float32).reshape(ext_len, 3, local_width)
    mixed = (
        short_filter[0] * proj[2:]
        + short_filter[1] * proj[1:-1]
        + short_filter[2] * proj[:-2]
    )
    query = mixed[:, 0]
    gated = (mixed[:, 1] * mixed[:, 2]).astype(jnp.bfloat16)
    x = gated.reshape(block_len, group_count, GROUP)

    pole_weight = residue * jnp.sqrt(2.0 * decay_rate)
    pos = jnp.arange(block_len, dtype=jnp.float32)
    lam = decay_rate[:, None, :]
    a_mat = pole_weight[:, None, :] * jnp.exp(-lam * pos[None, :, None])
    b_mat = jnp.exp(lam * pos[None, :, None])
    toep = jnp.einsum("gtr,gsr->gts", a_mat, b_mat, precision=HIGH)
    causal = pos[:, None] >= pos[None, :]
    toep = jnp.where(causal[None], toep, 0.0)
    near = dot_split("gts,sgc->tgc", toep, x)

    e_mat = jnp.exp(-lam * (block_len - 1 - pos)[None, :, None])
    s_loc = dot_split("gsr,sgc->grc", e_mat, x)
    n_ctx = n_chip * lax.axis_size("c")
    me = chip * lax.axis_size("c") + core
    s_flat = s_loc.reshape(group_count, -1)
    s_all = gather_earlier(s_flat, n_ctx).reshape((n_ctx,) + s_loc.shape)
    gap = (me - 1 - jnp.arange(n_ctx)).astype(jnp.float32)
    fac = jnp.exp(-decay_rate[None] * (block_len * jnp.maximum(gap, 0.0))[:, None, None])
    fac = jnp.where(gap[:, None, None] >= 0.0, fac, 0.0)
    s_in = jnp.sum(fac[..., None] * s_all, axis=0)
    f_mat = pole_weight[:, None, :] * jnp.exp(-lam * (pos + 1.0)[None, :, None])
    far = jnp.einsum("gtr,grc->tgc", f_mat, s_in, precision=HIGH)
    long_out = (near + far).reshape(block_len, local_width)
    out = query * (long_out + skip * gated.astype(jnp.float32))
    return out.astype(jnp.bfloat16)


def solution(mesh):
    n_ctx, n_ch = mesh.devices.shape
    sub = Mesh(mesh.devices.reshape(n_ctx // 2, 2, n_ch), ("p", "c", "ch"))
    ctx = ("p", "c")
    return jax.shard_map(
        local,
        mesh=sub,
        in_specs=(
            P(ctx, "ch"),
            P(ctx, None, "ch"),
            P(None, None, "ch"),
            P("ch", None),
            P("ch", None),
            P("ch"),
        ),
        out_specs=P(ctx, "ch"),
        check_vma=False,
    )
```

```python
import jax
import jax.numpy as jnp
from jax import lax
from jax.experimental import pallas as pl
from jax.experimental.pallas import tpu as pltpu
from jax.sharding import Mesh
from jax.sharding import PartitionSpec as P

GROUP = 16
HIGH = lax.Precision.HIGHEST


def split_bf16(x):
    hi = x.astype(jnp.bfloat16)
    lo = (x - hi.astype(jnp.float32)).astype(jnp.bfloat16)
    return hi, lo


def dot_split(spec, weight, data):
    hi, lo = split_bf16(weight)
    return jnp.einsum(spec, hi, data, preferred_element_type=jnp.float32) + jnp.einsum(
        spec, lo, data, preferred_element_type=jnp.float32
    )


def ring_chip(r, n):
    hi = r // (n // 2)
    return 2 * (r + hi * (n - 1 - 2 * r)) + hi


def ring_pos(p, n):
    z, y = p // 2, p % 2
    return z + y * (n - 1 - 2 * z)


def rs_kernel(tok_ref, w_ref, taps_ref, q_ref, g_ref, sbuf, rbuf, proj, send_sem, recv_sem):
    n, ext_len, _ = tok_ref.shape
    width = w_ref.shape[1]
    n_ring = sbuf.shape[0]
    chunk = width // n_ring
    chip = lax.axis_index("p")
    core = lax.axis_index("c")
    col = lax.axis_index("ch")
    r = ring_pos(chip, n)
    nxt = ring_chip((r + 1) % n, n)
    prv = ring_chip((r - 1 + n) % n, n)
    mesh_id = pl.DeviceIdType.MESH
    barrier = pltpu.get_barrier_semaphore()
    for nb in (nxt, prv):
        pl.semaphore_signal(barrier, 1, device_id=(nb, core, col), device_id_type=mesh_id)
    pl.semaphore_wait(barrier, 2)

    def part(blk, cols):
        return jnp.dot(tok_ref[blk], w_ref[:, cols], preferred_element_type=jnp.float32)

    copies = [[] for _ in range(n_ring)]
    order = [h * (n_ring // 2) + k for k in range(n_ring // 2) for h in range(2)]
    for s in range(n - 1):
        for ring in order:
            d, dest = (1, nxt) if ring < n_ring // 2 else (-1, prv)
            cols = pl.ds(ring * chunk, chunk)
            q = ring_chip((r - d * (1 + s) + 2 * n) % n, n)
            if s == 0:
                sbuf[ring, 0] = part(q, cols).astype(sbuf.dtype)
            else:
                mine = part(q, cols)
                copies[ring][s - 1].wait_recv()
                sbuf[ring, s] = (rbuf[ring, s - 1].astype(jnp.float32) + mine).astype(sbuf.dtype)
            copy = pltpu.make_async_remote_copy(
                src_ref=sbuf.at[ring, s],
                dst_ref=rbuf.at[ring, s],
                send_sem=send_sem.at[ring, s],
                recv_sem=recv_sem.at[ring, s],
                device_id=(dest, core, col),
                device_id_type=mesh_id,
            )
            copy.start()
            copies[ring].append(copy)
    for ring in order:
        cols = pl.ds(ring * chunk, chunk)
        mine = part(chip, cols)
        copies[ring][-1].wait_recv()
        total = rbuf[ring, n - 2].astype(jnp.float32) + mine
        proj[:, cols] = total.astype(jnp.bfloat16).astype(jnp.float32)

    @pl.when(jnp.logical_and(chip == 0, core == 0))
    def _():
        proj[0:2, :] = jnp.zeros((2, width), jnp.float32)

    rows = ext_len - 2
    third = width // 3
    mixed = []
    for j in range(3):
        cols = pl.ds(j * third, third)
        mixed.append(
            taps_ref[0, j][None, :] * proj[pl.ds(2, rows), cols]
            + taps_ref[1, j][None, :] * proj[pl.ds(1, rows), cols]
            + taps_ref[2, j][None, :] * proj[pl.ds(0, rows), cols]
        )
    q_ref[...] = mixed[0]
    g_ref[...] = (mixed[1] * mixed[2]).astype(g_ref.dtype)
    for ring in order:
        for copy in copies[ring]:
            copy.wait_send()


def project_and_gate(tok_ext, w_flat, taps, n_ring=6):
    n, ext_len, _ = tok_ext.shape
    width = w_flat.shape[1]
    rows, third = ext_len - 2, width // 3
    vmem = pl.BlockSpec(memory_space=pltpu.VMEM)
    return pl.pallas_call(
        rs_kernel,
        out_shape=(
            jax.ShapeDtypeStruct((rows, third), jnp.float32),
            jax.ShapeDtypeStruct((rows, third), jnp.bfloat16),
        ),
        in_specs=[vmem, vmem, vmem],
        out_specs=(vmem, vmem),
        scratch_shapes=[
            pltpu.VMEM((n_ring, n - 1, ext_len, width // n_ring), jnp.bfloat16),
            pltpu.VMEM((n_ring, n - 1, ext_len, width // n_ring), jnp.bfloat16),
            pltpu.VMEM((ext_len, width), jnp.float32),
            pltpu.SemaphoreType.DMA((n_ring, n - 1)),
            pltpu.SemaphoreType.DMA((n_ring, n - 1)),
        ],
        compiler_params=pltpu.CompilerParams(
            collective_id=0, has_side_effects=True, vmem_limit_bytes=48 * 1024 * 1024
        ),
    )(tok_ext, w_flat, taps)


def tok_kernel(src_ref, out_ref, send_sem, recv_sem):
    n = out_ref.shape[0]
    chip = lax.axis_index("p")
    core = lax.axis_index("c")
    col = lax.axis_index("ch")
    mesh_id = pl.DeviceIdType.MESH
    diag = chip == col
    barrier = pltpu.get_barrier_semaphore()
    for k in range(n):
        dest = (col, core, (chip + k) % n)
        srce = ((chip + k) % n, core, chip)
        if k == 0:
            @pl.when(jnp.logical_not(diag))
            def _():
                pl.semaphore_signal(barrier, 1, device_id=dest, device_id_type=mesh_id)
                pl.semaphore_signal(barrier, 1, device_id=srce, device_id_type=mesh_id)
        else:
            pl.semaphore_signal(barrier, 1, device_id=dest, device_id_type=mesh_id)
            pl.semaphore_signal(barrier, 1, device_id=srce, device_id_type=mesh_id)
    pl.semaphore_wait(barrier, 2 * n - 2 * diag.astype(jnp.int32))
    copies = []
    for k in range(n):
        copy = pltpu.make_async_remote_copy(
            src_ref=src_ref,
            dst_ref=out_ref.at[chip],
            send_sem=send_sem.at[k],
            recv_sem=recv_sem.at[chip],
            device_id=(col, core, (chip + k) % n),
            device_id_type=mesh_id,
        )
        if k == 0:
            own = pltpu.make_async_copy(src_ref, out_ref.at[chip], recv_sem.at[chip])

            @pl.when(diag)
            def _():
                own.start()

            @pl.when(jnp.logical_not(diag))
            def _():
                copy.start()
        else:
            copy.start()
        copies.append(copy)
    for j in range(n):
        pltpu.make_async_copy(src_ref, out_ref.at[j], recv_sem.at[j]).wait()
    for k in range(n):
        if k == 0:
            @pl.when(jnp.logical_not(diag))
            def _():
                copies[0].wait_send()
        else:
            copies[k].wait_send()


def spread_tokens(tokens, n):
    rows, width = tokens.shape
    return pl.pallas_call(
        tok_kernel,
        out_shape=jax.ShapeDtypeStruct((n, rows, width), tokens.dtype),
        in_specs=[pl.BlockSpec(memory_space=pltpu.VMEM)],
        out_specs=pl.BlockSpec(memory_space=pltpu.VMEM),
        scratch_shapes=[pltpu.SemaphoreType.DMA((n,)), pltpu.SemaphoreType.DMA((n,))],
        compiler_params=pltpu.CompilerParams(collective_id=1, has_side_effects=True),
    )(tokens)


def state_kernel(src_ref, out_ref, send_sem, recv_sem):
    n = out_ref.shape[0]
    n_core = lax.axis_size("c")
    me = lax.axis_index("p") * n_core + lax.axis_index("c")
    col = lax.axis_index("ch")
    mesh_id = pl.DeviceIdType.MESH
    barrier = pltpu.get_barrier_semaphore()
    for k in range(1, n):
        other = (me + k) % n
        pl.semaphore_signal(
            barrier, 1, device_id=(other // n_core, other % n_core, col), device_id_type=mesh_id
        )
    for j in range(n):
        @pl.when(j >= me)
        def _():
            out_ref[j] = jnp.zeros(out_ref.shape[1:], out_ref.dtype)
    pl.semaphore_wait(barrier, n - 1)
    copies = []
    for k in range(1, n):
        other = me + k
        copy = pltpu.make_async_remote_copy(
            src_ref=src_ref,
            dst_ref=out_ref.at[me],
            send_sem=send_sem.at[k],
            recv_sem=recv_sem.at[me],
            device_id=(other // n_core, other % n_core, col),
            device_id_type=mesh_id,
        )

        @pl.when(other < n)
        def _():
            copy.start()

        copies.append((other, copy))
    for j in range(n):
        @pl.when(j < me)
        def _():
            pltpu.make_async_copy(src_ref, out_ref.at[j], recv_sem.at[j]).wait()
    for other, copy in copies:
        @pl.when(other < n)
        def _():
            copy.wait_send()


def gather_earlier(state, n):
    return pl.pallas_call(
        state_kernel,
        out_shape=jax.ShapeDtypeStruct((n,) + state.shape, state.dtype),
        in_specs=[pl.BlockSpec(memory_space=pltpu.VMEM)],
        out_specs=pl.BlockSpec(memory_space=pltpu.VMEM),
        scratch_shapes=[pltpu.SemaphoreType.DMA((n,)), pltpu.SemaphoreType.DMA((n,))],
        compiler_params=pltpu.CompilerParams(collective_id=2, has_side_effects=True),
    )(state)


def local(tokens, w_in, short_filter, decay_rate, residue, skip):
    n_chip = lax.axis_size("p")
    block_len = tokens.shape[0]
    local_width = w_in.shape[2]
    group_count = local_width // GROUP
    chip = lax.axis_index("p")
    core = lax.axis_index("c")
    col = lax.axis_index("ch")

    n_col = lax.axis_size("ch")
    tok_t = spread_tokens(tokens, n_col)
    w_flat = w_in.reshape(w_in.shape[0], -1)
    w_other = lax.ppermute(w_flat, "c", [(0, 1), (1, 0)])
    flat_w = jnp.where(
        core == 0,
        jnp.concatenate([w_flat, w_other], axis=0),
        jnp.concatenate([w_other, w_flat], axis=0),
    )

    tail = tok_t[:, block_len - 2 :]
    partner_tail = lax.ppermute(tail, "c", [(0, 1), (1, 0)])
    shifted_tail = jnp.concatenate([jnp.zeros_like(partner_tail[:1]), partner_tail[:-1]], axis=0)
    prior = jnp.where(core == 1, partner_tail, shifted_tail)
    tok_ext = jnp.concatenate([prior, tok_t], axis=1)
    query, gated = project_and_gate(tok_ext, flat_w, short_filter)
    x = gated.reshape(block_len, group_count, GROUP)

    pole_weight = residue * jnp.sqrt(2.0 * decay_rate)
    pos = jnp.arange(block_len, dtype=jnp.float32)
    lam = decay_rate[:, None, :]
    a_mat = pole_weight[:, None, :] * jnp.exp(-lam * pos[None, :, None])
    b_mat = jnp.exp(lam * pos[None, :, None])
    toep = jnp.einsum("gtr,gsr->gts", a_mat, b_mat, precision=HIGH)
    causal = pos[:, None] >= pos[None, :]
    toep = jnp.where(causal[None], toep, 0.0)
    near = dot_split("gts,sgc->tgc", toep, x)

    e_mat = jnp.exp(-lam * (block_len - 1 - pos)[None, :, None])
    s_loc = dot_split("gsr,sgc->grc", e_mat, x)
    n_ctx = n_chip * lax.axis_size("c")
    me = chip * lax.axis_size("c") + core
    s_flat = s_loc.reshape(group_count, -1)
    s_all = gather_earlier(s_flat, n_ctx).reshape((n_ctx,) + s_loc.shape)
    gap = (me - 1 - jnp.arange(n_ctx)).astype(jnp.float32)
    fac = jnp.exp(-decay_rate[None] * (block_len * jnp.maximum(gap, 0.0))[:, None, None])
    fac = jnp.where(gap[:, None, None] >= 0.0, fac, 0.0)
    s_in = jnp.einsum("kgr,kgrc->grc", fac, s_all, precision=HIGH)
    f_mat = pole_weight[:, None, :] * jnp.exp(-lam * (pos + 1.0)[None, :, None])
    far = jnp.einsum("gtr,grc->tgc", f_mat, s_in, precision=HIGH)
    long_out = (near + far).reshape(block_len, local_width)
    out = query * (long_out + skip * gated.astype(jnp.float32))
    return out.astype(jnp.bfloat16)


def solution(mesh):
    n_ctx, n_ch = mesh.devices.shape
    sub = Mesh(mesh.devices.reshape(n_ctx // 2, 2, n_ch), ("p", "c", "ch"))
    ctx = ("p", "c")
    return jax.shard_map(
        local,
        mesh=sub,
        in_specs=(
            P(ctx, "ch"),
            P(ctx, None, "ch"),
            P(None, None, "ch"),
            P("ch", None),
            P("ch", None),
            P("ch"),
        ),
        out_specs=P(ctx, "ch"),
        check_vma=False,
    )
```

```python
import jax
import jax.numpy as jnp
from jax import lax
from jax.experimental import pallas as pl
from jax.experimental.pallas import tpu as pltpu
from jax.sharding import Mesh
from jax.sharding import PartitionSpec as P

GROUP = 16
HIGH = lax.Precision.HIGHEST


def split_bf16(x):
    hi = x.astype(jnp.bfloat16)
    lo = (x - hi.astype(jnp.float32)).astype(jnp.bfloat16)
    return hi, lo


def dot_split(spec, weight, data):
    hi, lo = split_bf16(weight)
    return jnp.einsum(spec, hi, data, preferred_element_type=jnp.float32) + jnp.einsum(
        spec, lo, data, preferred_element_type=jnp.float32
    )


CYCLES = (
    (0, 1, 3, 2, 4, 5, 7, 6),
    (0, 1, 3, 5, 7, 6, 4, 2),
    (0, 1, 7, 5, 3, 2, 4, 6),
    (0, 1, 7, 6, 4, 5, 3, 2),
    (0, 2, 3, 1, 7, 5, 4, 6),
    (0, 2, 4, 5, 3, 1, 7, 6),
)


def lookup(table, v):
    n = len(table)
    total = 0
    for k, t in enumerate(table):
        if t:
            total = total + t * (1 - ((v - k + n) % n + n - 1) // n)
    return total


def ring_chip(r, n):
    hi = r // (n // 2)
    return 2 * (r + hi * (n - 1 - 2 * r)) + hi


def ring_pos(p, n):
    z, y = p // 2, p % 2
    return z + y * (n - 1 - 2 * z)


def rs_kernel(tok_ref, w_ref, taps_ref, q_ref, g_ref, sbuf, rbuf, proj, send_sem, recv_sem):
    n, ext_len, _ = tok_ref.shape
    width = w_ref.shape[1]
    n_ring = sbuf.shape[0]
    chunk = width // n_ring
    chip = lax.axis_index("p")
    core = lax.axis_index("c")
    col = lax.axis_index("ch")
    mesh_id = pl.DeviceIdType.MESH
    rings = []
    for cyc in CYCLES:
        inv = [cyc.index(p) for p in range(n)]
        r = lookup(inv, chip)
        for d in (1, -1):
            rings.append((cyc, d, r, lookup(cyc, (r + d + n) % n)))
    z, y = chip // 2, chip % 2
    n_z = n // 2
    neighbours = (2 * ((z + 1) % n_z) + y, 2 * ((z + n_z - 1) % n_z) + y, 2 * z + 1 - y)
    barrier = pltpu.get_barrier_semaphore()
    for nb in neighbours:
        pl.semaphore_signal(barrier, 1, device_id=(nb, core, col), device_id_type=mesh_id)
    pl.semaphore_wait(barrier, len(neighbours))

    def part(blk, cols):
        return jnp.dot(tok_ref[blk], w_ref[:, cols], preferred_element_type=jnp.float32)

    copies = [[] for _ in range(n_ring)]
    order = list(range(n_ring))
    for s in range(n - 1):
        for ring in order:
            cyc, d, r, dest = rings[ring]
            cols = pl.ds(ring * chunk, chunk)
            q = lookup(cyc, (r - d * (1 + s) + 2 * n) % n)
            if s == 0:
                sbuf[ring, 0] = part(q, cols).astype(sbuf.dtype)
            else:
                mine = part(q, cols)
                copies[ring][s - 1].wait_recv()
                sbuf[ring, s] = (rbuf[ring, s - 1].astype(jnp.float32) + mine).astype(sbuf.dtype)
            copy = pltpu.make_async_remote_copy(
                src_ref=sbuf.at[ring, s],
                dst_ref=rbuf.at[ring, s],
                send_sem=send_sem.at[ring, s],
                recv_sem=recv_sem.at[ring, s],
                device_id=(dest, core, col),
                device_id_type=mesh_id,
            )
            copy.start()
            copies[ring].append(copy)
    for ring in order:
        cols = pl.ds(ring * chunk, chunk)
        mine = part(chip, cols)
        copies[ring][-1].wait_recv()
        total = rbuf[ring, n - 2].astype(jnp.float32) + mine
        proj[:, cols] = total.astype(jnp.bfloat16).astype(jnp.float32)

    @pl.when(jnp.logical_and(chip == 0, core == 0))
    def _():
        proj[0:2, :] = jnp.zeros((2, width), jnp.float32)

    rows = ext_len - 2
    third = width // 3
    mixed = []
    for j in range(3):
        cols = pl.ds(j * third, third)
        mixed.append(
            taps_ref[0, j][None, :] * proj[pl.ds(2, rows), cols]
            + taps_ref[1, j][None, :] * proj[pl.ds(1, rows), cols]
            + taps_ref[2, j][None, :] * proj[pl.ds(0, rows), cols]
        )
    q_ref[...] = mixed[0]
    g_ref[...] = (mixed[1] * mixed[2]).astype(g_ref.dtype)
    for ring in order:
        for copy in copies[ring]:
            copy.wait_send()


def project_and_gate(tok_ext, w_flat, taps, n_ring=2 * len(CYCLES)):
    n, ext_len, _ = tok_ext.shape
    width = w_flat.shape[1]
    rows, third = ext_len - 2, width // 3
    vmem = pl.BlockSpec(memory_space=pltpu.VMEM)
    return pl.pallas_call(
        rs_kernel,
        out_shape=(
            jax.ShapeDtypeStruct((rows, third), jnp.float32),
            jax.ShapeDtypeStruct((rows, third), jnp.bfloat16),
        ),
        in_specs=[vmem, vmem, vmem],
        out_specs=(vmem, vmem),
        scratch_shapes=[
            pltpu.VMEM((n_ring, n - 1, ext_len, width // n_ring), jnp.bfloat16),
            pltpu.VMEM((n_ring, n - 1, ext_len, width // n_ring), jnp.bfloat16),
            pltpu.VMEM((ext_len, width), jnp.float32),
            pltpu.SemaphoreType.DMA((n_ring, n - 1)),
            pltpu.SemaphoreType.DMA((n_ring, n - 1)),
        ],
        compiler_params=pltpu.CompilerParams(
            collective_id=0, has_side_effects=True, vmem_limit_bytes=48 * 1024 * 1024
        ),
    )(tok_ext, w_flat, taps)


def tok_kernel(src_ref, out_ref, send_sem, recv_sem):
    n = out_ref.shape[0]
    chip = lax.axis_index("p")
    core = lax.axis_index("c")
    col = lax.axis_index("ch")
    mesh_id = pl.DeviceIdType.MESH
    diag = chip == col
    barrier = pltpu.get_barrier_semaphore()
    for k in range(n):
        dest = (col, core, (chip + k) % n)
        srce = ((chip + k) % n, core, chip)
        if k == 0:
            @pl.when(jnp.logical_not(diag))
            def _():
                pl.semaphore_signal(barrier, 1, device_id=dest, device_id_type=mesh_id)
                pl.semaphore_signal(barrier, 1, device_id=srce, device_id_type=mesh_id)
        else:
            pl.semaphore_signal(barrier, 1, device_id=dest, device_id_type=mesh_id)
            pl.semaphore_signal(barrier, 1, device_id=srce, device_id_type=mesh_id)
    pl.semaphore_wait(barrier, 2 * n - 2 * diag.astype(jnp.int32))
    copies = []
    for k in range(n):
        copy = pltpu.make_async_remote_copy(
            src_ref=src_ref,
            dst_ref=out_ref.at[chip],
            send_sem=send_sem.at[k],
            recv_sem=recv_sem.at[chip],
            device_id=(col, core, (chip + k) % n),
            device_id_type=mesh_id,
        )
        if k == 0:
            own = pltpu.make_async_copy(src_ref, out_ref.at[chip], recv_sem.at[chip])

            @pl.when(diag)
            def _():
                own.start()

            @pl.when(jnp.logical_not(diag))
            def _():
                copy.start()
        else:
            copy.start()
        copies.append(copy)
    for j in range(n):
        pltpu.make_async_copy(src_ref, out_ref.at[j], recv_sem.at[j]).wait()
    for k in range(n):
        if k == 0:
            @pl.when(jnp.logical_not(diag))
            def _():
                copies[0].wait_send()
        else:
            copies[k].wait_send()


def spread_tokens(tokens, n):
    rows, width = tokens.shape
    return pl.pallas_call(
        tok_kernel,
        out_shape=jax.ShapeDtypeStruct((n, rows, width), tokens.dtype),
        in_specs=[pl.BlockSpec(memory_space=pltpu.VMEM)],
        out_specs=pl.BlockSpec(memory_space=pltpu.VMEM),
        scratch_shapes=[pltpu.SemaphoreType.DMA((n,)), pltpu.SemaphoreType.DMA((n,))],
        compiler_params=pltpu.CompilerParams(collective_id=1, has_side_effects=True),
    )(tokens)


def state_kernel(src_ref, out_ref, send_sem, recv_sem):
    n = out_ref.shape[0]
    n_core = lax.axis_size("c")
    me = lax.axis_index("p") * n_core + lax.axis_index("c")
    col = lax.axis_index("ch")
    mesh_id = pl.DeviceIdType.MESH
    barrier = pltpu.get_barrier_semaphore()
    for k in range(1, n):
        other = (me + k) % n
        pl.semaphore_signal(
            barrier, 1, device_id=(other // n_core, other % n_core, col), device_id_type=mesh_id
        )
    for j in range(n):
        @pl.when(j >= me)
        def _():
            out_ref[j] = jnp.zeros(out_ref.shape[1:], out_ref.dtype)
    pl.semaphore_wait(barrier, n - 1)
    copies = []
    for k in range(1, n):
        other = me + k
        copy = pltpu.make_async_remote_copy(
            src_ref=src_ref,
            dst_ref=out_ref.at[me],
            send_sem=send_sem.at[k],
            recv_sem=recv_sem.at[me],
            device_id=(other // n_core, other % n_core, col),
            device_id_type=mesh_id,
        )

        @pl.when(other < n)
        def _():
            copy.start()

        copies.append((other, copy))
    for j in range(n):
        @pl.when(j < me)
        def _():
            pltpu.make_async_copy(src_ref, out_ref.at[j], recv_sem.at[j]).wait()
    for other, copy in copies:
        @pl.when(other < n)
        def _():
            copy.wait_send()


def gather_earlier(state, n):
    return pl.pallas_call(
        state_kernel,
        out_shape=jax.ShapeDtypeStruct((n,) + state.shape, state.dtype),
        in_specs=[pl.BlockSpec(memory_space=pltpu.VMEM)],
        out_specs=pl.BlockSpec(memory_space=pltpu.VMEM),
        scratch_shapes=[pltpu.SemaphoreType.DMA((n,)), pltpu.SemaphoreType.DMA((n,))],
        compiler_params=pltpu.CompilerParams(collective_id=2, has_side_effects=True),
    )(state)


def local(tokens, w_in, short_filter, decay_rate, residue, skip):
    n_chip = lax.axis_size("p")
    block_len = tokens.shape[0]
    local_width = w_in.shape[2]
    group_count = local_width // GROUP
    chip = lax.axis_index("p")
    core = lax.axis_index("c")
    col = lax.axis_index("ch")

    n_col = lax.axis_size("ch")
    tok_t = spread_tokens(tokens, n_col)
    w_flat = w_in.reshape(w_in.shape[0], -1)
    w_other = lax.ppermute(w_flat, "c", [(0, 1), (1, 0)])
    flat_w = jnp.where(
        core == 0,
        jnp.concatenate([w_flat, w_other], axis=0),
        jnp.concatenate([w_other, w_flat], axis=0),
    )

    tail = tok_t[:, block_len - 2 :]
    partner_tail = lax.ppermute(tail, "c", [(0, 1), (1, 0)])
    shifted_tail = jnp.concatenate([jnp.zeros_like(partner_tail[:1]), partner_tail[:-1]], axis=0)
    prior = jnp.where(core == 1, partner_tail, shifted_tail)
    tok_ext = jnp.concatenate([prior, tok_t], axis=1)
    query, gated = project_and_gate(tok_ext, flat_w, short_filter)
    x = gated.reshape(block_len, group_count, GROUP)

    pole_weight = residue * jnp.sqrt(2.0 * decay_rate)
    pos = jnp.arange(block_len, dtype=jnp.float32)
    lam = decay_rate[:, None, :]
    a_mat = pole_weight[:, None, :] * jnp.exp(-lam * pos[None, :, None])
    b_mat = jnp.exp(lam * pos[None, :, None])
    toep = jnp.einsum("gtr,gsr->gts", a_mat, b_mat, precision=HIGH)
    causal = pos[:, None] >= pos[None, :]
    toep = jnp.where(causal[None], toep, 0.0)
    near = dot_split("gts,sgc->tgc", toep, x)

    e_mat = jnp.exp(-lam * (block_len - 1 - pos)[None, :, None])
    s_loc = dot_split("gsr,sgc->grc", e_mat, x)
    n_ctx = n_chip * lax.axis_size("c")
    me = chip * lax.axis_size("c") + core
    s_flat = s_loc.reshape(group_count, -1)
    s_all = gather_earlier(s_flat, n_ctx).reshape((n_ctx,) + s_loc.shape)
    gap = (me - 1 - jnp.arange(n_ctx)).astype(jnp.float32)
    fac = jnp.exp(-decay_rate[None] * (block_len * jnp.maximum(gap, 0.0))[:, None, None])
    fac = jnp.where(gap[:, None, None] >= 0.0, fac, 0.0)
    s_in = jnp.einsum("kgr,kgrc->grc", fac, s_all, precision=HIGH)
    f_mat = pole_weight[:, None, :] * jnp.exp(-lam * (pos + 1.0)[None, :, None])
    far = jnp.einsum("gtr,grc->tgc", f_mat, s_in, precision=HIGH)
    long_out = (near + far).reshape(block_len, local_width)
    out = query * (long_out + skip * gated.astype(jnp.float32))
    return out.astype(jnp.bfloat16)


def solution(mesh):
    n_ctx, n_ch = mesh.devices.shape
    sub = Mesh(mesh.devices.reshape(n_ctx // 2, 2, n_ch), ("p", "c", "ch"))
    ctx = ("p", "c")
    return jax.shard_map(
        local,
        mesh=sub,
        in_specs=(
            P(ctx, "ch"),
            P(ctx, None, "ch"),
            P(None, None, "ch"),
            P("ch", None),
            P("ch", None),
            P("ch"),
        ),
        out_specs=P(ctx, "ch"),
        check_vma=False,
    )
```

```python
import jax
import jax.numpy as jnp
from jax import lax
from jax.experimental import pallas as pl
from jax.experimental.pallas import tpu as pltpu
from jax.sharding import Mesh
from jax.sharding import PartitionSpec as P

GROUP = 16
HIGH = lax.Precision.HIGHEST


def split_bf16(x):
    hi = x.astype(jnp.bfloat16)
    lo = (x - hi.astype(jnp.float32)).astype(jnp.bfloat16)
    return hi, lo


def dot_split(spec, weight, data):
    hi, lo = split_bf16(weight)
    return jnp.einsum(spec, hi, data, preferred_element_type=jnp.float32) + jnp.einsum(
        spec, lo, data, preferred_element_type=jnp.float32
    )


CYCLES = (
    (0, 1, 3, 2, 4, 5, 7, 6),
    (0, 1, 3, 5, 7, 6, 4, 2),
    (0, 1, 7, 5, 3, 2, 4, 6),
    (0, 1, 7, 6, 4, 5, 3, 2),
    (0, 2, 3, 1, 7, 5, 4, 6),
    (0, 2, 4, 5, 3, 1, 7, 6),
)


def lookup(table, v):
    n = len(table)
    total = 0
    for k, t in enumerate(table):
        if t:
            total = total + t * (1 - ((v - k + n) % n + n - 1) // n)
    return total


def ring_chip(r, n):
    hi = r // (n // 2)
    return 2 * (r + hi * (n - 1 - 2 * r)) + hi


def ring_pos(p, n):
    z, y = p // 2, p % 2
    return z + y * (n - 1 - 2 * z)


def rs_kernel(
    tok_ref, prior_ref, w_own, w_other, taps_ref, q_ref, g_ref, sbuf, rbuf, proj, send_sem, recv_sem
):
    n, rows, _ = tok_ref.shape
    tail = prior_ref.shape[1]
    ext_len = rows + tail
    half, width = w_own.shape
    n_ring = sbuf.shape[0]
    chunk = width // n_ring
    chip = lax.axis_index("p")
    core = lax.axis_index("c")
    col = lax.axis_index("ch")
    mesh_id = pl.DeviceIdType.MESH
    rings = []
    for cyc in CYCLES:
        inv = [cyc.index(p) for p in range(n)]
        r = lookup(inv, chip)
        for d in (1, -1):
            rings.append((cyc, d, r, lookup(cyc, (r + d + n) % n)))
    z, y = chip // 2, chip % 2
    n_z = n // 2
    neighbours = (2 * ((z + 1) % n_z) + y, 2 * ((z + n_z - 1) % n_z) + y, 2 * z + 1 - y)
    barrier = pltpu.get_barrier_semaphore()
    for nb in neighbours:
        pl.semaphore_signal(barrier, 1, device_id=(nb, core, col), device_id_type=mesh_id)
    pl.semaphore_wait(barrier, len(neighbours))

    own_cols = pl.ds(pl.multiple_of(core * half, half), half)
    other_cols = pl.ds(pl.multiple_of((1 - core) * half, half), half)

    def part(blk, cols):
        def proj_rows(ref):
            return jnp.dot(
                ref[blk, :, own_cols], w_own[:, cols], preferred_element_type=jnp.float32
            ) + jnp.dot(ref[blk, :, other_cols], w_other[:, cols], preferred_element_type=jnp.float32)

        return jnp.concatenate([proj_rows(tok_ref), proj_rows(prior_ref)], axis=0)

    copies = [[] for _ in range(n_ring)]
    order = list(range(n_ring))
    for s in range(n - 1):
        for ring in order:
            cyc, d, r, dest = rings[ring]
            cols = pl.ds(ring * chunk, chunk)
            q = lookup(cyc, (r - d * (1 + s) + 2 * n) % n)
            if s == 0:
                sbuf[ring, 0] = part(q, cols).astype(sbuf.dtype)
            else:
                mine = part(q, cols)
                copies[ring][s - 1].wait_recv()
                sbuf[ring, s] = (rbuf[ring, s - 1].astype(jnp.float32) + mine).astype(sbuf.dtype)
            copy = pltpu.make_async_remote_copy(
                src_ref=sbuf.at[ring, s],
                dst_ref=rbuf.at[ring, s],
                send_sem=send_sem.at[ring, s],
                recv_sem=recv_sem.at[ring, s],
                device_id=(dest, core, col),
                device_id_type=mesh_id,
            )
            copy.start()
            copies[ring].append(copy)
    for ring in order:
        cols = pl.ds(ring * chunk, chunk)
        mine = part(chip, cols)
        copies[ring][-1].wait_recv()
        total = (rbuf[ring, n - 2].astype(jnp.float32) + mine).astype(jnp.bfloat16)
        total = total.astype(jnp.float32)
        proj[pl.ds(tail, rows), cols] = total[:rows]
        proj[pl.ds(0, tail), cols] = total[rows:]

    @pl.when(jnp.logical_and(chip == 0, core == 0))
    def _():
        proj[0:2, :] = jnp.zeros((2, width), jnp.float32)

    third = width // 3
    mixed = []
    for j in range(3):
        cols = pl.ds(j * third, third)
        mixed.append(
            taps_ref[0, j][None, :] * proj[pl.ds(2, rows), cols]
            + taps_ref[1, j][None, :] * proj[pl.ds(1, rows), cols]
            + taps_ref[2, j][None, :] * proj[pl.ds(0, rows), cols]
        )
    q_ref[...] = mixed[0]
    g_ref[...] = (mixed[1] * mixed[2]).astype(g_ref.dtype)
    for ring in order:
        for copy in copies[ring]:
            copy.wait_send()


def project_and_gate(tok, prior, w_own, w_other, taps, n_ring=2 * len(CYCLES)):
    n, rows, _ = tok.shape
    ext_len = rows + prior.shape[1]
    width = w_own.shape[1]
    third = width // 3
    vmem = pl.BlockSpec(memory_space=pltpu.VMEM)
    return pl.pallas_call(
        rs_kernel,
        out_shape=(
            jax.ShapeDtypeStruct((rows, third), jnp.float32),
            jax.ShapeDtypeStruct((rows, third), jnp.bfloat16),
        ),
        in_specs=[vmem] * 5,
        out_specs=(vmem, vmem),
        scratch_shapes=[
            pltpu.VMEM((n_ring, n - 1, ext_len, width // n_ring), jnp.bfloat16),
            pltpu.VMEM((n_ring, n - 1, ext_len, width // n_ring), jnp.bfloat16),
            pltpu.VMEM((ext_len, width), jnp.float32),
            pltpu.SemaphoreType.DMA((n_ring, n - 1)),
            pltpu.SemaphoreType.DMA((n_ring, n - 1)),
        ],
        compiler_params=pltpu.CompilerParams(
            collective_id=0, has_side_effects=True, vmem_limit_bytes=48 * 1024 * 1024
        ),
    )(tok, prior, w_own, w_other, taps)


def tok_kernel(src_ref, out_ref, prior_ref, send_sem, recv_sem, psend_sem, precv_sem):
    n, rows, _ = out_ref.shape
    tail = prior_ref.shape[1]
    chip = lax.axis_index("p")
    core = lax.axis_index("c")
    col = lax.axis_index("ch")
    other = 1 - core
    mesh_id = pl.DeviceIdType.MESH
    diag = chip == col
    barrier = pltpu.get_barrier_semaphore()
    for k in range(n):
        dest = (col, core, (chip + k) % n)
        srce = ((chip + k) % n, core, chip)
        if k == 0:
            @pl.when(jnp.logical_not(diag))
            def _():
                pl.semaphore_signal(barrier, 1, device_id=dest, device_id_type=mesh_id)
                pl.semaphore_signal(barrier, 1, device_id=srce, device_id_type=mesh_id)
        else:
            pl.semaphore_signal(barrier, 1, device_id=dest, device_id_type=mesh_id)
            pl.semaphore_signal(barrier, 1, device_id=srce, device_id_type=mesh_id)
        pl.semaphore_signal(
            barrier, 1, device_id=(col, other, (chip + k) % n), device_id_type=mesh_id
        )
        pl.semaphore_signal(
            barrier, 1, device_id=((chip + k) % n, other, chip), device_id_type=mesh_id
        )
    pl.semaphore_wait(barrier, 4 * n - 2 * diag.astype(jnp.int32))
    slot = (chip + core) % n
    copies = []
    for k in range(n):
        copy = pltpu.make_async_remote_copy(
            src_ref=src_ref,
            dst_ref=out_ref.at[chip],
            send_sem=send_sem.at[k],
            recv_sem=recv_sem.at[chip],
            device_id=(col, core, (chip + k) % n),
            device_id_type=mesh_id,
        )
        if k == 0:
            own = pltpu.make_async_copy(src_ref, out_ref.at[chip], recv_sem.at[chip])

            @pl.when(diag)
            def _():
                own.start()

            @pl.when(jnp.logical_not(diag))
            def _():
                copy.start()
        else:
            copy.start()
        copies.append(copy)
    pcopies = []
    for k in range(n):
        pcopy = pltpu.make_async_remote_copy(
            src_ref=src_ref.at[pl.ds(rows - tail, tail)],
            dst_ref=prior_ref.at[slot],
            send_sem=psend_sem.at[k],
            recv_sem=precv_sem.at[slot],
            device_id=(col, other, (chip + k) % n),
            device_id_type=mesh_id,
        )
        pcopy.start()
        pcopies.append(pcopy)
    for j in range(n):
        pltpu.make_async_copy(src_ref, out_ref.at[j], recv_sem.at[j]).wait()
        pltpu.make_async_copy(
            src_ref.at[pl.ds(rows - tail, tail)], prior_ref.at[j], precv_sem.at[j]
        ).wait()
    for k in range(n):
        if k == 0:
            @pl.when(jnp.logical_not(diag))
            def _():
                copies[0].wait_send()
        else:
            copies[k].wait_send()
        pcopies[k].wait_send()


def spread_tokens(tokens, n, tail=2):
    rows, width = tokens.shape
    vmem = pl.BlockSpec(memory_space=pltpu.VMEM)
    return pl.pallas_call(
        tok_kernel,
        out_shape=(
            jax.ShapeDtypeStruct((n, rows, width), tokens.dtype),
            jax.ShapeDtypeStruct((n, tail, width), tokens.dtype),
        ),
        in_specs=[vmem],
        out_specs=(vmem, vmem),
        scratch_shapes=[pltpu.SemaphoreType.DMA((n,))] * 4,
        compiler_params=pltpu.CompilerParams(collective_id=1, has_side_effects=True),
    )(tokens)


def state_kernel(src_ref, out_ref, send_sem, recv_sem):
    n = out_ref.shape[0]
    n_core = lax.axis_size("c")
    me = lax.axis_index("p") * n_core + lax.axis_index("c")
    col = lax.axis_index("ch")
    mesh_id = pl.DeviceIdType.MESH
    barrier = pltpu.get_barrier_semaphore()
    for k in range(1, n):
        other = (me + k) % n
        pl.semaphore_signal(
            barrier, 1, device_id=(other // n_core, other % n_core, col), device_id_type=mesh_id
        )
    for j in range(n):
        @pl.when(j >= me)
        def _():
            out_ref[j] = jnp.zeros(out_ref.shape[1:], out_ref.dtype)
    pl.semaphore_wait(barrier, n - 1)
    copies = []
    for k in range(1, n):
        other = me + k
        copy = pltpu.make_async_remote_copy(
            src_ref=src_ref,
            dst_ref=out_ref.at[me],
            send_sem=send_sem.at[k],
            recv_sem=recv_sem.at[me],
            device_id=(other // n_core, other % n_core, col),
            device_id_type=mesh_id,
        )

        @pl.when(other < n)
        def _():
            copy.start()

        copies.append((other, copy))
    for j in range(n):
        @pl.when(j < me)
        def _():
            pltpu.make_async_copy(src_ref, out_ref.at[j], recv_sem.at[j]).wait()
    for other, copy in copies:
        @pl.when(other < n)
        def _():
            copy.wait_send()


def gather_earlier(state, n):
    return pl.pallas_call(
        state_kernel,
        out_shape=jax.ShapeDtypeStruct((n,) + state.shape, state.dtype),
        in_specs=[pl.BlockSpec(memory_space=pltpu.VMEM)],
        out_specs=pl.BlockSpec(memory_space=pltpu.VMEM),
        scratch_shapes=[pltpu.SemaphoreType.DMA((n,)), pltpu.SemaphoreType.DMA((n,))],
        compiler_params=pltpu.CompilerParams(collective_id=2, has_side_effects=True),
    )(state)


def local(tokens, w_in, short_filter, decay_rate, residue, skip):
    n_chip = lax.axis_size("p")
    block_len = tokens.shape[0]
    local_width = w_in.shape[2]
    group_count = local_width // GROUP
    chip = lax.axis_index("p")
    core = lax.axis_index("c")
    col = lax.axis_index("ch")

    n_col = lax.axis_size("ch")
    tok_t, prior = spread_tokens(tokens, n_col)
    w_own = w_in.reshape(w_in.shape[0], -1)
    w_other = lax.ppermute(w_own, "c", [(0, 1), (1, 0)])
    query, gated = project_and_gate(tok_t, prior, w_own, w_other, short_filter)
    x = gated.reshape(block_len, group_count, GROUP)

    pole_weight = residue * jnp.sqrt(2.0 * decay_rate)
    pos = jnp.arange(block_len, dtype=jnp.float32)
    lam = decay_rate[:, None, :]
    a_mat = pole_weight[:, None, :] * jnp.exp(-lam * pos[None, :, None])
    b_mat = jnp.exp(lam * pos[None, :, None])
    toep = jnp.einsum("gtr,gsr->gts", a_mat, b_mat, precision=HIGH)
    causal = pos[:, None] >= pos[None, :]
    toep = jnp.where(causal[None], toep, 0.0)
    near = dot_split("gts,sgc->tgc", toep, x)

    e_mat = jnp.exp(-lam * (block_len - 1 - pos)[None, :, None])
    s_loc = dot_split("gsr,sgc->grc", e_mat, x)
    n_ctx = n_chip * lax.axis_size("c")
    me = chip * lax.axis_size("c") + core
    s_flat = s_loc.reshape(group_count, -1)
    s_all = gather_earlier(s_flat, n_ctx).reshape((n_ctx,) + s_loc.shape)
    gap = (me - 1 - jnp.arange(n_ctx)).astype(jnp.float32)
    fac = jnp.exp(-decay_rate[None] * (block_len * jnp.maximum(gap, 0.0))[:, None, None])
    fac = jnp.where(gap[:, None, None] >= 0.0, fac, 0.0)
    s_in = jnp.einsum("kgr,kgrc->grc", fac, s_all, precision=HIGH)
    f_mat = pole_weight[:, None, :] * jnp.exp(-lam * (pos + 1.0)[None, :, None])
    far = jnp.einsum("gtr,grc->tgc", f_mat, s_in, precision=HIGH)
    long_out = (near + far).reshape(block_len, local_width)
    out = query * (long_out + skip * gated.astype(jnp.float32))
    return out.astype(jnp.bfloat16)


def solution(mesh):
    n_ctx, n_ch = mesh.devices.shape
    sub = Mesh(mesh.devices.reshape(n_ctx // 2, 2, n_ch), ("p", "c", "ch"))
    ctx = ("p", "c")
    return jax.shard_map(
        local,
        mesh=sub,
        in_specs=(
            P(ctx, "ch"),
            P(ctx, None, "ch"),
            P(None, None, "ch"),
            P("ch", None),
            P("ch", None),
            P("ch"),
        ),
        out_specs=P(ctx, "ch"),
        check_vma=False,
    )
```

```python
import jax
import jax.numpy as jnp
from jax import lax
from jax.experimental import pallas as pl
from jax.experimental.pallas import tpu as pltpu
from jax.sharding import Mesh
from jax.sharding import PartitionSpec as P

GROUP = 16
HIGH = lax.Precision.HIGHEST


def split_bf16(x):
    hi = x.astype(jnp.bfloat16)
    lo = (x - hi.astype(jnp.float32)).astype(jnp.bfloat16)
    return hi, lo


def dot_split(spec, weight, data):
    hi, lo = split_bf16(weight)
    return jnp.einsum(spec, hi, data, preferred_element_type=jnp.float32) + jnp.einsum(
        spec, lo, data, preferred_element_type=jnp.float32
    )


CYCLES = (
    (0, 1, 3, 2, 4, 5, 7, 6),
    (0, 1, 3, 5, 7, 6, 4, 2),
    (0, 1, 7, 5, 3, 2, 4, 6),
    (0, 1, 7, 6, 4, 5, 3, 2),
    (0, 2, 3, 1, 7, 5, 4, 6),
    (0, 2, 4, 5, 3, 1, 7, 6),
)


def lookup(table, v):
    n = len(table)
    total = 0
    for k, t in enumerate(table):
        if t:
            total = total + t * (1 - ((v - k + n) % n + n - 1) // n)
    return total


def ring_chip(r, n):
    hi = r // (n // 2)
    return 2 * (r + hi * (n - 1 - 2 * r)) + hi


def ring_pos(p, n):
    z, y = p // 2, p % 2
    return z + y * (n - 1 - 2 * z)


def rs_kernel(
    src_ref, w_own, w_other, taps_ref, q_ref, g_ref,
    tok_buf, prior_buf, sbuf, rbuf, proj,
    tsend, trecv, psend, precv, send_sem, recv_sem,
):
    n, rows, _ = tok_buf.shape
    tail = prior_buf.shape[1]
    ext_len = rows + tail
    half, width = w_own.shape
    n_ring = sbuf.shape[0]
    chunk = width // n_ring
    chip = lax.axis_index("p")
    core = lax.axis_index("c")
    col = lax.axis_index("ch")
    other = 1 - core
    mesh_id = pl.DeviceIdType.MESH
    diag = chip == col
    cyc = CYCLES[0]
    r = lookup([cyc.index(p) for p in range(n)], chip)
    nxt = lookup(cyc, (r + 1) % n)
    prv = lookup(cyc, (r + n - 1) % n)

    barrier = pltpu.get_barrier_semaphore()
    for k in range(n):
        dest = (col, core, (chip + k) % n)
        srce = ((chip + k) % n, core, chip)
        if k == 0:
            @pl.when(jnp.logical_not(diag))
            def _():
                pl.semaphore_signal(barrier, 1, device_id=dest, device_id_type=mesh_id)
                pl.semaphore_signal(barrier, 1, device_id=srce, device_id_type=mesh_id)
        else:
            pl.semaphore_signal(barrier, 1, device_id=dest, device_id_type=mesh_id)
            pl.semaphore_signal(barrier, 1, device_id=srce, device_id_type=mesh_id)
        pl.semaphore_signal(
            barrier, 1, device_id=(col, other, (chip + k) % n), device_id_type=mesh_id
        )
        pl.semaphore_signal(
            barrier, 1, device_id=((chip + k) % n, other, chip), device_id_type=mesh_id
        )
    for nb in (nxt, prv):
        pl.semaphore_signal(barrier, 1, device_id=(nb, core, col), device_id_type=mesh_id)
    pl.semaphore_wait(barrier, 4 * n + 2 - 2 * diag.astype(jnp.int32))

    slot = (chip + core) % n
    tail_rows = src_ref.at[pl.ds(rows - tail, tail)]
    tcopies, pcopies = [], []
    for k in range(n):
        dev = (col, core, (chip + k) % n)
        copy = pltpu.make_async_remote_copy(
            src_ref=src_ref, dst_ref=tok_buf.at[chip], send_sem=tsend.at[k],
            recv_sem=trecv.at[chip], device_id=dev, device_id_type=mesh_id,
        )
        if k == 0:
            own = pltpu.make_async_copy(src_ref, tok_buf.at[chip], trecv.at[chip])

            @pl.when(diag)
            def _():
                own.start()

            @pl.when(jnp.logical_not(diag))
            def _():
                copy.start()
        else:
            copy.start()
        tcopies.append(copy)
    for k in range(n):
        pcopy = pltpu.make_async_remote_copy(
            src_ref=tail_rows, dst_ref=prior_buf.at[slot], send_sem=psend.at[k],
            recv_sem=precv.at[slot], device_id=(col, other, (chip + k) % n),
            device_id_type=mesh_id,
        )
        pcopy.start()
        pcopies.append(pcopy)

    waited = set()

    def arrive(offset):
        if offset in waited:
            return
        waited.add(offset)
        blk = lookup(cyc, (r + offset) % n)
        pltpu.make_async_copy(src_ref, tok_buf.at[blk], trecv.at[blk]).wait()
        pltpu.make_async_copy(tail_rows, prior_buf.at[blk], precv.at[blk]).wait()

    own_cols = pl.ds(pl.multiple_of(core * half, half), half)
    other_cols = pl.ds(pl.multiple_of((1 - core) * half, half), half)

    def part(blk, cols):
        def proj_rows(ref):
            return jnp.dot(
                ref[blk, :, own_cols], w_own[:, cols], preferred_element_type=jnp.float32
            ) + jnp.dot(ref[blk, :, other_cols], w_other[:, cols], preferred_element_type=jnp.float32)

        return jnp.concatenate([proj_rows(tok_buf), proj_rows(prior_buf)], axis=0)

    copies = [[] for _ in range(n_ring)]
    for s in range(n - 1):
        arrive((n - 1 - s) % n)
        arrive((1 + s) % n)
        for ring in range(n_ring):
            fwd = ring < n_ring // 2
            d, dest = (1, nxt) if fwd else (-1, prv)
            cols = pl.ds(ring * chunk, chunk)
            q = lookup(cyc, (r - d * (1 + s) + 2 * n) % n)
            if s == 0:
                sbuf[ring, 0] = part(q, cols).astype(sbuf.dtype)
            else:
                mine = part(q, cols)
                copies[ring][s - 1].wait_recv()
                sbuf[ring, s] = (rbuf[ring, s - 1].astype(jnp.float32) + mine).astype(sbuf.dtype)
            copy = pltpu.make_async_remote_copy(
                src_ref=sbuf.at[ring, s],
                dst_ref=rbuf.at[ring, s],
                send_sem=send_sem.at[ring, s],
                recv_sem=recv_sem.at[ring, s],
                device_id=(dest, core, col),
                device_id_type=mesh_id,
            )
            copy.start()
            copies[ring].append(copy)
    arrive(0)
    for ring in range(n_ring):
        cols = pl.ds(ring * chunk, chunk)
        mine = part(chip, cols)
        copies[ring][-1].wait_recv()
        total = (rbuf[ring, n - 2].astype(jnp.float32) + mine).astype(jnp.bfloat16)
        total = total.astype(jnp.float32)
        proj[pl.ds(tail, rows), cols] = total[:rows]
        proj[pl.ds(0, tail), cols] = total[rows:]

    @pl.when(jnp.logical_and(chip == 0, core == 0))
    def _():
        proj[0:tail, :] = jnp.zeros((tail, width), jnp.float32)

    third = width // 3
    mixed = []
    for j in range(3):
        cols = pl.ds(j * third, third)
        mixed.append(
            taps_ref[0, j][None, :] * proj[pl.ds(2, rows), cols]
            + taps_ref[1, j][None, :] * proj[pl.ds(1, rows), cols]
            + taps_ref[2, j][None, :] * proj[pl.ds(0, rows), cols]
        )
    q_ref[...] = mixed[0]
    g_ref[...] = (mixed[1] * mixed[2]).astype(g_ref.dtype)
    for ring in range(n_ring):
        for copy in copies[ring]:
            copy.wait_send()
    for k in range(n):
        if k == 0:
            @pl.when(jnp.logical_not(diag))
            def _():
                tcopies[0].wait_send()
        else:
            tcopies[k].wait_send()
        pcopies[k].wait_send()


def project_and_gate(tokens, w_own, w_other, taps, n_ring=12, tail=2):
    rows, tok_width = tokens.shape
    n = lax.axis_size("p")
    ext_len = rows + tail
    width = w_own.shape[1]
    third = width // 3
    vmem = pl.BlockSpec(memory_space=pltpu.VMEM)
    return pl.pallas_call(
        rs_kernel,
        out_shape=(
            jax.ShapeDtypeStruct((rows, third), jnp.float32),
            jax.ShapeDtypeStruct((rows, third), jnp.bfloat16),
        ),
        in_specs=[vmem] * 4,
        out_specs=(vmem, vmem),
        scratch_shapes=[
            pltpu.VMEM((n, rows, tok_width), tokens.dtype),
            pltpu.VMEM((n, tail, tok_width), tokens.dtype),
            pltpu.VMEM((n_ring, n - 1, ext_len, width // n_ring), jnp.bfloat16),
            pltpu.VMEM((n_ring, n - 1, ext_len, width // n_ring), jnp.bfloat16),
            pltpu.VMEM((ext_len, width), jnp.float32),
        ]
        + [pltpu.SemaphoreType.DMA((n,))] * 4
        + [pltpu.SemaphoreType.DMA((n_ring, n - 1))] * 2,
        compiler_params=pltpu.CompilerParams(
            collective_id=0, has_side_effects=True, vmem_limit_bytes=48 * 1024 * 1024
        ),
    )(tokens, w_own, w_other, taps)


def tok_kernel(src_ref, out_ref, prior_ref, send_sem, recv_sem, psend_sem, precv_sem):
    n, rows, _ = out_ref.shape
    tail = prior_ref.shape[1]
    chip = lax.axis_index("p")
    core = lax.axis_index("c")
    col = lax.axis_index("ch")
    other = 1 - core
    mesh_id = pl.DeviceIdType.MESH
    diag = chip == col
    barrier = pltpu.get_barrier_semaphore()
    for k in range(n):
        dest = (col, core, (chip + k) % n)
        srce = ((chip + k) % n, core, chip)
        if k == 0:
            @pl.when(jnp.logical_not(diag))
            def _():
                pl.semaphore_signal(barrier, 1, device_id=dest, device_id_type=mesh_id)
                pl.semaphore_signal(barrier, 1, device_id=srce, device_id_type=mesh_id)
        else:
            pl.semaphore_signal(barrier, 1, device_id=dest, device_id_type=mesh_id)
            pl.semaphore_signal(barrier, 1, device_id=srce, device_id_type=mesh_id)
        pl.semaphore_signal(
            barrier, 1, device_id=(col, other, (chip + k) % n), device_id_type=mesh_id
        )
        pl.semaphore_signal(
            barrier, 1, device_id=((chip + k) % n, other, chip), device_id_type=mesh_id
        )
    pl.semaphore_wait(barrier, 4 * n - 2 * diag.astype(jnp.int32))
    slot = (chip + core) % n
    copies = []
    for k in range(n):
        copy = pltpu.make_async_remote_copy(
            src_ref=src_ref,
            dst_ref=out_ref.at[chip],
            send_sem=send_sem.at[k],
            recv_sem=recv_sem.at[chip],
            device_id=(col, core, (chip + k) % n),
            device_id_type=mesh_id,
        )
        if k == 0:
            own = pltpu.make_async_copy(src_ref, out_ref.at[chip], recv_sem.at[chip])

            @pl.when(diag)
            def _():
                own.start()

            @pl.when(jnp.logical_not(diag))
            def _():
                copy.start()
        else:
            copy.start()
        copies.append(copy)
    pcopies = []
    for k in range(n):
        pcopy = pltpu.make_async_remote_copy(
            src_ref=src_ref.at[pl.ds(rows - tail, tail)],
            dst_ref=prior_ref.at[slot],
            send_sem=psend_sem.at[k],
            recv_sem=precv_sem.at[slot],
            device_id=(col, other, (chip + k) % n),
            device_id_type=mesh_id,
        )
        pcopy.start()
        pcopies.append(pcopy)
    for j in range(n):
        pltpu.make_async_copy(src_ref, out_ref.at[j], recv_sem.at[j]).wait()
        pltpu.make_async_copy(
            src_ref.at[pl.ds(rows - tail, tail)], prior_ref.at[j], precv_sem.at[j]
        ).wait()
    for k in range(n):
        if k == 0:
            @pl.when(jnp.logical_not(diag))
            def _():
                copies[0].wait_send()
        else:
            copies[k].wait_send()
        pcopies[k].wait_send()


def spread_tokens(tokens, n, tail=2):
    rows, width = tokens.shape
    vmem = pl.BlockSpec(memory_space=pltpu.VMEM)
    return pl.pallas_call(
        tok_kernel,
        out_shape=(
            jax.ShapeDtypeStruct((n, rows, width), tokens.dtype),
            jax.ShapeDtypeStruct((n, tail, width), tokens.dtype),
        ),
        in_specs=[vmem],
        out_specs=(vmem, vmem),
        scratch_shapes=[pltpu.SemaphoreType.DMA((n,))] * 4,
        compiler_params=pltpu.CompilerParams(collective_id=1, has_side_effects=True),
    )(tokens)


def state_kernel(src_ref, out_ref, send_sem, recv_sem):
    n = out_ref.shape[0]
    n_core = lax.axis_size("c")
    me = lax.axis_index("p") * n_core + lax.axis_index("c")
    col = lax.axis_index("ch")
    mesh_id = pl.DeviceIdType.MESH
    barrier = pltpu.get_barrier_semaphore()
    for k in range(1, n):
        other = (me + k) % n
        pl.semaphore_signal(
            barrier, 1, device_id=(other // n_core, other % n_core, col), device_id_type=mesh_id
        )
    for j in range(n):
        @pl.when(j >= me)
        def _():
            out_ref[j] = jnp.zeros(out_ref.shape[1:], out_ref.dtype)
    pl.semaphore_wait(barrier, n - 1)
    copies = []
    for k in range(1, n):
        other = me + k
        copy = pltpu.make_async_remote_copy(
            src_ref=src_ref,
            dst_ref=out_ref.at[me],
            send_sem=send_sem.at[k],
            recv_sem=recv_sem.at[me],
            device_id=(other // n_core, other % n_core, col),
            device_id_type=mesh_id,
        )

        @pl.when(other < n)
        def _():
            copy.start()

        copies.append((other, copy))
    for j in range(n):
        @pl.when(j < me)
        def _():
            pltpu.make_async_copy(src_ref, out_ref.at[j], recv_sem.at[j]).wait()
    for other, copy in copies:
        @pl.when(other < n)
        def _():
            copy.wait_send()


def gather_earlier(state, n):
    return pl.pallas_call(
        state_kernel,
        out_shape=jax.ShapeDtypeStruct((n,) + state.shape, state.dtype),
        in_specs=[pl.BlockSpec(memory_space=pltpu.VMEM)],
        out_specs=pl.BlockSpec(memory_space=pltpu.VMEM),
        scratch_shapes=[pltpu.SemaphoreType.DMA((n,)), pltpu.SemaphoreType.DMA((n,))],
        compiler_params=pltpu.CompilerParams(collective_id=2, has_side_effects=True),
    )(state)


def local(tokens, w_in, short_filter, decay_rate, residue, skip):
    n_chip = lax.axis_size("p")
    block_len = tokens.shape[0]
    local_width = w_in.shape[2]
    group_count = local_width // GROUP
    chip = lax.axis_index("p")
    core = lax.axis_index("c")
    col = lax.axis_index("ch")

    n_col = lax.axis_size("ch")
    w_own = w_in.reshape(w_in.shape[0], -1)
    w_other = lax.ppermute(w_own, "c", [(0, 1), (1, 0)])
    query, gated = project_and_gate(tokens, w_own, w_other, short_filter)
    x = gated.reshape(block_len, group_count, GROUP)

    pole_weight = residue * jnp.sqrt(2.0 * decay_rate)
    pos = jnp.arange(block_len, dtype=jnp.float32)
    lam = decay_rate[:, None, :]
    a_mat = pole_weight[:, None, :] * jnp.exp(-lam * pos[None, :, None])
    b_mat = jnp.exp(lam * pos[None, :, None])
    toep = jnp.einsum("gtr,gsr->gts", a_mat, b_mat, precision=HIGH)
    causal = pos[:, None] >= pos[None, :]
    toep = jnp.where(causal[None], toep, 0.0)
    near = dot_split("gts,sgc->tgc", toep, x)

    e_mat = jnp.exp(-lam * (block_len - 1 - pos)[None, :, None])
    s_loc = dot_split("gsr,sgc->grc", e_mat, x)
    n_ctx = n_chip * lax.axis_size("c")
    me = chip * lax.axis_size("c") + core
    s_flat = s_loc.reshape(group_count, -1)
    s_all = gather_earlier(s_flat, n_ctx).reshape((n_ctx,) + s_loc.shape)
    gap = (me - 1 - jnp.arange(n_ctx)).astype(jnp.float32)
    fac = jnp.exp(-decay_rate[None] * (block_len * jnp.maximum(gap, 0.0))[:, None, None])
    fac = jnp.where(gap[:, None, None] >= 0.0, fac, 0.0)
    s_in = jnp.einsum("kgr,kgrc->grc", fac, s_all, precision=HIGH)
    f_mat = pole_weight[:, None, :] * jnp.exp(-lam * (pos + 1.0)[None, :, None])
    far = jnp.einsum("gtr,grc->tgc", f_mat, s_in, precision=HIGH)
    long_out = (near + far).reshape(block_len, local_width)
    out = query * (long_out + skip * gated.astype(jnp.float32))
    return out.astype(jnp.bfloat16)


def solution(mesh):
    n_ctx, n_ch = mesh.devices.shape
    sub = Mesh(mesh.devices.reshape(n_ctx // 2, 2, n_ch), ("p", "c", "ch"))
    ctx = ("p", "c")
    return jax.shard_map(
        local,
        mesh=sub,
        in_specs=(
            P(ctx, "ch"),
            P(ctx, None, "ch"),
            P(None, None, "ch"),
            P("ch", None),
            P("ch", None),
            P("ch"),
        ),
        out_specs=P(ctx, "ch"),
        check_vma=False,
    )
```

```python
import jax
import jax.numpy as jnp
from jax import lax
from jax.experimental import pallas as pl
from jax.experimental.pallas import tpu as pltpu
from jax.sharding import Mesh
from jax.sharding import PartitionSpec as P

GROUP = 16
HIGH = lax.Precision.HIGHEST


def split_bf16(x):
    hi = x.astype(jnp.bfloat16)
    lo = (x - hi.astype(jnp.float32)).astype(jnp.bfloat16)
    return hi, lo


def dot_split(spec, weight, data):
    hi, lo = split_bf16(weight)
    return jnp.einsum(spec, hi, data, preferred_element_type=jnp.float32) + jnp.einsum(
        spec, lo, data, preferred_element_type=jnp.float32
    )


CYCLES = (
    (0, 1, 3, 2, 4, 5, 7, 6),
    (0, 1, 3, 5, 7, 6, 4, 2),
    (0, 1, 7, 5, 3, 2, 4, 6),
    (0, 1, 7, 6, 4, 5, 3, 2),
    (0, 2, 3, 1, 7, 5, 4, 6),
    (0, 2, 4, 5, 3, 1, 7, 6),
)


def lookup(table, v):
    n = len(table)
    total = 0
    for k, t in enumerate(table):
        if t:
            total = total + t * (1 - ((v - k + n) % n + n - 1) // n)
    return total


def ring_chip(r, n):
    hi = r // (n // 2)
    return 2 * (r + hi * (n - 1 - 2 * r)) + hi


def ring_pos(p, n):
    z, y = p // 2, p % 2
    return z + y * (n - 1 - 2 * z)


def rs_kernel(
    src_ref, w_own, w_other, taps_ref, q_ref, g_ref,
    tok_buf, prior_buf, sbuf, rbuf, proj,
    tsend, trecv, psend, precv, send_sem, recv_sem,
):
    n, rows, _ = tok_buf.shape
    tail = prior_buf.shape[1]
    ext_len = rows + tail
    half, width = w_own.shape
    n_ring = sbuf.shape[0]
    chunk = width // n_ring
    chip = lax.axis_index("p")
    core = lax.axis_index("c")
    col = lax.axis_index("ch")
    other = 1 - core
    mesh_id = pl.DeviceIdType.MESH
    diag = chip == col
    cyc = CYCLES[0]
    r = lookup([cyc.index(p) for p in range(n)], chip)
    nxt = lookup(cyc, (r + 1) % n)
    prv = lookup(cyc, (r + n - 1) % n)

    barrier = pltpu.get_barrier_semaphore()
    for k in range(n):
        dest = (col, core, (chip + k) % n)
        srce = ((chip + k) % n, core, chip)
        if k == 0:
            @pl.when(jnp.logical_not(diag))
            def _():
                pl.semaphore_signal(barrier, 1, device_id=dest, device_id_type=mesh_id)
                pl.semaphore_signal(barrier, 1, device_id=srce, device_id_type=mesh_id)
        else:
            pl.semaphore_signal(barrier, 1, device_id=dest, device_id_type=mesh_id)
            pl.semaphore_signal(barrier, 1, device_id=srce, device_id_type=mesh_id)
        pl.semaphore_signal(
            barrier, 1, device_id=(col, other, (chip + k) % n), device_id_type=mesh_id
        )
        pl.semaphore_signal(
            barrier, 1, device_id=((chip + k) % n, other, chip), device_id_type=mesh_id
        )
    for nb in (nxt, prv):
        pl.semaphore_signal(barrier, 1, device_id=(nb, core, col), device_id_type=mesh_id)
    pl.semaphore_wait(barrier, 4 * n + 2 - 2 * diag.astype(jnp.int32))

    slot = (chip + core) % n
    tail_rows = src_ref.at[pl.ds(rows - tail, tail)]
    tcopies, pcopies = [], []
    for k in range(n):
        dev = (col, core, (chip + k) % n)
        copy = pltpu.make_async_remote_copy(
            src_ref=src_ref, dst_ref=tok_buf.at[chip], send_sem=tsend.at[k],
            recv_sem=trecv.at[chip], device_id=dev, device_id_type=mesh_id,
        )
        if k == 0:
            own = pltpu.make_async_copy(src_ref, tok_buf.at[chip], trecv.at[chip])

            @pl.when(diag)
            def _():
                own.start()

            @pl.when(jnp.logical_not(diag))
            def _():
                copy.start()
        else:
            copy.start()
        tcopies.append(copy)
    for k in range(n):
        pcopy = pltpu.make_async_remote_copy(
            src_ref=tail_rows, dst_ref=prior_buf.at[slot], send_sem=psend.at[k],
            recv_sem=precv.at[slot], device_id=(col, other, (chip + k) % n),
            device_id_type=mesh_id,
        )
        pcopy.start()
        pcopies.append(pcopy)

    waited = set()

    def arrive(offset):
        if offset in waited:
            return
        waited.add(offset)
        blk = lookup(cyc, (r + offset) % n)
        pltpu.make_async_copy(src_ref, tok_buf.at[blk], trecv.at[blk]).wait()
        pltpu.make_async_copy(tail_rows, prior_buf.at[blk], precv.at[blk]).wait()

    own_cols = pl.ds(pl.multiple_of(core * half, half), half)
    other_cols = pl.ds(pl.multiple_of((1 - core) * half, half), half)

    def part(blk, cols):
        def proj_rows(ref):
            return jnp.dot(
                ref[blk, :, own_cols], w_own[:, cols], preferred_element_type=jnp.float32
            ) + jnp.dot(ref[blk, :, other_cols], w_other[:, cols], preferred_element_type=jnp.float32)

        return jnp.concatenate([proj_rows(tok_buf), proj_rows(prior_buf)], axis=0)

    copies = [[] for _ in range(n_ring)]
    for s in range(n - 1):
        arrive((n - 1 - s) % n)
        arrive((1 + s) % n)
        for ring in range(n_ring):
            fwd = ring < n_ring // 2
            d, dest = (1, nxt) if fwd else (-1, prv)
            cols = pl.ds(ring * chunk, chunk)
            q = lookup(cyc, (r - d * (1 + s) + 2 * n) % n)
            if s == 0:
                sbuf[ring, 0] = part(q, cols).astype(sbuf.dtype)
            else:
                mine = part(q, cols)
                copies[ring][s - 1].wait_recv()
                sbuf[ring, s] = (rbuf[ring, s - 1].astype(jnp.float32) + mine).astype(sbuf.dtype)
            copy = pltpu.make_async_remote_copy(
                src_ref=sbuf.at[ring, s],
                dst_ref=rbuf.at[ring, s],
                send_sem=send_sem.at[ring, s],
                recv_sem=recv_sem.at[ring, s],
                device_id=(dest, core, col),
                device_id_type=mesh_id,
            )
            copy.start()
            copies[ring].append(copy)
    arrive(0)
    for ring in range(n_ring):
        cols = pl.ds(ring * chunk, chunk)
        mine = part(chip, cols)
        copies[ring][-1].wait_recv()
        total = (rbuf[ring, n - 2].astype(jnp.float32) + mine).astype(jnp.bfloat16)
        total = total.astype(jnp.float32)
        proj[pl.ds(tail, rows), cols] = total[:rows]
        proj[pl.ds(0, tail), cols] = total[rows:]

    @pl.when(jnp.logical_and(chip == 0, core == 0))
    def _():
        proj[0:tail, :] = jnp.zeros((tail, width), jnp.float32)

    third = width // 3
    mixed = []
    for j in range(3):
        cols = pl.ds(j * third, third)
        mixed.append(
            taps_ref[0, j][None, :] * proj[pl.ds(2, rows), cols]
            + taps_ref[1, j][None, :] * proj[pl.ds(1, rows), cols]
            + taps_ref[2, j][None, :] * proj[pl.ds(0, rows), cols]
        )
    q_ref[...] = mixed[0]
    g_ref[...] = (mixed[1] * mixed[2]).astype(g_ref.dtype)
    for ring in range(n_ring):
        for copy in copies[ring]:
            copy.wait_send()
    for k in range(n):
        if k == 0:
            @pl.when(jnp.logical_not(diag))
            def _():
                tcopies[0].wait_send()
        else:
            tcopies[k].wait_send()
        pcopies[k].wait_send()


def project_and_gate(tokens, w_own, w_other, taps, n_ring=12, tail=2):
    rows, tok_width = tokens.shape
    n = lax.axis_size("p")
    ext_len = rows + tail
    width = w_own.shape[1]
    third = width // 3
    vmem = pl.BlockSpec(memory_space=pltpu.VMEM)
    return pl.pallas_call(
        rs_kernel,
        out_shape=(
            jax.ShapeDtypeStruct((rows, third), jnp.float32),
            jax.ShapeDtypeStruct((rows, third), jnp.bfloat16),
        ),
        in_specs=[vmem] * 4,
        out_specs=(vmem, vmem),
        scratch_shapes=[
            pltpu.VMEM((n, rows, tok_width), tokens.dtype),
            pltpu.VMEM((n, tail, tok_width), tokens.dtype),
            pltpu.VMEM((n_ring, n - 1, ext_len, width // n_ring), jnp.bfloat16),
            pltpu.VMEM((n_ring, n - 1, ext_len, width // n_ring), jnp.bfloat16),
            pltpu.VMEM((ext_len, width), jnp.float32),
        ]
        + [pltpu.SemaphoreType.DMA((n,))] * 4
        + [pltpu.SemaphoreType.DMA((n_ring, n - 1))] * 2,
        compiler_params=pltpu.CompilerParams(
            collective_id=0, has_side_effects=True, vmem_limit_bytes=48 * 1024 * 1024
        ),
    )(tokens, w_own, w_other, taps)


def tok_kernel(src_ref, out_ref, prior_ref, send_sem, recv_sem, psend_sem, precv_sem):
    n, rows, _ = out_ref.shape
    tail = prior_ref.shape[1]
    chip = lax.axis_index("p")
    core = lax.axis_index("c")
    col = lax.axis_index("ch")
    other = 1 - core
    mesh_id = pl.DeviceIdType.MESH
    diag = chip == col
    barrier = pltpu.get_barrier_semaphore()
    for k in range(n):
        dest = (col, core, (chip + k) % n)
        srce = ((chip + k) % n, core, chip)
        if k == 0:
            @pl.when(jnp.logical_not(diag))
            def _():
                pl.semaphore_signal(barrier, 1, device_id=dest, device_id_type=mesh_id)
                pl.semaphore_signal(barrier, 1, device_id=srce, device_id_type=mesh_id)
        else:
            pl.semaphore_signal(barrier, 1, device_id=dest, device_id_type=mesh_id)
            pl.semaphore_signal(barrier, 1, device_id=srce, device_id_type=mesh_id)
        pl.semaphore_signal(
            barrier, 1, device_id=(col, other, (chip + k) % n), device_id_type=mesh_id
        )
        pl.semaphore_signal(
            barrier, 1, device_id=((chip + k) % n, other, chip), device_id_type=mesh_id
        )
    pl.semaphore_wait(barrier, 4 * n - 2 * diag.astype(jnp.int32))
    slot = (chip + core) % n
    copies = []
    for k in range(n):
        copy = pltpu.make_async_remote_copy(
            src_ref=src_ref,
            dst_ref=out_ref.at[chip],
            send_sem=send_sem.at[k],
            recv_sem=recv_sem.at[chip],
            device_id=(col, core, (chip + k) % n),
            device_id_type=mesh_id,
        )
        if k == 0:
            own = pltpu.make_async_copy(src_ref, out_ref.at[chip], recv_sem.at[chip])

            @pl.when(diag)
            def _():
                own.start()

            @pl.when(jnp.logical_not(diag))
            def _():
                copy.start()
        else:
            copy.start()
        copies.append(copy)
    pcopies = []
    for k in range(n):
        pcopy = pltpu.make_async_remote_copy(
            src_ref=src_ref.at[pl.ds(rows - tail, tail)],
            dst_ref=prior_ref.at[slot],
            send_sem=psend_sem.at[k],
            recv_sem=precv_sem.at[slot],
            device_id=(col, other, (chip + k) % n),
            device_id_type=mesh_id,
        )
        pcopy.start()
        pcopies.append(pcopy)
    for j in range(n):
        pltpu.make_async_copy(src_ref, out_ref.at[j], recv_sem.at[j]).wait()
        pltpu.make_async_copy(
            src_ref.at[pl.ds(rows - tail, tail)], prior_ref.at[j], precv_sem.at[j]
        ).wait()
    for k in range(n):
        if k == 0:
            @pl.when(jnp.logical_not(diag))
            def _():
                copies[0].wait_send()
        else:
            copies[k].wait_send()
        pcopies[k].wait_send()


def spread_tokens(tokens, n, tail=2):
    rows, width = tokens.shape
    vmem = pl.BlockSpec(memory_space=pltpu.VMEM)
    return pl.pallas_call(
        tok_kernel,
        out_shape=(
            jax.ShapeDtypeStruct((n, rows, width), tokens.dtype),
            jax.ShapeDtypeStruct((n, tail, width), tokens.dtype),
        ),
        in_specs=[vmem],
        out_specs=(vmem, vmem),
        scratch_shapes=[pltpu.SemaphoreType.DMA((n,))] * 4,
        compiler_params=pltpu.CompilerParams(collective_id=1, has_side_effects=True),
    )(tokens)


def state_kernel(src_ref, fac_ref, out_ref, got, send_sem, recv_sem):
    n = got.shape[0]
    n_core = lax.axis_size("c")
    me = lax.axis_index("p") * n_core + lax.axis_index("c")
    col = lax.axis_index("ch")
    mesh_id = pl.DeviceIdType.MESH
    barrier = pltpu.get_barrier_semaphore()
    for k in range(1, n):
        other = (me + k) % n
        pl.semaphore_signal(
            barrier, 1, device_id=(other // n_core, other % n_core, col), device_id_type=mesh_id
        )
    for j in range(n):
        @pl.when(j >= me)
        def _():
            got[j] = jnp.zeros(got.shape[1:], got.dtype)
    pl.semaphore_wait(barrier, n - 1)
    copies = []
    for k in range(1, n):
        other = me + k
        copy = pltpu.make_async_remote_copy(
            src_ref=src_ref,
            dst_ref=got.at[me],
            send_sem=send_sem.at[k],
            recv_sem=recv_sem.at[me],
            device_id=(other // n_core, other % n_core, col),
            device_id_type=mesh_id,
        )

        @pl.when(other < n)
        def _():
            copy.start()

        copies.append((other, copy))
    for j in range(n):
        @pl.when(j < me)
        def _():
            pltpu.make_async_copy(src_ref, got.at[j], recv_sem.at[j]).wait()
    acc = jnp.zeros(out_ref.shape, jnp.float32)
    for j in range(n):
        acc = acc + fac_ref[j] * got[j]
    out_ref[...] = acc
    for other, copy in copies:
        @pl.when(other < n)
        def _():
            copy.wait_send()


def gather_earlier(state, fac, n):
    vmem = pl.BlockSpec(memory_space=pltpu.VMEM)
    return pl.pallas_call(
        state_kernel,
        out_shape=jax.ShapeDtypeStruct(state.shape, state.dtype),
        in_specs=[vmem, vmem],
        out_specs=vmem,
        scratch_shapes=[
            pltpu.VMEM((n,) + state.shape, state.dtype),
            pltpu.SemaphoreType.DMA((n,)),
            pltpu.SemaphoreType.DMA((n,)),
        ],
        compiler_params=pltpu.CompilerParams(collective_id=2, has_side_effects=True),
    )(state, fac)


def local(tokens, w_in, short_filter, decay_rate, residue, skip):
    n_chip = lax.axis_size("p")
    block_len = tokens.shape[0]
    local_width = w_in.shape[2]
    group_count = local_width // GROUP
    chip = lax.axis_index("p")
    core = lax.axis_index("c")
    col = lax.axis_index("ch")

    n_col = lax.axis_size("ch")
    w_own = w_in.reshape(w_in.shape[0], -1)
    w_other = lax.ppermute(w_own, "c", [(0, 1), (1, 0)])
    query, gated = project_and_gate(tokens, w_own, w_other, short_filter)
    x = gated.reshape(block_len, group_count, GROUP)

    pole_weight = residue * jnp.sqrt(2.0 * decay_rate)
    pos = jnp.arange(block_len, dtype=jnp.float32)
    lam = decay_rate[:, None, :]
    a_mat = pole_weight[:, None, :] * jnp.exp(-lam * pos[None, :, None])
    b_mat = jnp.exp(lam * pos[None, :, None])
    toep = jnp.einsum("gtr,gsr->gts", a_mat, b_mat, precision=lax.Precision.HIGH)
    causal = pos[:, None] >= pos[None, :]
    toep = jnp.where(causal[None], toep, 0.0)
    near = dot_split("gts,sgc->tgc", toep, x)

    e_mat = jnp.exp(-lam * (block_len - 1 - pos)[None, :, None])
    s_loc = dot_split("gsr,sgc->grc", e_mat, x)
    n_ctx = n_chip * lax.axis_size("c")
    me = chip * lax.axis_size("c") + core
    s_flat = s_loc.reshape(group_count, -1)
    gap = (me - 1 - jnp.arange(n_ctx)).astype(jnp.float32)
    fac = jnp.exp(-decay_rate[None] * (block_len * jnp.maximum(gap, 0.0))[:, None, None])
    fac = jnp.where(gap[:, None, None] >= 0.0, fac, 0.0)
    fac = jnp.broadcast_to(fac[..., None], fac.shape + (GROUP,)).reshape(n_ctx, group_count, -1)
    s_in = gather_earlier(s_flat, fac, n_ctx).reshape(s_loc.shape)
    f_mat = pole_weight[:, None, :] * jnp.exp(-lam * (pos + 1.0)[None, :, None])
    far = jnp.einsum("gtr,grc->tgc", f_mat, s_in, precision=HIGH)
    long_out = (near + far).reshape(block_len, local_width)
    out = query * (long_out + skip * gated.astype(jnp.float32))
    return out.astype(jnp.bfloat16)


def solution(mesh):
    n_ctx, n_ch = mesh.devices.shape
    sub = Mesh(mesh.devices.reshape(n_ctx // 2, 2, n_ch), ("p", "c", "ch"))
    ctx = ("p", "c")
    return jax.shard_map(
        local,
        mesh=sub,
        in_specs=(
            P(ctx, "ch"),
            P(ctx, None, "ch"),
            P(None, None, "ch"),
            P("ch", None),
            P("ch", None),
            P("ch"),
        ),
        out_specs=P(ctx, "ch"),
        check_vma=False,
    )
```

```python
import functools

import jax
import jax.numpy as jnp
from jax import lax
from jax.experimental import pallas as pl
from jax.experimental.pallas import tpu as pltpu
from jax.sharding import Mesh
from jax.sharding import PartitionSpec as P

GROUP = 16
HIGH = lax.Precision.HIGHEST


def split_bf16(x):
    hi = x.astype(jnp.bfloat16)
    lo = (x - hi.astype(jnp.float32)).astype(jnp.bfloat16)
    return hi, lo


def dot_split(spec, weight, data):
    hi, lo = split_bf16(weight)
    return jnp.einsum(spec, hi, data, preferred_element_type=jnp.float32) + jnp.einsum(
        spec, lo, data, preferred_element_type=jnp.float32
    )


CYCLES = (
    (0, 1, 3, 2, 4, 5, 7, 6),
    (0, 1, 3, 5, 7, 6, 4, 2),
    (0, 1, 7, 5, 3, 2, 4, 6),
    (0, 1, 7, 6, 4, 5, 3, 2),
    (0, 2, 3, 1, 7, 5, 4, 6),
    (0, 2, 4, 5, 3, 1, 7, 6),
)


def lookup(table, v):
    n = len(table)
    total = 0
    for k, t in enumerate(table):
        if t:
            total = total + t * (1 - ((v - k + n) % n + n - 1) // n)
    return total


def ring_chip(r, n):
    hi = r // (n // 2)
    return 2 * (r + hi * (n - 1 - 2 * r)) + hi


def ring_pos(p, n):
    z, y = p // 2, p % 2
    return z + y * (n - 1 - 2 * z)


def rs_kernel(
    src_ref, w_own, w_other, taps_ref, q_ref, g_ref,
    tok_buf, prior_buf, sbuf, rbuf, proj,
    tsend, trecv, psend, precv, send_sem, recv_sem,
):
    n, rows, _ = tok_buf.shape
    tail = prior_buf.shape[1]
    ext_len = rows + tail
    half, width = w_own.shape
    n_ring = sbuf.shape[0]
    chunk = width // n_ring
    chip = lax.axis_index("p")
    core = lax.axis_index("c")
    col = lax.axis_index("ch")
    other = 1 - core
    mesh_id = pl.DeviceIdType.MESH
    diag = chip == col
    cyc = CYCLES[0]
    r = lookup([cyc.index(p) for p in range(n)], chip)
    nxt = lookup(cyc, (r + 1) % n)
    prv = lookup(cyc, (r + n - 1) % n)

    barrier = pltpu.get_barrier_semaphore()
    for k in range(n):
        dest = (col, core, (chip + k) % n)
        srce = ((chip + k) % n, core, chip)
        if k == 0:
            @pl.when(jnp.logical_not(diag))
            def _():
                pl.semaphore_signal(barrier, 1, device_id=dest, device_id_type=mesh_id)
                pl.semaphore_signal(barrier, 1, device_id=srce, device_id_type=mesh_id)
        else:
            pl.semaphore_signal(barrier, 1, device_id=dest, device_id_type=mesh_id)
            pl.semaphore_signal(barrier, 1, device_id=srce, device_id_type=mesh_id)
        pl.semaphore_signal(
            barrier, 1, device_id=(col, other, (chip + k) % n), device_id_type=mesh_id
        )
        pl.semaphore_signal(
            barrier, 1, device_id=((chip + k) % n, other, chip), device_id_type=mesh_id
        )
    for nb in (nxt, prv):
        pl.semaphore_signal(barrier, 1, device_id=(nb, core, col), device_id_type=mesh_id)
    pl.semaphore_wait(barrier, 4 * n + 2 - 2 * diag.astype(jnp.int32))

    slot = (chip + core) % n
    tail_rows = src_ref.at[pl.ds(rows - tail, tail)]
    tcopies, pcopies = [], []
    for k in range(n):
        dev = (col, core, (chip + k) % n)
        copy = pltpu.make_async_remote_copy(
            src_ref=src_ref, dst_ref=tok_buf.at[chip], send_sem=tsend.at[k],
            recv_sem=trecv.at[chip], device_id=dev, device_id_type=mesh_id,
        )
        if k == 0:
            own = pltpu.make_async_copy(src_ref, tok_buf.at[chip], trecv.at[chip])

            @pl.when(diag)
            def _():
                own.start()

            @pl.when(jnp.logical_not(diag))
            def _():
                copy.start()
        else:
            copy.start()
        tcopies.append(copy)
    for k in range(n):
        pcopy = pltpu.make_async_remote_copy(
            src_ref=tail_rows, dst_ref=prior_buf.at[slot], send_sem=psend.at[k],
            recv_sem=precv.at[slot], device_id=(col, other, (chip + k) % n),
            device_id_type=mesh_id,
        )
        pcopy.start()
        pcopies.append(pcopy)

    waited = set()

    def arrive(offset):
        if offset in waited:
            return
        waited.add(offset)
        blk = lookup(cyc, (r + offset) % n)
        pltpu.make_async_copy(src_ref, tok_buf.at[blk], trecv.at[blk]).wait()
        pltpu.make_async_copy(tail_rows, prior_buf.at[blk], precv.at[blk]).wait()

    own_cols = pl.ds(pl.multiple_of(core * half, half), half)
    other_cols = pl.ds(pl.multiple_of((1 - core) * half, half), half)

    def part(blk, cols):
        def proj_rows(ref):
            return jnp.dot(
                ref[blk, :, own_cols], w_own[:, cols], preferred_element_type=jnp.float32
            ) + jnp.dot(ref[blk, :, other_cols], w_other[:, cols], preferred_element_type=jnp.float32)

        return jnp.concatenate([proj_rows(tok_buf), proj_rows(prior_buf)], axis=0)

    copies = [[] for _ in range(n_ring)]
    for s in range(n - 1):
        arrive((n - 1 - s) % n)
        arrive((1 + s) % n)
        for ring in range(n_ring):
            fwd = ring < n_ring // 2
            d, dest = (1, nxt) if fwd else (-1, prv)
            cols = pl.ds(ring * chunk, chunk)
            q = lookup(cyc, (r - d * (1 + s) + 2 * n) % n)
            if s == 0:
                sbuf[ring, 0] = part(q, cols).astype(sbuf.dtype)
            else:
                mine = part(q, cols)
                copies[ring][s - 1].wait_recv()
                sbuf[ring, s] = (rbuf[ring, s - 1].astype(jnp.float32) + mine).astype(sbuf.dtype)
            copy = pltpu.make_async_remote_copy(
                src_ref=sbuf.at[ring, s],
                dst_ref=rbuf.at[ring, s],
                send_sem=send_sem.at[ring, s],
                recv_sem=recv_sem.at[ring, s],
                device_id=(dest, core, col),
                device_id_type=mesh_id,
            )
            copy.start()
            copies[ring].append(copy)
    arrive(0)
    for ring in range(n_ring):
        cols = pl.ds(ring * chunk, chunk)
        mine = part(chip, cols)
        copies[ring][-1].wait_recv()
        total = (rbuf[ring, n - 2].astype(jnp.float32) + mine).astype(jnp.bfloat16)
        total = total.astype(jnp.float32)
        proj[pl.ds(tail, rows), cols] = total[:rows]
        proj[pl.ds(0, tail), cols] = total[rows:]

    @pl.when(jnp.logical_and(chip == 0, core == 0))
    def _():
        proj[0:tail, :] = jnp.zeros((tail, width), jnp.float32)

    third = width // 3
    mixed = []
    for j in range(3):
        cols = pl.ds(j * third, third)
        mixed.append(
            taps_ref[0, j][None, :] * proj[pl.ds(2, rows), cols]
            + taps_ref[1, j][None, :] * proj[pl.ds(1, rows), cols]
            + taps_ref[2, j][None, :] * proj[pl.ds(0, rows), cols]
        )
    q_ref[...] = mixed[0]
    g_ref[...] = (mixed[1] * mixed[2]).astype(g_ref.dtype)
    for ring in range(n_ring):
        for copy in copies[ring]:
            copy.wait_send()
    for k in range(n):
        if k == 0:
            @pl.when(jnp.logical_not(diag))
            def _():
                tcopies[0].wait_send()
        else:
            tcopies[k].wait_send()
        pcopies[k].wait_send()


def project_and_gate(tokens, w_own, w_other, taps, n_ring=12, tail=2):
    rows, tok_width = tokens.shape
    n = lax.axis_size("p")
    ext_len = rows + tail
    width = w_own.shape[1]
    third = width // 3
    vmem = pl.BlockSpec(memory_space=pltpu.VMEM)
    return pl.pallas_call(
        rs_kernel,
        out_shape=(
            jax.ShapeDtypeStruct((rows, third), jnp.float32),
            jax.ShapeDtypeStruct((rows, third), jnp.bfloat16),
        ),
        in_specs=[vmem] * 4,
        out_specs=(vmem, vmem),
        scratch_shapes=[
            pltpu.VMEM((n, rows, tok_width), tokens.dtype),
            pltpu.VMEM((n, tail, tok_width), tokens.dtype),
            pltpu.VMEM((n_ring, n - 1, ext_len, width // n_ring), jnp.bfloat16),
            pltpu.VMEM((n_ring, n - 1, ext_len, width // n_ring), jnp.bfloat16),
            pltpu.VMEM((ext_len, width), jnp.float32),
        ]
        + [pltpu.SemaphoreType.DMA((n,))] * 4
        + [pltpu.SemaphoreType.DMA((n_ring, n - 1))] * 2,
        compiler_params=pltpu.CompilerParams(
            collective_id=0, has_side_effects=True, vmem_limit_bytes=48 * 1024 * 1024
        ),
    )(tokens, w_own, w_other, taps)


def tok_kernel(src_ref, out_ref, prior_ref, send_sem, recv_sem, psend_sem, precv_sem):
    n, rows, _ = out_ref.shape
    tail = prior_ref.shape[1]
    chip = lax.axis_index("p")
    core = lax.axis_index("c")
    col = lax.axis_index("ch")
    other = 1 - core
    mesh_id = pl.DeviceIdType.MESH
    diag = chip == col
    barrier = pltpu.get_barrier_semaphore()
    for k in range(n):
        dest = (col, core, (chip + k) % n)
        srce = ((chip + k) % n, core, chip)
        if k == 0:
            @pl.when(jnp.logical_not(diag))
            def _():
                pl.semaphore_signal(barrier, 1, device_id=dest, device_id_type=mesh_id)
                pl.semaphore_signal(barrier, 1, device_id=srce, device_id_type=mesh_id)
        else:
            pl.semaphore_signal(barrier, 1, device_id=dest, device_id_type=mesh_id)
            pl.semaphore_signal(barrier, 1, device_id=srce, device_id_type=mesh_id)
        pl.semaphore_signal(
            barrier, 1, device_id=(col, other, (chip + k) % n), device_id_type=mesh_id
        )
        pl.semaphore_signal(
            barrier, 1, device_id=((chip + k) % n, other, chip), device_id_type=mesh_id
        )
    pl.semaphore_wait(barrier, 4 * n - 2 * diag.astype(jnp.int32))
    slot = (chip + core) % n
    copies = []
    for k in range(n):
        copy = pltpu.make_async_remote_copy(
            src_ref=src_ref,
            dst_ref=out_ref.at[chip],
            send_sem=send_sem.at[k],
            recv_sem=recv_sem.at[chip],
            device_id=(col, core, (chip + k) % n),
            device_id_type=mesh_id,
        )
        if k == 0:
            own = pltpu.make_async_copy(src_ref, out_ref.at[chip], recv_sem.at[chip])

            @pl.when(diag)
            def _():
                own.start()

            @pl.when(jnp.logical_not(diag))
            def _():
                copy.start()
        else:
            copy.start()
        copies.append(copy)
    pcopies = []
    for k in range(n):
        pcopy = pltpu.make_async_remote_copy(
            src_ref=src_ref.at[pl.ds(rows - tail, tail)],
            dst_ref=prior_ref.at[slot],
            send_sem=psend_sem.at[k],
            recv_sem=precv_sem.at[slot],
            device_id=(col, other, (chip + k) % n),
            device_id_type=mesh_id,
        )
        pcopy.start()
        pcopies.append(pcopy)
    for j in range(n):
        pltpu.make_async_copy(src_ref, out_ref.at[j], recv_sem.at[j]).wait()
        pltpu.make_async_copy(
            src_ref.at[pl.ds(rows - tail, tail)], prior_ref.at[j], precv_sem.at[j]
        ).wait()
    for k in range(n):
        if k == 0:
            @pl.when(jnp.logical_not(diag))
            def _():
                copies[0].wait_send()
        else:
            copies[k].wait_send()
        pcopies[k].wait_send()


def spread_tokens(tokens, n, tail=2):
    rows, width = tokens.shape
    vmem = pl.BlockSpec(memory_space=pltpu.VMEM)
    return pl.pallas_call(
        tok_kernel,
        out_shape=(
            jax.ShapeDtypeStruct((n, rows, width), tokens.dtype),
            jax.ShapeDtypeStruct((n, tail, width), tokens.dtype),
        ),
        in_specs=[vmem],
        out_specs=(vmem, vmem),
        scratch_shapes=[pltpu.SemaphoreType.DMA((n,))] * 4,
        compiler_params=pltpu.CompilerParams(collective_id=1, has_side_effects=True),
    )(tokens)


def state_kernel(src_ref, lam_ref, out_ref, got, fac, send_sem, recv_sem, block_len):
    n = got.shape[0]
    n_core = lax.axis_size("c")
    me = lax.axis_index("p") * n_core + lax.axis_index("c")
    col = lax.axis_index("ch")
    mesh_id = pl.DeviceIdType.MESH
    barrier = pltpu.get_barrier_semaphore()
    for k in range(1, n):
        other = (me + k) % n
        pl.semaphore_signal(
            barrier, 1, device_id=(other // n_core, other % n_core, col), device_id_type=mesh_id
        )
    for j in range(n):
        @pl.when(j >= me)
        def _():
            got[j] = jnp.zeros(got.shape[1:], got.dtype)

        gap = jnp.maximum(me - 1 - j, 0).astype(jnp.float32)
        fac[j] = jnp.exp(-lam_ref[...] * (block_len * gap))
    pl.semaphore_wait(barrier, n - 1)
    copies = []
    for k in range(1, n):
        other = me + k
        copy = pltpu.make_async_remote_copy(
            src_ref=src_ref,
            dst_ref=got.at[me],
            send_sem=send_sem.at[k],
            recv_sem=recv_sem.at[me],
            device_id=(other // n_core, other % n_core, col),
            device_id_type=mesh_id,
        )

        @pl.when(other < n)
        def _():
            copy.start()

        copies.append((other, copy))
    for j in range(n):
        @pl.when(j < me)
        def _():
            pltpu.make_async_copy(src_ref, got.at[j], recv_sem.at[j]).wait()
    acc = jnp.zeros(out_ref.shape, jnp.float32)
    for j in range(n):
        acc = acc + fac[j] * got[j]
    out_ref[...] = acc
    for other, copy in copies:
        @pl.when(other < n)
        def _():
            copy.wait_send()


def gather_earlier(state, lam, n, block_len):
    vmem = pl.BlockSpec(memory_space=pltpu.VMEM)
    return pl.pallas_call(
        functools.partial(state_kernel, block_len=float(block_len)),
        out_shape=jax.ShapeDtypeStruct(state.shape, state.dtype),
        in_specs=[vmem, vmem],
        out_specs=vmem,
        scratch_shapes=[
            pltpu.VMEM((n,) + state.shape, state.dtype),
            pltpu.VMEM((n,) + state.shape, jnp.float32),
            pltpu.SemaphoreType.DMA((n,)),
            pltpu.SemaphoreType.DMA((n,)),
        ],
        compiler_params=pltpu.CompilerParams(collective_id=2, has_side_effects=True),
    )(state, lam)


def local(tokens, w_in, short_filter, decay_rate, residue, skip):
    n_chip = lax.axis_size("p")
    block_len = tokens.shape[0]
    local_width = w_in.shape[2]
    group_count = local_width // GROUP
    chip = lax.axis_index("p")
    core = lax.axis_index("c")
    col = lax.axis_index("ch")

    n_col = lax.axis_size("ch")
    w_own = w_in.reshape(w_in.shape[0], -1)
    w_other = lax.ppermute(w_own, "c", [(0, 1), (1, 0)])
    query, gated = project_and_gate(tokens, w_own, w_other, short_filter)
    x = gated.reshape(block_len, group_count, GROUP)

    pole_weight = residue * jnp.sqrt(2.0 * decay_rate)
    pos = jnp.arange(block_len, dtype=jnp.float32)
    lam = decay_rate[:, None, :]
    a_mat = pole_weight[:, None, :] * jnp.exp(-lam * pos[None, :, None])
    b_mat = jnp.exp(lam * pos[None, :, None])
    toep = jnp.einsum("gtr,gsr->gts", a_mat, b_mat, precision=lax.Precision.HIGH)
    causal = pos[:, None] >= pos[None, :]
    toep = jnp.where(causal[None], toep, 0.0)
    near = dot_split("gts,sgc->tgc", toep, x)

    e_mat = jnp.exp(-lam * (block_len - 1 - pos)[None, :, None])
    s_loc = dot_split("gsr,sgc->grc", e_mat, x)
    n_ctx = n_chip * lax.axis_size("c")
    me = chip * lax.axis_size("c") + core
    s_flat = s_loc.reshape(group_count, -1)
    lam_b = jnp.broadcast_to(decay_rate[..., None], decay_rate.shape + (GROUP,))
    s_in = gather_earlier(s_flat, lam_b.reshape(group_count, -1), n_ctx, block_len)
    s_in = s_in.reshape(s_loc.shape)
    f_mat = pole_weight[:, None, :] * jnp.exp(-lam * (pos + 1.0)[None, :, None])
    far = jnp.einsum("gtr,grc->tgc", f_mat, s_in, precision=HIGH)
    long_out = (near + far).reshape(block_len, local_width)
    out = query * (long_out + skip * gated.astype(jnp.float32))
    return out.astype(jnp.bfloat16)


def solution(mesh):
    n_ctx, n_ch = mesh.devices.shape
    sub = Mesh(mesh.devices.reshape(n_ctx // 2, 2, n_ch), ("p", "c", "ch"))
    ctx = ("p", "c")
    return jax.shard_map(
        local,
        mesh=sub,
        in_specs=(
            P(ctx, "ch"),
            P(ctx, None, "ch"),
            P(None, None, "ch"),
            P("ch", None),
            P("ch", None),
            P("ch"),
        ),
        out_specs=P(ctx, "ch"),
        check_vma=False,
    )
```

```python
import functools

import jax
import jax.numpy as jnp
from jax import lax
from jax.experimental import pallas as pl
from jax.experimental.pallas import tpu as pltpu
from jax.sharding import Mesh
from jax.sharding import PartitionSpec as P

GROUP = 16
HIGH = lax.Precision.HIGHEST


def split_bf16(x):
    hi = x.astype(jnp.bfloat16)
    lo = (x - hi.astype(jnp.float32)).astype(jnp.bfloat16)
    return hi, lo


def dot_split(spec, weight, data):
    hi, lo = split_bf16(weight)
    return jnp.einsum(spec, hi, data, preferred_element_type=jnp.float32) + jnp.einsum(
        spec, lo, data, preferred_element_type=jnp.float32
    )


CYCLES = (
    (0, 1, 3, 2, 4, 5, 7, 6),
    (0, 1, 3, 5, 7, 6, 4, 2),
    (0, 1, 7, 5, 3, 2, 4, 6),
    (0, 1, 7, 6, 4, 5, 3, 2),
    (0, 2, 3, 1, 7, 5, 4, 6),
    (0, 2, 4, 5, 3, 1, 7, 6),
)


def lookup(table, v):
    n = len(table)
    total = 0
    for k, t in enumerate(table):
        if t:
            total = total + t * (1 - ((v - k + n) % n + n - 1) // n)
    return total


def ring_chip(r, n):
    hi = r // (n // 2)
    return 2 * (r + hi * (n - 1 - 2 * r)) + hi


def ring_pos(p, n):
    z, y = p // 2, p % 2
    return z + y * (n - 1 - 2 * z)


def rs_kernel(
    src_ref, w_hbm, taps_ref, q_ref, g_ref,
    tok_buf, prior_buf, w_own, w_other, sbuf, rbuf, proj,
    tsend, trecv, psend, precv, send_sem, recv_sem, wsem,
):
    n, rows, _ = tok_buf.shape
    tail = prior_buf.shape[1]
    ext_len = rows + tail
    half, width = w_own.shape
    n_ring = sbuf.shape[0]
    chunk = width // n_ring
    chip = lax.axis_index("p")
    core = lax.axis_index("c")
    col = lax.axis_index("ch")
    other = 1 - core
    mesh_id = pl.DeviceIdType.MESH
    diag = chip == col
    cyc = CYCLES[0]
    r = lookup([cyc.index(p) for p in range(n)], chip)
    nxt = lookup(cyc, (r + 1) % n)
    prv = lookup(cyc, (r + n - 1) % n)

    barrier = pltpu.get_barrier_semaphore()
    for k in range(n):
        dest = (col, core, (chip + k) % n)
        srce = ((chip + k) % n, core, chip)
        if k == 0:
            @pl.when(jnp.logical_not(diag))
            def _():
                pl.semaphore_signal(barrier, 1, device_id=dest, device_id_type=mesh_id)
                pl.semaphore_signal(barrier, 1, device_id=srce, device_id_type=mesh_id)
        else:
            pl.semaphore_signal(barrier, 1, device_id=dest, device_id_type=mesh_id)
            pl.semaphore_signal(barrier, 1, device_id=srce, device_id_type=mesh_id)
        pl.semaphore_signal(
            barrier, 1, device_id=(col, other, (chip + k) % n), device_id_type=mesh_id
        )
        pl.semaphore_signal(
            barrier, 1, device_id=((chip + k) % n, other, chip), device_id_type=mesh_id
        )
    for nb in (nxt, prv):
        pl.semaphore_signal(barrier, 1, device_id=(nb, core, col), device_id_type=mesh_id)
    pl.semaphore_signal(barrier, 1, device_id=(chip, other, col), device_id_type=mesh_id)
    w_load = pltpu.make_async_copy(w_hbm, w_own, wsem.at[0])
    w_load.start()
    pl.semaphore_wait(barrier, 4 * n + 3 - 2 * diag.astype(jnp.int32))
    w_swap = pltpu.make_async_remote_copy(
        src_ref=w_hbm, dst_ref=w_other, send_sem=wsem.at[1], recv_sem=wsem.at[2],
        device_id=(chip, other, col), device_id_type=mesh_id,
    )
    w_swap.start()

    slot = (chip + core) % n
    tail_rows = src_ref.at[pl.ds(rows - tail, tail)]
    tcopies, pcopies = [], []
    for k in range(n):
        dev = (col, core, (chip + k) % n)
        copy = pltpu.make_async_remote_copy(
            src_ref=src_ref, dst_ref=tok_buf.at[chip], send_sem=tsend.at[k],
            recv_sem=trecv.at[chip], device_id=dev, device_id_type=mesh_id,
        )
        if k == 0:
            own = pltpu.make_async_copy(src_ref, tok_buf.at[chip], trecv.at[chip])

            @pl.when(diag)
            def _():
                own.start()

            @pl.when(jnp.logical_not(diag))
            def _():
                copy.start()
        else:
            copy.start()
        tcopies.append(copy)
    for k in range(n):
        pcopy = pltpu.make_async_remote_copy(
            src_ref=tail_rows, dst_ref=prior_buf.at[slot], send_sem=psend.at[k],
            recv_sem=precv.at[slot], device_id=(col, other, (chip + k) % n),
            device_id_type=mesh_id,
        )
        pcopy.start()
        pcopies.append(pcopy)

    waited = set()

    def arrive(offset):
        if offset in waited:
            return
        waited.add(offset)
        blk = lookup(cyc, (r + offset) % n)
        pltpu.make_async_copy(src_ref, tok_buf.at[blk], trecv.at[blk]).wait()
        pltpu.make_async_copy(tail_rows, prior_buf.at[blk], precv.at[blk]).wait()

    w_load.wait()
    w_swap.wait_recv()
    own_cols = pl.ds(pl.multiple_of(core * half, half), half)
    other_cols = pl.ds(pl.multiple_of((1 - core) * half, half), half)

    def part(blk, cols):
        def proj_rows(ref):
            return jnp.dot(
                ref[blk, :, own_cols], w_own[:, cols], preferred_element_type=jnp.float32
            ) + jnp.dot(ref[blk, :, other_cols], w_other[:, cols], preferred_element_type=jnp.float32)

        return jnp.concatenate([proj_rows(tok_buf), proj_rows(prior_buf)], axis=0)

    copies = [[] for _ in range(n_ring)]
    for s in range(n - 1):
        arrive((n - 1 - s) % n)
        arrive((1 + s) % n)
        for ring in range(n_ring):
            fwd = ring < n_ring // 2
            d, dest = (1, nxt) if fwd else (-1, prv)
            cols = pl.ds(ring * chunk, chunk)
            q = lookup(cyc, (r - d * (1 + s) + 2 * n) % n)
            if s == 0:
                sbuf[ring, 0] = part(q, cols).astype(sbuf.dtype)
            else:
                mine = part(q, cols)
                copies[ring][s - 1].wait_recv()
                sbuf[ring, s] = (rbuf[ring, s - 1].astype(jnp.float32) + mine).astype(sbuf.dtype)
            copy = pltpu.make_async_remote_copy(
                src_ref=sbuf.at[ring, s],
                dst_ref=rbuf.at[ring, s],
                send_sem=send_sem.at[ring, s],
                recv_sem=recv_sem.at[ring, s],
                device_id=(dest, core, col),
                device_id_type=mesh_id,
            )
            copy.start()
            copies[ring].append(copy)
    arrive(0)
    for ring in range(n_ring):
        cols = pl.ds(ring * chunk, chunk)
        mine = part(chip, cols)
        copies[ring][-1].wait_recv()
        total = (rbuf[ring, n - 2].astype(jnp.float32) + mine).astype(jnp.bfloat16)
        total = total.astype(jnp.float32)
        proj[pl.ds(tail, rows), cols] = total[:rows]
        proj[pl.ds(0, tail), cols] = total[rows:]

    @pl.when(jnp.logical_and(chip == 0, core == 0))
    def _():
        proj[0:tail, :] = jnp.zeros((tail, width), jnp.float32)

    third = width // 3
    mixed = []
    for j in range(3):
        cols = pl.ds(j * third, third)
        mixed.append(
            taps_ref[0, j][None, :] * proj[pl.ds(2, rows), cols]
            + taps_ref[1, j][None, :] * proj[pl.ds(1, rows), cols]
            + taps_ref[2, j][None, :] * proj[pl.ds(0, rows), cols]
        )
    q_ref[...] = mixed[0]
    g_ref[...] = (mixed[1] * mixed[2]).astype(g_ref.dtype)
    for ring in range(n_ring):
        for copy in copies[ring]:
            copy.wait_send()
    for k in range(n):
        if k == 0:
            @pl.when(jnp.logical_not(diag))
            def _():
                tcopies[0].wait_send()
        else:
            tcopies[k].wait_send()
        pcopies[k].wait_send()
    w_swap.wait_send()


def project_and_gate(tokens, w_own, taps, n_ring=12, tail=2):
    rows, tok_width = tokens.shape
    n = lax.axis_size("p")
    ext_len = rows + tail
    width = w_own.shape[1]
    third = width // 3
    vmem = pl.BlockSpec(memory_space=pltpu.VMEM)
    return pl.pallas_call(
        rs_kernel,
        out_shape=(
            jax.ShapeDtypeStruct((rows, third), jnp.float32),
            jax.ShapeDtypeStruct((rows, third), jnp.bfloat16),
        ),
        in_specs=[vmem, pl.BlockSpec(memory_space=pl.ANY), vmem],
        out_specs=(vmem, vmem),
        scratch_shapes=[
            pltpu.VMEM((n, rows, tok_width), tokens.dtype),
            pltpu.VMEM((n, tail, tok_width), tokens.dtype),
            pltpu.VMEM(w_own.shape, w_own.dtype),
            pltpu.VMEM(w_own.shape, w_own.dtype),
            pltpu.VMEM((n_ring, n - 1, ext_len, width // n_ring), jnp.bfloat16),
            pltpu.VMEM((n_ring, n - 1, ext_len, width // n_ring), jnp.bfloat16),
            pltpu.VMEM((ext_len, width), jnp.float32),
        ]
        + [pltpu.SemaphoreType.DMA((n,))] * 4
        + [pltpu.SemaphoreType.DMA((n_ring, n - 1))] * 2
        + [pltpu.SemaphoreType.DMA((3,))],
        compiler_params=pltpu.CompilerParams(
            collective_id=0, has_side_effects=True, vmem_limit_bytes=48 * 1024 * 1024
        ),
    )(tokens, w_own, taps)


def tok_kernel(src_ref, out_ref, prior_ref, send_sem, recv_sem, psend_sem, precv_sem):
    n, rows, _ = out_ref.shape
    tail = prior_ref.shape[1]
    chip = lax.axis_index("p")
    core = lax.axis_index("c")
    col = lax.axis_index("ch")
    other = 1 - core
    mesh_id = pl.DeviceIdType.MESH
    diag = chip == col
    barrier = pltpu.get_barrier_semaphore()
    for k in range(n):
        dest = (col, core, (chip + k) % n)
        srce = ((chip + k) % n, core, chip)
        if k == 0:
            @pl.when(jnp.logical_not(diag))
            def _():
                pl.semaphore_signal(barrier, 1, device_id=dest, device_id_type=mesh_id)
                pl.semaphore_signal(barrier, 1, device_id=srce, device_id_type=mesh_id)
        else:
            pl.semaphore_signal(barrier, 1, device_id=dest, device_id_type=mesh_id)
            pl.semaphore_signal(barrier, 1, device_id=srce, device_id_type=mesh_id)
        pl.semaphore_signal(
            barrier, 1, device_id=(col, other, (chip + k) % n), device_id_type=mesh_id
        )
        pl.semaphore_signal(
            barrier, 1, device_id=((chip + k) % n, other, chip), device_id_type=mesh_id
        )
    pl.semaphore_wait(barrier, 4 * n - 2 * diag.astype(jnp.int32))
    slot = (chip + core) % n
    copies = []
    for k in range(n):
        copy = pltpu.make_async_remote_copy(
            src_ref=src_ref,
            dst_ref=out_ref.at[chip],
            send_sem=send_sem.at[k],
            recv_sem=recv_sem.at[chip],
            device_id=(col, core, (chip + k) % n),
            device_id_type=mesh_id,
        )
        if k == 0:
            own = pltpu.make_async_copy(src_ref, out_ref.at[chip], recv_sem.at[chip])

            @pl.when(diag)
            def _():
                own.start()

            @pl.when(jnp.logical_not(diag))
            def _():
                copy.start()
        else:
            copy.start()
        copies.append(copy)
    pcopies = []
    for k in range(n):
        pcopy = pltpu.make_async_remote_copy(
            src_ref=src_ref.at[pl.ds(rows - tail, tail)],
            dst_ref=prior_ref.at[slot],
            send_sem=psend_sem.at[k],
            recv_sem=precv_sem.at[slot],
            device_id=(col, other, (chip + k) % n),
            device_id_type=mesh_id,
        )
        pcopy.start()
        pcopies.append(pcopy)
    for j in range(n):
        pltpu.make_async_copy(src_ref, out_ref.at[j], recv_sem.at[j]).wait()
        pltpu.make_async_copy(
            src_ref.at[pl.ds(rows - tail, tail)], prior_ref.at[j], precv_sem.at[j]
        ).wait()
    for k in range(n):
        if k == 0:
            @pl.when(jnp.logical_not(diag))
            def _():
                copies[0].wait_send()
        else:
            copies[k].wait_send()
        pcopies[k].wait_send()


def spread_tokens(tokens, n, tail=2):
    rows, width = tokens.shape
    vmem = pl.BlockSpec(memory_space=pltpu.VMEM)
    return pl.pallas_call(
        tok_kernel,
        out_shape=(
            jax.ShapeDtypeStruct((n, rows, width), tokens.dtype),
            jax.ShapeDtypeStruct((n, tail, width), tokens.dtype),
        ),
        in_specs=[vmem],
        out_specs=(vmem, vmem),
        scratch_shapes=[pltpu.SemaphoreType.DMA((n,))] * 4,
        compiler_params=pltpu.CompilerParams(collective_id=1, has_side_effects=True),
    )(tokens)


def state_kernel(src_ref, lam_ref, out_ref, got, fac, send_sem, recv_sem, block_len):
    n = got.shape[0]
    n_core = lax.axis_size("c")
    me = lax.axis_index("p") * n_core + lax.axis_index("c")
    col = lax.axis_index("ch")
    mesh_id = pl.DeviceIdType.MESH
    barrier = pltpu.get_barrier_semaphore()
    for k in range(1, n):
        other = (me + k) % n
        pl.semaphore_signal(
            barrier, 1, device_id=(other // n_core, other % n_core, col), device_id_type=mesh_id
        )
    for j in range(n):
        @pl.when(j >= me)
        def _():
            got[j] = jnp.zeros(got.shape[1:], got.dtype)

        gap = jnp.maximum(me - 1 - j, 0).astype(jnp.float32)
        fac[j] = jnp.exp(-lam_ref[...] * (block_len * gap))
    pl.semaphore_wait(barrier, n - 1)
    copies = []
    for k in range(1, n):
        other = me + k
        copy = pltpu.make_async_remote_copy(
            src_ref=src_ref,
            dst_ref=got.at[me],
            send_sem=send_sem.at[k],
            recv_sem=recv_sem.at[me],
            device_id=(other // n_core, other % n_core, col),
            device_id_type=mesh_id,
        )

        @pl.when(other < n)
        def _():
            copy.start()

        copies.append((other, copy))
    for j in range(n):
        @pl.when(j < me)
        def _():
            pltpu.make_async_copy(src_ref, got.at[j], recv_sem.at[j]).wait()
    acc = jnp.zeros(out_ref.shape, jnp.float32)
    for j in range(n):
        acc = acc + fac[j] * got[j]
    out_ref[...] = acc
    for other, copy in copies:
        @pl.when(other < n)
        def _():
            copy.wait_send()


def gather_earlier(state, lam, n, block_len):
    vmem = pl.BlockSpec(memory_space=pltpu.VMEM)
    return pl.pallas_call(
        functools.partial(state_kernel, block_len=float(block_len)),
        out_shape=jax.ShapeDtypeStruct(state.shape, state.dtype),
        in_specs=[vmem, vmem],
        out_specs=vmem,
        scratch_shapes=[
            pltpu.VMEM((n,) + state.shape, state.dtype),
            pltpu.VMEM((n,) + state.shape, jnp.float32),
            pltpu.SemaphoreType.DMA((n,)),
            pltpu.SemaphoreType.DMA((n,)),
        ],
        compiler_params=pltpu.CompilerParams(collective_id=2, has_side_effects=True),
    )(state, lam)


def local(tokens, w_in, short_filter, decay_rate, residue, skip):
    n_chip = lax.axis_size("p")
    block_len = tokens.shape[0]
    local_width = w_in.shape[2]
    group_count = local_width // GROUP
    chip = lax.axis_index("p")
    core = lax.axis_index("c")
    col = lax.axis_index("ch")

    n_col = lax.axis_size("ch")
    w_own = w_in.reshape(w_in.shape[0], -1)
    query, gated = project_and_gate(tokens, w_own, short_filter)
    x = gated.reshape(block_len, group_count, GROUP)

    pole_weight = residue * jnp.sqrt(2.0 * decay_rate)
    pos = jnp.arange(block_len, dtype=jnp.float32)
    lam = decay_rate[:, None, :]
    a_mat = pole_weight[:, None, :] * jnp.exp(-lam * pos[None, :, None])
    b_mat = jnp.exp(lam * pos[None, :, None])
    toep = jnp.einsum("gtr,gsr->gts", a_mat, b_mat, precision=lax.Precision.HIGH)
    causal = pos[:, None] >= pos[None, :]
    toep = jnp.where(causal[None], toep, 0.0)
    near = dot_split("gts,sgc->tgc", toep, x)

    e_mat = jnp.exp(-lam * (block_len - 1 - pos)[None, :, None])
    s_loc = dot_split("gsr,sgc->grc", e_mat, x)
    n_ctx = n_chip * lax.axis_size("c")
    me = chip * lax.axis_size("c") + core
    s_flat = s_loc.reshape(group_count, -1)
    lam_b = jnp.broadcast_to(decay_rate[..., None], decay_rate.shape + (GROUP,))
    s_in = gather_earlier(s_flat, lam_b.reshape(group_count, -1), n_ctx, block_len)
    s_in = s_in.reshape(s_loc.shape)
    f_mat = pole_weight[:, None, :] * jnp.exp(-lam * (pos + 1.0)[None, :, None])
    far = jnp.einsum("gtr,grc->tgc", f_mat, s_in, precision=HIGH)
    long_out = (near + far).reshape(block_len, local_width)
    out = query * (long_out + skip * gated.astype(jnp.float32))
    return out.astype(jnp.bfloat16)


def solution(mesh):
    n_ctx, n_ch = mesh.devices.shape
    sub = Mesh(mesh.devices.reshape(n_ctx // 2, 2, n_ch), ("p", "c", "ch"))
    ctx = ("p", "c")
    return jax.shard_map(
        local,
        mesh=sub,
        in_specs=(
            P(ctx, "ch"),
            P(ctx, None, "ch"),
            P(None, None, "ch"),
            P("ch", None),
            P("ch", None),
            P("ch"),
        ),
        out_specs=P(ctx, "ch"),
        check_vma=False,
    )
```

```python
import functools

import jax
import jax.numpy as jnp
from jax import lax
from jax.experimental import pallas as pl
from jax.experimental.pallas import tpu as pltpu
from jax.sharding import Mesh
from jax.sharding import PartitionSpec as P

GROUP = 16
HIGH = lax.Precision.HIGHEST


def split_bf16(x):
    hi = x.astype(jnp.bfloat16)
    lo = (x - hi.astype(jnp.float32)).astype(jnp.bfloat16)
    return hi, lo


def dot_split(spec, weight, data):
    hi, lo = split_bf16(weight)
    return jnp.einsum(spec, hi, data, preferred_element_type=jnp.float32) + jnp.einsum(
        spec, lo, data, preferred_element_type=jnp.float32
    )


CYCLES = (
    (0, 1, 3, 2, 4, 5, 7, 6),
    (0, 1, 3, 5, 7, 6, 4, 2),
    (0, 1, 7, 5, 3, 2, 4, 6),
    (0, 1, 7, 6, 4, 5, 3, 2),
    (0, 2, 3, 1, 7, 5, 4, 6),
    (0, 2, 4, 5, 3, 1, 7, 6),
)


def lookup(table, v):
    n = len(table)
    total = 0
    for k, t in enumerate(table):
        if t:
            total = total + t * (1 - ((v - k + n) % n + n - 1) // n)
    return total


def ring_chip(r, n):
    hi = r // (n // 2)
    return 2 * (r + hi * (n - 1 - 2 * r)) + hi


def ring_pos(p, n):
    z, y = p // 2, p % 2
    return z + y * (n - 1 - 2 * z)


def rs_kernel(
    src_ref, w_hbm, taps_ref, q_ref, g_ref,
    tok_buf, prior_buf, w_own, w_other, sbuf, rbuf, proj,
    tsend, trecv, psend, precv, send_sem, recv_sem, wsem,
):
    n, rows, _ = tok_buf.shape
    tail = prior_buf.shape[1]
    ext_len = rows + tail
    half, width = w_own.shape
    n_ring = sbuf.shape[0]
    chunk = width // n_ring
    chip = lax.axis_index("p")
    core = lax.axis_index("c")
    col = lax.axis_index("ch")
    other = 1 - core
    mesh_id = pl.DeviceIdType.MESH
    diag = chip == col
    cyc = CYCLES[0]
    r = lookup([cyc.index(p) for p in range(n)], chip)
    nxt = lookup(cyc, (r + 1) % n)
    prv = lookup(cyc, (r + n - 1) % n)

    barrier = pltpu.get_barrier_semaphore()
    for k in range(n):
        dest = (col, core, (chip + k) % n)
        srce = ((chip + k) % n, core, chip)
        if k == 0:
            @pl.when(jnp.logical_not(diag))
            def _():
                pl.semaphore_signal(barrier, 1, device_id=dest, device_id_type=mesh_id)
                pl.semaphore_signal(barrier, 1, device_id=srce, device_id_type=mesh_id)
        else:
            pl.semaphore_signal(barrier, 1, device_id=dest, device_id_type=mesh_id)
            pl.semaphore_signal(barrier, 1, device_id=srce, device_id_type=mesh_id)
        pl.semaphore_signal(
            barrier, 1, device_id=(col, other, (chip + k) % n), device_id_type=mesh_id
        )
        pl.semaphore_signal(
            barrier, 1, device_id=((chip + k) % n, other, chip), device_id_type=mesh_id
        )
    for nb in (nxt, prv):
        pl.semaphore_signal(barrier, 1, device_id=(nb, core, col), device_id_type=mesh_id)
    pl.semaphore_signal(barrier, 1, device_id=(chip, other, col), device_id_type=mesh_id)
    n_part, part_width = w_hbm.shape[0], w_hbm.shape[2]
    w_loads, w_swaps = [], []
    for j in range(n_part):
        w_cols = pl.ds(j * part_width, part_width)
        w_loads.append(pltpu.make_async_copy(w_hbm.at[j], w_own.at[:, w_cols], wsem.at[0, j]))
        w_loads[-1].start()
    pl.semaphore_wait(barrier, 4 * n + 3 - 2 * diag.astype(jnp.int32))
    for j in range(n_part):
        w_cols = pl.ds(j * part_width, part_width)
        w_swaps.append(
            pltpu.make_async_remote_copy(
                src_ref=w_hbm.at[j], dst_ref=w_other.at[:, w_cols], send_sem=wsem.at[1, j],
                recv_sem=wsem.at[2, j], device_id=(chip, other, col), device_id_type=mesh_id,
            )
        )
        w_swaps[-1].start()

    slot = (chip + core) % n
    tail_rows = src_ref.at[pl.ds(rows - tail, tail)]
    tcopies, pcopies = [], []
    for k in range(n):
        dev = (col, core, (chip + k) % n)
        copy = pltpu.make_async_remote_copy(
            src_ref=src_ref, dst_ref=tok_buf.at[chip], send_sem=tsend.at[k],
            recv_sem=trecv.at[chip], device_id=dev, device_id_type=mesh_id,
        )
        if k == 0:
            own = pltpu.make_async_copy(src_ref, tok_buf.at[chip], trecv.at[chip])

            @pl.when(diag)
            def _():
                own.start()

            @pl.when(jnp.logical_not(diag))
            def _():
                copy.start()
        else:
            copy.start()
        tcopies.append(copy)
    for k in range(n):
        pcopy = pltpu.make_async_remote_copy(
            src_ref=tail_rows, dst_ref=prior_buf.at[slot], send_sem=psend.at[k],
            recv_sem=precv.at[slot], device_id=(col, other, (chip + k) % n),
            device_id_type=mesh_id,
        )
        pcopy.start()
        pcopies.append(pcopy)

    waited = set()

    def arrive(offset):
        if offset in waited:
            return
        waited.add(offset)
        blk = lookup(cyc, (r + offset) % n)
        pltpu.make_async_copy(src_ref, tok_buf.at[blk], trecv.at[blk]).wait()
        pltpu.make_async_copy(tail_rows, prior_buf.at[blk], precv.at[blk]).wait()

    for j in range(n_part):
        w_loads[j].wait()
        w_swaps[j].wait_recv()
    own_cols = pl.ds(pl.multiple_of(core * half, half), half)
    other_cols = pl.ds(pl.multiple_of((1 - core) * half, half), half)

    def part(blk, cols):
        def proj_rows(ref):
            return jnp.dot(
                ref[blk, :, own_cols], w_own[:, cols], preferred_element_type=jnp.float32
            ) + jnp.dot(ref[blk, :, other_cols], w_other[:, cols], preferred_element_type=jnp.float32)

        return jnp.concatenate([proj_rows(tok_buf), proj_rows(prior_buf)], axis=0)

    copies = [[] for _ in range(n_ring)]
    for s in range(n - 1):
        arrive((n - 1 - s) % n)
        arrive((1 + s) % n)
        for ring in range(n_ring):
            fwd = ring < n_ring // 2
            d, dest = (1, nxt) if fwd else (-1, prv)
            cols = pl.ds(ring * chunk, chunk)
            q = lookup(cyc, (r - d * (1 + s) + 2 * n) % n)
            if s == 0:
                sbuf[ring, 0] = part(q, cols).astype(sbuf.dtype)
            else:
                mine = part(q, cols)
                copies[ring][s - 1].wait_recv()
                sbuf[ring, s] = (rbuf[ring, s - 1].astype(jnp.float32) + mine).astype(sbuf.dtype)
            copy = pltpu.make_async_remote_copy(
                src_ref=sbuf.at[ring, s],
                dst_ref=rbuf.at[ring, s],
                send_sem=send_sem.at[ring, s],
                recv_sem=recv_sem.at[ring, s],
                device_id=(dest, core, col),
                device_id_type=mesh_id,
            )
            copy.start()
            copies[ring].append(copy)
    arrive(0)
    for ring in range(n_ring):
        cols = pl.ds(ring * chunk, chunk)
        mine = part(chip, cols)
        copies[ring][-1].wait_recv()
        total = (rbuf[ring, n - 2].astype(jnp.float32) + mine).astype(jnp.bfloat16)
        total = total.astype(jnp.float32)
        proj[pl.ds(tail, rows), cols] = total[:rows]
        proj[pl.ds(0, tail), cols] = total[rows:]

    @pl.when(jnp.logical_and(chip == 0, core == 0))
    def _():
        proj[0:tail, :] = jnp.zeros((tail, width), jnp.float32)

    third = width // 3
    mixed = []
    for j in range(3):
        cols = pl.ds(j * third, third)
        mixed.append(
            taps_ref[0, j][None, :] * proj[pl.ds(2, rows), cols]
            + taps_ref[1, j][None, :] * proj[pl.ds(1, rows), cols]
            + taps_ref[2, j][None, :] * proj[pl.ds(0, rows), cols]
        )
    q_ref[...] = mixed[0]
    g_ref[...] = (mixed[1] * mixed[2]).astype(g_ref.dtype)
    for ring in range(n_ring):
        for copy in copies[ring]:
            copy.wait_send()
    for k in range(n):
        if k == 0:
            @pl.when(jnp.logical_not(diag))
            def _():
                tcopies[0].wait_send()
        else:
            tcopies[k].wait_send()
        pcopies[k].wait_send()
    for j in range(n_part):
        w_swaps[j].wait_send()


def project_and_gate(tokens, w_own, taps, n_ring=12, tail=2):
    rows, tok_width = tokens.shape
    n = lax.axis_size("p")
    ext_len = rows + tail
    n_part, half, part_width = w_own.shape
    width = n_part * part_width
    third = width // 3
    vmem = pl.BlockSpec(memory_space=pltpu.VMEM)
    return pl.pallas_call(
        rs_kernel,
        out_shape=(
            jax.ShapeDtypeStruct((rows, third), jnp.float32),
            jax.ShapeDtypeStruct((rows, third), jnp.bfloat16),
        ),
        in_specs=[vmem, pl.BlockSpec(memory_space=pl.ANY), vmem],
        out_specs=(vmem, vmem),
        scratch_shapes=[
            pltpu.VMEM((n, rows, tok_width), tokens.dtype),
            pltpu.VMEM((n, tail, tok_width), tokens.dtype),
            pltpu.VMEM((half, width), w_own.dtype),
            pltpu.VMEM((half, width), w_own.dtype),
            pltpu.VMEM((n_ring, n - 1, ext_len, width // n_ring), jnp.bfloat16),
            pltpu.VMEM((n_ring, n - 1, ext_len, width // n_ring), jnp.bfloat16),
            pltpu.VMEM((ext_len, width), jnp.float32),
        ]
        + [pltpu.SemaphoreType.DMA((n,))] * 4
        + [pltpu.SemaphoreType.DMA((n_ring, n - 1))] * 2
        + [pltpu.SemaphoreType.DMA((3, n_part))],
        compiler_params=pltpu.CompilerParams(
            collective_id=0, has_side_effects=True, vmem_limit_bytes=48 * 1024 * 1024
        ),
    )(tokens, w_own, taps)


def tok_kernel(src_ref, out_ref, prior_ref, send_sem, recv_sem, psend_sem, precv_sem):
    n, rows, _ = out_ref.shape
    tail = prior_ref.shape[1]
    chip = lax.axis_index("p")
    core = lax.axis_index("c")
    col = lax.axis_index("ch")
    other = 1 - core
    mesh_id = pl.DeviceIdType.MESH
    diag = chip == col
    barrier = pltpu.get_barrier_semaphore()
    for k in range(n):
        dest = (col, core, (chip + k) % n)
        srce = ((chip + k) % n, core, chip)
        if k == 0:
            @pl.when(jnp.logical_not(diag))
            def _():
                pl.semaphore_signal(barrier, 1, device_id=dest, device_id_type=mesh_id)
                pl.semaphore_signal(barrier, 1, device_id=srce, device_id_type=mesh_id)
        else:
            pl.semaphore_signal(barrier, 1, device_id=dest, device_id_type=mesh_id)
            pl.semaphore_signal(barrier, 1, device_id=srce, device_id_type=mesh_id)
        pl.semaphore_signal(
            barrier, 1, device_id=(col, other, (chip + k) % n), device_id_type=mesh_id
        )
        pl.semaphore_signal(
            barrier, 1, device_id=((chip + k) % n, other, chip), device_id_type=mesh_id
        )
    pl.semaphore_wait(barrier, 4 * n - 2 * diag.astype(jnp.int32))
    slot = (chip + core) % n
    copies = []
    for k in range(n):
        copy = pltpu.make_async_remote_copy(
            src_ref=src_ref,
            dst_ref=out_ref.at[chip],
            send_sem=send_sem.at[k],
            recv_sem=recv_sem.at[chip],
            device_id=(col, core, (chip + k) % n),
            device_id_type=mesh_id,
        )
        if k == 0:
            own = pltpu.make_async_copy(src_ref, out_ref.at[chip], recv_sem.at[chip])

            @pl.when(diag)
            def _():
                own.start()

            @pl.when(jnp.logical_not(diag))
            def _():
                copy.start()
        else:
            copy.start()
        copies.append(copy)
    pcopies = []
    for k in range(n):
        pcopy = pltpu.make_async_remote_copy(
            src_ref=src_ref.at[pl.ds(rows - tail, tail)],
            dst_ref=prior_ref.at[slot],
            send_sem=psend_sem.at[k],
            recv_sem=precv_sem.at[slot],
            device_id=(col, other, (chip + k) % n),
            device_id_type=mesh_id,
        )
        pcopy.start()
        pcopies.append(pcopy)
    for j in range(n):
        pltpu.make_async_copy(src_ref, out_ref.at[j], recv_sem.at[j]).wait()
        pltpu.make_async_copy(
            src_ref.at[pl.ds(rows - tail, tail)], prior_ref.at[j], precv_sem.at[j]
        ).wait()
    for k in range(n):
        if k == 0:
            @pl.when(jnp.logical_not(diag))
            def _():
                copies[0].wait_send()
        else:
            copies[k].wait_send()
        pcopies[k].wait_send()


def spread_tokens(tokens, n, tail=2):
    rows, width = tokens.shape
    vmem = pl.BlockSpec(memory_space=pltpu.VMEM)
    return pl.pallas_call(
        tok_kernel,
        out_shape=(
            jax.ShapeDtypeStruct((n, rows, width), tokens.dtype),
            jax.ShapeDtypeStruct((n, tail, width), tokens.dtype),
        ),
        in_specs=[vmem],
        out_specs=(vmem, vmem),
        scratch_shapes=[pltpu.SemaphoreType.DMA((n,))] * 4,
        compiler_params=pltpu.CompilerParams(collective_id=1, has_side_effects=True),
    )(tokens)


def state_kernel(src_ref, lam_ref, out_ref, got, fac, send_sem, recv_sem, block_len):
    n = got.shape[0]
    n_core = lax.axis_size("c")
    me = lax.axis_index("p") * n_core + lax.axis_index("c")
    col = lax.axis_index("ch")
    mesh_id = pl.DeviceIdType.MESH
    barrier = pltpu.get_barrier_semaphore()
    for k in range(1, n):
        other = (me + k) % n
        pl.semaphore_signal(
            barrier, 1, device_id=(other // n_core, other % n_core, col), device_id_type=mesh_id
        )
    for j in range(n):
        @pl.when(j >= me)
        def _():
            got[j] = jnp.zeros(got.shape[1:], got.dtype)

        gap = jnp.maximum(me - 1 - j, 0).astype(jnp.float32)
        fac[j] = jnp.exp(-lam_ref[...] * (block_len * gap))
    pl.semaphore_wait(barrier, n - 1)
    copies = []
    for k in range(1, n):
        other = me + k
        copy = pltpu.make_async_remote_copy(
            src_ref=src_ref,
            dst_ref=got.at[me],
            send_sem=send_sem.at[k],
            recv_sem=recv_sem.at[me],
            device_id=(other // n_core, other % n_core, col),
            device_id_type=mesh_id,
        )

        @pl.when(other < n)
        def _():
            copy.start()

        copies.append((other, copy))
    for j in range(n):
        @pl.when(j < me)
        def _():
            pltpu.make_async_copy(src_ref, got.at[j], recv_sem.at[j]).wait()
    acc = jnp.zeros(out_ref.shape, jnp.float32)
    for j in range(n):
        acc = acc + fac[j] * got[j]
    out_ref[...] = acc
    for other, copy in copies:
        @pl.when(other < n)
        def _():
            copy.wait_send()


def gather_earlier(state, lam, n, block_len):
    vmem = pl.BlockSpec(memory_space=pltpu.VMEM)
    return pl.pallas_call(
        functools.partial(state_kernel, block_len=float(block_len)),
        out_shape=jax.ShapeDtypeStruct(state.shape, state.dtype),
        in_specs=[vmem, vmem],
        out_specs=vmem,
        scratch_shapes=[
            pltpu.VMEM((n,) + state.shape, state.dtype),
            pltpu.VMEM((n,) + state.shape, jnp.float32),
            pltpu.SemaphoreType.DMA((n,)),
            pltpu.SemaphoreType.DMA((n,)),
        ],
        compiler_params=pltpu.CompilerParams(collective_id=2, has_side_effects=True),
    )(state, lam)


def local(tokens, w_in, short_filter, decay_rate, residue, skip):
    n_chip = lax.axis_size("p")
    block_len = tokens.shape[0]
    local_width = w_in.shape[2]
    group_count = local_width // GROUP
    chip = lax.axis_index("p")
    core = lax.axis_index("c")
    col = lax.axis_index("ch")

    n_col = lax.axis_size("ch")
    w_parts = jnp.transpose(w_in, (1, 0, 2))
    query, gated = project_and_gate(tokens, w_parts, short_filter)
    x = gated.reshape(block_len, group_count, GROUP)

    pole_weight = residue * jnp.sqrt(2.0 * decay_rate)
    pos = jnp.arange(block_len, dtype=jnp.float32)
    lam = decay_rate[:, None, :]
    a_mat = pole_weight[:, None, :] * jnp.exp(-lam * pos[None, :, None])
    b_mat = jnp.exp(lam * pos[None, :, None])
    toep = jnp.einsum("gtr,gsr->gts", a_mat, b_mat, precision=lax.Precision.HIGH)
    causal = pos[:, None] >= pos[None, :]
    toep = jnp.where(causal[None], toep, 0.0)
    near = dot_split("gts,sgc->tgc", toep, x)

    e_mat = jnp.exp(-lam * (block_len - 1 - pos)[None, :, None])
    s_loc = dot_split("gsr,sgc->grc", e_mat, x)
    n_ctx = n_chip * lax.axis_size("c")
    me = chip * lax.axis_size("c") + core
    s_flat = s_loc.reshape(group_count, -1)
    lam_b = jnp.broadcast_to(decay_rate[..., None], decay_rate.shape + (GROUP,))
    s_in = gather_earlier(s_flat, lam_b.reshape(group_count, -1), n_ctx, block_len)
    s_in = s_in.reshape(s_loc.shape)
    f_mat = pole_weight[:, None, :] * jnp.exp(-lam * (pos + 1.0)[None, :, None])
    far = jnp.einsum("gtr,grc->tgc", f_mat, s_in, precision=HIGH)
    long_out = (near + far).reshape(block_len, local_width)
    out = query * (long_out + skip * gated.astype(jnp.float32))
    return out.astype(jnp.bfloat16)


def solution(mesh):
    n_ctx, n_ch = mesh.devices.shape
    sub = Mesh(mesh.devices.reshape(n_ctx // 2, 2, n_ch), ("p", "c", "ch"))
    ctx = ("p", "c")
    return jax.shard_map(
        local,
        mesh=sub,
        in_specs=(
            P(ctx, "ch"),
            P(ctx, None, "ch"),
            P(None, None, "ch"),
            P("ch", None),
            P("ch", None),
            P("ch"),
        ),
        out_specs=P(ctx, "ch"),
        check_vma=False,
    )
```

```python
import functools

import jax
import jax.numpy as jnp
from jax import lax
from jax.experimental import pallas as pl
from jax.experimental.pallas import tpu as pltpu
from jax.sharding import Mesh
from jax.sharding import PartitionSpec as P

GROUP = 16
HIGH = lax.Precision.HIGHEST


def split_bf16(x):
    hi = x.astype(jnp.bfloat16)
    lo = (x - hi.astype(jnp.float32)).astype(jnp.bfloat16)
    return hi, lo


def dot_split(spec, weight, data):
    hi, lo = split_bf16(weight)
    return jnp.einsum(spec, hi, data, preferred_element_type=jnp.float32) + jnp.einsum(
        spec, lo, data, preferred_element_type=jnp.float32
    )


CYCLES = (
    (0, 1, 3, 2, 4, 5, 7, 6),
    (0, 1, 3, 5, 7, 6, 4, 2),
    (0, 1, 7, 5, 3, 2, 4, 6),
    (0, 1, 7, 6, 4, 5, 3, 2),
    (0, 2, 3, 1, 7, 5, 4, 6),
    (0, 2, 4, 5, 3, 1, 7, 6),
)


def lookup(table, v):
    n = len(table)
    total = 0
    for k, t in enumerate(table):
        if t:
            total = total + t * (1 - ((v - k + n) % n + n - 1) // n)
    return total


def ring_chip(r, n):
    hi = r // (n // 2)
    return 2 * (r + hi * (n - 1 - 2 * r)) + hi


def ring_pos(p, n):
    z, y = p // 2, p % 2
    return z + y * (n - 1 - 2 * z)


def rs_kernel(
    src_ref, w_hbm, taps_ref, q_ref, g_ref,
    tok_buf, prior_buf, w_own, w_other, sbuf, rbuf, proj,
    tsend, trecv, psend, precv, send_sem, recv_sem, wsem,
):
    n, rows, _ = tok_buf.shape
    tail = prior_buf.shape[1]
    ext_len = rows + tail
    half, width = w_own.shape
    n_ring = sbuf.shape[0]
    chunk = width // n_ring
    chip = lax.axis_index("p")
    core = lax.axis_index("c")
    col = lax.axis_index("ch")
    other = 1 - core
    mesh_id = pl.DeviceIdType.MESH
    diag = chip == col
    cyc = CYCLES[0]
    r = lookup([cyc.index(p) for p in range(n)], chip)
    nxt = lookup(cyc, (r + 1) % n)
    prv = lookup(cyc, (r + n - 1) % n)

    barrier = pltpu.get_barrier_semaphore()
    for k in range(n):
        dest = (col, core, (chip + k) % n)
        srce = ((chip + k) % n, core, chip)
        if k == 0:
            @pl.when(jnp.logical_not(diag))
            def _():
                pl.semaphore_signal(barrier, 1, device_id=dest, device_id_type=mesh_id)
                pl.semaphore_signal(barrier, 1, device_id=srce, device_id_type=mesh_id)
        else:
            pl.semaphore_signal(barrier, 1, device_id=dest, device_id_type=mesh_id)
            pl.semaphore_signal(barrier, 1, device_id=srce, device_id_type=mesh_id)
        pl.semaphore_signal(
            barrier, 1, device_id=(col, other, (chip + k) % n), device_id_type=mesh_id
        )
        pl.semaphore_signal(
            barrier, 1, device_id=((chip + k) % n, other, chip), device_id_type=mesh_id
        )
    for nb in (nxt, prv):
        pl.semaphore_signal(barrier, 1, device_id=(nb, core, col), device_id_type=mesh_id)
    pl.semaphore_signal(barrier, 1, device_id=(chip, other, col), device_id_type=mesh_id)
    n_part, part_width = w_hbm.shape[0], w_hbm.shape[2]
    w_loads, w_swaps = [], []
    for j in range(n_part):
        w_cols = pl.ds(j * part_width, part_width)
        w_loads.append(pltpu.make_async_copy(w_hbm.at[j], w_own.at[:, w_cols], wsem.at[0, j]))
        w_loads[-1].start()
    pl.semaphore_wait(barrier, 4 * n + 3 - 2 * diag.astype(jnp.int32))
    for j in range(n_part):
        w_cols = pl.ds(j * part_width, part_width)
        w_swaps.append(
            pltpu.make_async_remote_copy(
                src_ref=w_hbm.at[j], dst_ref=w_other.at[:, w_cols], send_sem=wsem.at[1, j],
                recv_sem=wsem.at[2, j], device_id=(chip, other, col), device_id_type=mesh_id,
            )
        )
        w_swaps[-1].start()

    slot = (chip + core) % n
    tail_rows = src_ref.at[pl.ds(rows - tail, tail)]
    tcopies, pcopies = [], []
    for k in range(n):
        dev = (col, core, (chip + k) % n)
        copy = pltpu.make_async_remote_copy(
            src_ref=src_ref, dst_ref=tok_buf.at[chip], send_sem=tsend.at[k],
            recv_sem=trecv.at[chip], device_id=dev, device_id_type=mesh_id,
        )
        if k == 0:
            own = pltpu.make_async_copy(src_ref, tok_buf.at[chip], trecv.at[chip])

            @pl.when(diag)
            def _():
                own.start()

            @pl.when(jnp.logical_not(diag))
            def _():
                copy.start()
        else:
            copy.start()
        tcopies.append(copy)
    for k in range(n):
        pcopy = pltpu.make_async_remote_copy(
            src_ref=tail_rows, dst_ref=prior_buf.at[slot], send_sem=psend.at[k],
            recv_sem=precv.at[slot], device_id=(col, other, (chip + k) % n),
            device_id_type=mesh_id,
        )
        pcopy.start()
        pcopies.append(pcopy)

    waited = set()

    def arrive(offset):
        if offset in waited:
            return
        waited.add(offset)
        blk = lookup(cyc, (r + offset) % n)
        pltpu.make_async_copy(src_ref, tok_buf.at[blk], trecv.at[blk]).wait()
        pltpu.make_async_copy(tail_rows, prior_buf.at[blk], precv.at[blk]).wait()

    for j in range(n_part):
        w_loads[j].wait()
        w_swaps[j].wait_recv()
    own_cols = pl.ds(pl.multiple_of(core * half, half), half)
    other_cols = pl.ds(pl.multiple_of((1 - core) * half, half), half)

    def part(blk, cols):
        def proj_rows(ref):
            return jnp.dot(
                ref[blk, :, own_cols], w_own[:, cols], preferred_element_type=jnp.float32
            ) + jnp.dot(ref[blk, :, other_cols], w_other[:, cols], preferred_element_type=jnp.float32)

        return jnp.concatenate([proj_rows(tok_buf), proj_rows(prior_buf)], axis=0)

    copies = [[] for _ in range(n_ring)]
    for s in range(n - 1):
        arrive((n - 1 - s) % n)
        arrive((1 + s) % n)
        for ring in range(n_ring):
            fwd = ring < n_ring // 2
            d, dest = (1, nxt) if fwd else (-1, prv)
            cols = pl.ds(ring * chunk, chunk)
            q = lookup(cyc, (r - d * (1 + s) + 2 * n) % n)
            if s == 0:
                sbuf[ring, 0] = part(q, cols).astype(sbuf.dtype)
            else:
                mine = part(q, cols)
                copies[ring][s - 1].wait_recv()
                sbuf[ring, s] = (rbuf[ring, s - 1].astype(jnp.float32) + mine).astype(sbuf.dtype)
            copy = pltpu.make_async_remote_copy(
                src_ref=sbuf.at[ring, s],
                dst_ref=rbuf.at[ring, s],
                send_sem=send_sem.at[ring, s],
                recv_sem=recv_sem.at[ring, s],
                device_id=(dest, core, col),
                device_id_type=mesh_id,
            )
            copy.start()
            copies[ring].append(copy)
    arrive(0)
    for ring in range(n_ring):
        cols = pl.ds(ring * chunk, chunk)
        mine = part(chip, cols)
        copies[ring][-1].wait_recv()
        total = (rbuf[ring, n - 2].astype(jnp.float32) + mine).astype(jnp.bfloat16)
        total = total.astype(jnp.float32)
        proj[pl.ds(tail, rows), cols] = total[:rows]
        proj[pl.ds(0, tail), cols] = total[rows:]

    @pl.when(jnp.logical_and(chip == 0, core == 0))
    def _():
        proj[0:tail, :] = jnp.zeros((tail, width), jnp.float32)

    third = width // 3
    mixed = []
    for j in range(3):
        cols = pl.ds(j * third, third)
        mixed.append(
            taps_ref[0, j][None, :] * proj[pl.ds(2, rows), cols]
            + taps_ref[1, j][None, :] * proj[pl.ds(1, rows), cols]
            + taps_ref[2, j][None, :] * proj[pl.ds(0, rows), cols]
        )
    q_ref[...] = mixed[0]
    g_ref[...] = (mixed[1] * mixed[2]).astype(g_ref.dtype)
    for ring in range(n_ring):
        for copy in copies[ring]:
            copy.wait_send()
    for k in range(n):
        if k == 0:
            @pl.when(jnp.logical_not(diag))
            def _():
                tcopies[0].wait_send()
        else:
            tcopies[k].wait_send()
        pcopies[k].wait_send()
    for j in range(n_part):
        w_swaps[j].wait_send()


def project_and_gate(tokens, w_own, taps, n_ring=6, tail=2):
    rows, tok_width = tokens.shape
    n = lax.axis_size("p")
    ext_len = rows + tail
    n_part, half, part_width = w_own.shape
    width = n_part * part_width
    third = width // 3
    vmem = pl.BlockSpec(memory_space=pltpu.VMEM)
    return pl.pallas_call(
        rs_kernel,
        out_shape=(
            jax.ShapeDtypeStruct((rows, third), jnp.float32),
            jax.ShapeDtypeStruct((rows, third), jnp.bfloat16),
        ),
        in_specs=[vmem, pl.BlockSpec(memory_space=pl.ANY), vmem],
        out_specs=(vmem, vmem),
        scratch_shapes=[
            pltpu.VMEM((n, rows, tok_width), tokens.dtype),
            pltpu.VMEM((n, tail, tok_width), tokens.dtype),
            pltpu.VMEM((half, width), w_own.dtype),
            pltpu.VMEM((half, width), w_own.dtype),
            pltpu.VMEM((n_ring, n - 1, ext_len, width // n_ring), jnp.bfloat16),
            pltpu.VMEM((n_ring, n - 1, ext_len, width // n_ring), jnp.bfloat16),
            pltpu.VMEM((ext_len, width), jnp.float32),
        ]
        + [pltpu.SemaphoreType.DMA((n,))] * 4
        + [pltpu.SemaphoreType.DMA((n_ring, n - 1))] * 2
        + [pltpu.SemaphoreType.DMA((3, n_part))],
        compiler_params=pltpu.CompilerParams(
            collective_id=0, has_side_effects=True, vmem_limit_bytes=48 * 1024 * 1024
        ),
    )(tokens, w_own, taps)


def tok_kernel(src_ref, out_ref, prior_ref, send_sem, recv_sem, psend_sem, precv_sem):
    n, rows, _ = out_ref.shape
    tail = prior_ref.shape[1]
    chip = lax.axis_index("p")
    core = lax.axis_index("c")
    col = lax.axis_index("ch")
    other = 1 - core
    mesh_id = pl.DeviceIdType.MESH
    diag = chip == col
    barrier = pltpu.get_barrier_semaphore()
    for k in range(n):
        dest = (col, core, (chip + k) % n)
        srce = ((chip + k) % n, core, chip)
        if k == 0:
            @pl.when(jnp.logical_not(diag))
            def _():
                pl.semaphore_signal(barrier, 1, device_id=dest, device_id_type=mesh_id)
                pl.semaphore_signal(barrier, 1, device_id=srce, device_id_type=mesh_id)
        else:
            pl.semaphore_signal(barrier, 1, device_id=dest, device_id_type=mesh_id)
            pl.semaphore_signal(barrier, 1, device_id=srce, device_id_type=mesh_id)
        pl.semaphore_signal(
            barrier, 1, device_id=(col, other, (chip + k) % n), device_id_type=mesh_id
        )
        pl.semaphore_signal(
            barrier, 1, device_id=((chip + k) % n, other, chip), device_id_type=mesh_id
        )
    pl.semaphore_wait(barrier, 4 * n - 2 * diag.astype(jnp.int32))
    slot = (chip + core) % n
    copies = []
    for k in range(n):
        copy = pltpu.make_async_remote_copy(
            src_ref=src_ref,
            dst_ref=out_ref.at[chip],
            send_sem=send_sem.at[k],
            recv_sem=recv_sem.at[chip],
            device_id=(col, core, (chip + k) % n),
            device_id_type=mesh_id,
        )
        if k == 0:
            own = pltpu.make_async_copy(src_ref, out_ref.at[chip], recv_sem.at[chip])

            @pl.when(diag)
            def _():
                own.start()

            @pl.when(jnp.logical_not(diag))
            def _():
                copy.start()
        else:
            copy.start()
        copies.append(copy)
    pcopies = []
    for k in range(n):
        pcopy = pltpu.make_async_remote_copy(
            src_ref=src_ref.at[pl.ds(rows - tail, tail)],
            dst_ref=prior_ref.at[slot],
            send_sem=psend_sem.at[k],
            recv_sem=precv_sem.at[slot],
            device_id=(col, other, (chip + k) % n),
            device_id_type=mesh_id,
        )
        pcopy.start()
        pcopies.append(pcopy)
    for j in range(n):
        pltpu.make_async_copy(src_ref, out_ref.at[j], recv_sem.at[j]).wait()
        pltpu.make_async_copy(
            src_ref.at[pl.ds(rows - tail, tail)], prior_ref.at[j], precv_sem.at[j]
        ).wait()
    for k in range(n):
        if k == 0:
            @pl.when(jnp.logical_not(diag))
            def _():
                copies[0].wait_send()
        else:
            copies[k].wait_send()
        pcopies[k].wait_send()


def spread_tokens(tokens, n, tail=2):
    rows, width = tokens.shape
    vmem = pl.BlockSpec(memory_space=pltpu.VMEM)
    return pl.pallas_call(
        tok_kernel,
        out_shape=(
            jax.ShapeDtypeStruct((n, rows, width), tokens.dtype),
            jax.ShapeDtypeStruct((n, tail, width), tokens.dtype),
        ),
        in_specs=[vmem],
        out_specs=(vmem, vmem),
        scratch_shapes=[pltpu.SemaphoreType.DMA((n,))] * 4,
        compiler_params=pltpu.CompilerParams(collective_id=1, has_side_effects=True),
    )(tokens)


def state_kernel(src_ref, lam_ref, out_ref, got, fac, send_sem, recv_sem, block_len):
    n = got.shape[0]
    n_core = lax.axis_size("c")
    me = lax.axis_index("p") * n_core + lax.axis_index("c")
    col = lax.axis_index("ch")
    mesh_id = pl.DeviceIdType.MESH
    barrier = pltpu.get_barrier_semaphore()
    for k in range(1, n):
        other = (me + k) % n
        pl.semaphore_signal(
            barrier, 1, device_id=(other // n_core, other % n_core, col), device_id_type=mesh_id
        )
    for j in range(n):
        @pl.when(j >= me)
        def _():
            got[j] = jnp.zeros(got.shape[1:], got.dtype)

        gap = jnp.maximum(me - 1 - j, 0).astype(jnp.float32)
        fac[j] = jnp.exp(-lam_ref[...] * (block_len * gap))
    pl.semaphore_wait(barrier, n - 1)
    copies = []
    for k in range(1, n):
        other = me + k
        copy = pltpu.make_async_remote_copy(
            src_ref=src_ref,
            dst_ref=got.at[me],
            send_sem=send_sem.at[k],
            recv_sem=recv_sem.at[me],
            device_id=(other // n_core, other % n_core, col),
            device_id_type=mesh_id,
        )

        @pl.when(other < n)
        def _():
            copy.start()

        copies.append((other, copy))
    for j in range(n):
        @pl.when(j < me)
        def _():
            pltpu.make_async_copy(src_ref, got.at[j], recv_sem.at[j]).wait()
    acc = jnp.zeros(out_ref.shape, jnp.float32)
    for j in range(n):
        acc = acc + fac[j] * got[j]
    out_ref[...] = acc
    for other, copy in copies:
        @pl.when(other < n)
        def _():
            copy.wait_send()


def gather_earlier(state, lam, n, block_len):
    vmem = pl.BlockSpec(memory_space=pltpu.VMEM)
    return pl.pallas_call(
        functools.partial(state_kernel, block_len=float(block_len)),
        out_shape=jax.ShapeDtypeStruct(state.shape, state.dtype),
        in_specs=[vmem, vmem],
        out_specs=vmem,
        scratch_shapes=[
            pltpu.VMEM((n,) + state.shape, state.dtype),
            pltpu.VMEM((n,) + state.shape, jnp.float32),
            pltpu.SemaphoreType.DMA((n,)),
            pltpu.SemaphoreType.DMA((n,)),
        ],
        compiler_params=pltpu.CompilerParams(collective_id=2, has_side_effects=True),
    )(state, lam)


def local(tokens, w_in, short_filter, decay_rate, residue, skip):
    n_chip = lax.axis_size("p")
    block_len = tokens.shape[0]
    local_width = w_in.shape[2]
    group_count = local_width // GROUP
    chip = lax.axis_index("p")
    core = lax.axis_index("c")
    col = lax.axis_index("ch")

    n_col = lax.axis_size("ch")
    w_parts = jnp.transpose(w_in, (1, 0, 2))
    query, gated = project_and_gate(tokens, w_parts, short_filter)
    x = gated.reshape(block_len, group_count, GROUP)

    pole_weight = residue * jnp.sqrt(2.0 * decay_rate)
    pos = jnp.arange(block_len, dtype=jnp.float32)
    lam = decay_rate[:, None, :]
    a_mat = pole_weight[:, None, :] * jnp.exp(-lam * pos[None, :, None])
    b_mat = jnp.exp(lam * pos[None, :, None])
    toep = jnp.einsum("gtr,gsr->gts", a_mat, b_mat, precision=lax.Precision.HIGH)
    causal = pos[:, None] >= pos[None, :]
    toep = jnp.where(causal[None], toep, 0.0)
    near = dot_split("gts,sgc->tgc", toep, x)

    e_mat = jnp.exp(-lam * (block_len - 1 - pos)[None, :, None])
    s_loc = dot_split("gsr,sgc->grc", e_mat, x)
    n_ctx = n_chip * lax.axis_size("c")
    me = chip * lax.axis_size("c") + core
    s_flat = s_loc.reshape(group_count, -1)
    lam_b = jnp.broadcast_to(decay_rate[..., None], decay_rate.shape + (GROUP,))
    s_in = gather_earlier(s_flat, lam_b.reshape(group_count, -1), n_ctx, block_len)
    s_in = s_in.reshape(s_loc.shape)
    f_mat = pole_weight[:, None, :] * jnp.exp(-lam * (pos + 1.0)[None, :, None])
    far = jnp.einsum("gtr,grc->tgc", f_mat, s_in, precision=HIGH)
    long_out = (near + far).reshape(block_len, local_width)
    out = query * (long_out + skip * gated.astype(jnp.float32))
    return out.astype(jnp.bfloat16)


def solution(mesh):
    n_ctx, n_ch = mesh.devices.shape
    sub = Mesh(mesh.devices.reshape(n_ctx // 2, 2, n_ch), ("p", "c", "ch"))
    ctx = ("p", "c")
    return jax.shard_map(
        local,
        mesh=sub,
        in_specs=(
            P(ctx, "ch"),
            P(ctx, None, "ch"),
            P(None, None, "ch"),
            P("ch", None),
            P("ch", None),
            P("ch"),
        ),
        out_specs=P(ctx, "ch"),
        check_vma=False,
    )
```

```python
import functools

import jax
import jax.numpy as jnp
from jax import lax
from jax.experimental import pallas as pl
from jax.experimental.pallas import tpu as pltpu
from jax.sharding import Mesh
from jax.sharding import PartitionSpec as P

GROUP = 16
HIGH = lax.Precision.HIGHEST


def split_bf16(x):
    hi = x.astype(jnp.bfloat16)
    lo = (x - hi.astype(jnp.float32)).astype(jnp.bfloat16)
    return hi, lo


def dot_split(spec, weight, data):
    hi, lo = split_bf16(weight)
    return jnp.einsum(spec, hi, data, preferred_element_type=jnp.float32) + jnp.einsum(
        spec, lo, data, preferred_element_type=jnp.float32
    )


CYCLES = (
    (0, 1, 3, 2, 4, 5, 7, 6),
    (0, 1, 3, 5, 7, 6, 4, 2),
    (0, 1, 7, 5, 3, 2, 4, 6),
    (0, 1, 7, 6, 4, 5, 3, 2),
    (0, 2, 3, 1, 7, 5, 4, 6),
    (0, 2, 4, 5, 3, 1, 7, 6),
)


def lookup(table, v):
    n = len(table)
    total = 0
    for k, t in enumerate(table):
        if t:
            total = total + t * (1 - ((v - k + n) % n + n - 1) // n)
    return total


def ring_chip(r, n):
    hi = r // (n // 2)
    return 2 * (r + hi * (n - 1 - 2 * r)) + hi


def ring_pos(p, n):
    z, y = p // 2, p % 2
    return z + y * (n - 1 - 2 * z)


def rs_kernel(
    src_ref, w_hbm, taps_ref, q_ref, g_ref,
    tok_buf, prior_buf, w_own, w_other, sbuf, rbuf, proj,
    tsend, trecv, psend, precv, send_sem, recv_sem, wsem,
):
    n, rows, _ = tok_buf.shape
    tail = prior_buf.shape[1]
    ext_len = rows + tail
    half, width = w_own.shape
    n_ring = sbuf.shape[0]
    chunk = width // n_ring
    chip = lax.axis_index("p")
    core = lax.axis_index("c")
    col = lax.axis_index("ch")
    other = 1 - core
    mesh_id = pl.DeviceIdType.MESH
    diag = chip == col
    cyc = CYCLES[0]
    r = lookup([cyc.index(p) for p in range(n)], chip)
    nxt = lookup(cyc, (r + 1) % n)
    prv = lookup(cyc, (r + n - 1) % n)

    barrier = pltpu.get_barrier_semaphore()
    for k in range(n):
        dest = (col, core, (chip + k) % n)
        srce = ((chip + k) % n, core, chip)
        if k == 0:
            @pl.when(jnp.logical_not(diag))
            def _():
                pl.semaphore_signal(barrier, 1, device_id=dest, device_id_type=mesh_id)
                pl.semaphore_signal(barrier, 1, device_id=srce, device_id_type=mesh_id)
        else:
            pl.semaphore_signal(barrier, 1, device_id=dest, device_id_type=mesh_id)
            pl.semaphore_signal(barrier, 1, device_id=srce, device_id_type=mesh_id)
        pl.semaphore_signal(
            barrier, 1, device_id=(col, other, (chip + k) % n), device_id_type=mesh_id
        )
        pl.semaphore_signal(
            barrier, 1, device_id=((chip + k) % n, other, chip), device_id_type=mesh_id
        )
    for nb in (nxt, prv):
        pl.semaphore_signal(barrier, 1, device_id=(nb, core, col), device_id_type=mesh_id)
    pl.semaphore_signal(barrier, 1, device_id=(chip, other, col), device_id_type=mesh_id)
    n_part, part_width = w_hbm.shape[0], w_hbm.shape[2]
    w_loads, w_swaps = [], []
    for j in range(n_part):
        w_cols = pl.ds(j * part_width, part_width)
        w_loads.append(pltpu.make_async_copy(w_hbm.at[j], w_own.at[:, w_cols], wsem.at[0, j]))
        w_loads[-1].start()
    pl.semaphore_wait(barrier, 4 * n + 3 - 2 * diag.astype(jnp.int32))
    for j in range(n_part):
        w_cols = pl.ds(j * part_width, part_width)
        w_swaps.append(
            pltpu.make_async_remote_copy(
                src_ref=w_hbm.at[j], dst_ref=w_other.at[:, w_cols], send_sem=wsem.at[1, j],
                recv_sem=wsem.at[2, j], device_id=(chip, other, col), device_id_type=mesh_id,
            )
        )
        w_swaps[-1].start()

    slot = (chip + core) % n
    tail_rows = src_ref.at[pl.ds(rows - tail, tail)]
    tcopies, pcopies = [], []
    for k in range(n):
        dev = (col, core, (chip + k) % n)
        copy = pltpu.make_async_remote_copy(
            src_ref=src_ref, dst_ref=tok_buf.at[chip], send_sem=tsend.at[k],
            recv_sem=trecv.at[chip], device_id=dev, device_id_type=mesh_id,
        )
        if k == 0:
            own = pltpu.make_async_copy(src_ref, tok_buf.at[chip], trecv.at[chip])

            @pl.when(diag)
            def _():
                own.start()

            @pl.when(jnp.logical_not(diag))
            def _():
                copy.start()
        else:
            copy.start()
        tcopies.append(copy)
    for k in range(n):
        pcopy = pltpu.make_async_remote_copy(
            src_ref=tail_rows, dst_ref=prior_buf.at[slot], send_sem=psend.at[k],
            recv_sem=precv.at[slot], device_id=(col, other, (chip + k) % n),
            device_id_type=mesh_id,
        )
        pcopy.start()
        pcopies.append(pcopy)

    waited = set()

    def arrive(offset):
        if offset in waited:
            return
        waited.add(offset)
        blk = lookup(cyc, (r + offset) % n)
        pltpu.make_async_copy(src_ref, tok_buf.at[blk], trecv.at[blk]).wait()
        pltpu.make_async_copy(tail_rows, prior_buf.at[blk], precv.at[blk]).wait()

    for j in range(n_part):
        w_loads[j].wait()
        w_swaps[j].wait_recv()
    own_cols = pl.ds(pl.multiple_of(core * half, half), half)
    other_cols = pl.ds(pl.multiple_of((1 - core) * half, half), half)

    def part(blk, cols):
        def proj_rows(ref):
            return jnp.dot(
                ref[blk, :, own_cols], w_own[:, cols], preferred_element_type=jnp.float32
            ) + jnp.dot(ref[blk, :, other_cols], w_other[:, cols], preferred_element_type=jnp.float32)

        return jnp.concatenate([proj_rows(tok_buf), proj_rows(prior_buf)], axis=0)

    copies = [[] for _ in range(n_ring)]
    for s in range(n - 1):
        arrive((n - 1 - s) % n)
        arrive((1 + s) % n)
        for ring in range(n_ring):
            fwd = ring < n_ring // 2
            d, dest = (1, nxt) if fwd else (-1, prv)
            cols = pl.ds(ring * chunk, chunk)
            q = lookup(cyc, (r - d * (1 + s) + 2 * n) % n)
            if s == 0:
                sbuf[ring, 0] = part(q, cols).astype(sbuf.dtype)
            else:
                mine = part(q, cols)
                copies[ring][s - 1].wait_recv()
                sbuf[ring, s] = (rbuf[ring, s - 1].astype(jnp.float32) + mine).astype(sbuf.dtype)
            copy = pltpu.make_async_remote_copy(
                src_ref=sbuf.at[ring, s],
                dst_ref=rbuf.at[ring, s],
                send_sem=send_sem.at[ring, s],
                recv_sem=recv_sem.at[ring, s],
                device_id=(dest, core, col),
                device_id_type=mesh_id,
            )
            copy.start()
            copies[ring].append(copy)
    arrive(0)
    for ring in range(n_ring):
        cols = pl.ds(ring * chunk, chunk)
        mine = part(chip, cols)
        copies[ring][-1].wait_recv()
        total = (rbuf[ring, n - 2].astype(jnp.float32) + mine).astype(jnp.bfloat16)
        total = total.astype(jnp.float32)
        proj[pl.ds(tail, rows), cols] = total[:rows]
        proj[pl.ds(0, tail), cols] = total[rows:]

    @pl.when(jnp.logical_and(chip == 0, core == 0))
    def _():
        proj[0:tail, :] = jnp.zeros((tail, width), jnp.float32)

    third = width // 3
    mixed = []
    for j in range(3):
        cols = pl.ds(j * third, third)
        mixed.append(
            taps_ref[0, j][None, :] * proj[pl.ds(2, rows), cols]
            + taps_ref[1, j][None, :] * proj[pl.ds(1, rows), cols]
            + taps_ref[2, j][None, :] * proj[pl.ds(0, rows), cols]
        )
    q_ref[...] = mixed[0]
    g_ref[...] = (mixed[1] * mixed[2]).astype(g_ref.dtype)
    for ring in range(n_ring):
        for copy in copies[ring]:
            copy.wait_send()
    for k in range(n):
        if k == 0:
            @pl.when(jnp.logical_not(diag))
            def _():
                tcopies[0].wait_send()
        else:
            tcopies[k].wait_send()
        pcopies[k].wait_send()
    for j in range(n_part):
        w_swaps[j].wait_send()


def project_and_gate(tokens, w_own, taps, n_ring=4, tail=2):
    rows, tok_width = tokens.shape
    n = lax.axis_size("p")
    ext_len = rows + tail
    n_part, half, part_width = w_own.shape
    width = n_part * part_width
    third = width // 3
    vmem = pl.BlockSpec(memory_space=pltpu.VMEM)
    return pl.pallas_call(
        rs_kernel,
        out_shape=(
            jax.ShapeDtypeStruct((rows, third), jnp.float32),
            jax.ShapeDtypeStruct((rows, third), jnp.bfloat16),
        ),
        in_specs=[vmem, pl.BlockSpec(memory_space=pl.ANY), vmem],
        out_specs=(vmem, vmem),
        scratch_shapes=[
            pltpu.VMEM((n, rows, tok_width), tokens.dtype),
            pltpu.VMEM((n, tail, tok_width), tokens.dtype),
            pltpu.VMEM((half, width), w_own.dtype),
            pltpu.VMEM((half, width), w_own.dtype),
            pltpu.VMEM((n_ring, n - 1, ext_len, width // n_ring), jnp.bfloat16),
            pltpu.VMEM((n_ring, n - 1, ext_len, width // n_ring), jnp.bfloat16),
            pltpu.VMEM((ext_len, width), jnp.float32),
        ]
        + [pltpu.SemaphoreType.DMA((n,))] * 4
        + [pltpu.SemaphoreType.DMA((n_ring, n - 1))] * 2
        + [pltpu.SemaphoreType.DMA((3, n_part))],
        compiler_params=pltpu.CompilerParams(
            collective_id=0, has_side_effects=True, vmem_limit_bytes=48 * 1024 * 1024
        ),
    )(tokens, w_own, taps)


def tok_kernel(src_ref, out_ref, prior_ref, send_sem, recv_sem, psend_sem, precv_sem):
    n, rows, _ = out_ref.shape
    tail = prior_ref.shape[1]
    chip = lax.axis_index("p")
    core = lax.axis_index("c")
    col = lax.axis_index("ch")
    other = 1 - core
    mesh_id = pl.DeviceIdType.MESH
    diag = chip == col
    barrier = pltpu.get_barrier_semaphore()
    for k in range(n):
        dest = (col, core, (chip + k) % n)
        srce = ((chip + k) % n, core, chip)
        if k == 0:
            @pl.when(jnp.logical_not(diag))
            def _():
                pl.semaphore_signal(barrier, 1, device_id=dest, device_id_type=mesh_id)
                pl.semaphore_signal(barrier, 1, device_id=srce, device_id_type=mesh_id)
        else:
            pl.semaphore_signal(barrier, 1, device_id=dest, device_id_type=mesh_id)
            pl.semaphore_signal(barrier, 1, device_id=srce, device_id_type=mesh_id)
        pl.semaphore_signal(
            barrier, 1, device_id=(col, other, (chip + k) % n), device_id_type=mesh_id
        )
        pl.semaphore_signal(
            barrier, 1, device_id=((chip + k) % n, other, chip), device_id_type=mesh_id
        )
    pl.semaphore_wait(barrier, 4 * n - 2 * diag.astype(jnp.int32))
    slot = (chip + core) % n
    copies = []
    for k in range(n):
        copy = pltpu.make_async_remote_copy(
            src_ref=src_ref,
            dst_ref=out_ref.at[chip],
            send_sem=send_sem.at[k],
            recv_sem=recv_sem.at[chip],
            device_id=(col, core, (chip + k) % n),
            device_id_type=mesh_id,
        )
        if k == 0:
            own = pltpu.make_async_copy(src_ref, out_ref.at[chip], recv_sem.at[chip])

            @pl.when(diag)
            def _():
                own.start()

            @pl.when(jnp.logical_not(diag))
            def _():
                copy.start()
        else:
            copy.start()
        copies.append(copy)
    pcopies = []
    for k in range(n):
        pcopy = pltpu.make_async_remote_copy(
            src_ref=src_ref.at[pl.ds(rows - tail, tail)],
            dst_ref=prior_ref.at[slot],
            send_sem=psend_sem.at[k],
            recv_sem=precv_sem.at[slot],
            device_id=(col, other, (chip + k) % n),
            device_id_type=mesh_id,
        )
        pcopy.start()
        pcopies.append(pcopy)
    for j in range(n):
        pltpu.make_async_copy(src_ref, out_ref.at[j], recv_sem.at[j]).wait()
        pltpu.make_async_copy(
            src_ref.at[pl.ds(rows - tail, tail)], prior_ref.at[j], precv_sem.at[j]
        ).wait()
    for k in range(n):
        if k == 0:
            @pl.when(jnp.logical_not(diag))
            def _():
                copies[0].wait_send()
        else:
            copies[k].wait_send()
        pcopies[k].wait_send()


def spread_tokens(tokens, n, tail=2):
    rows, width = tokens.shape
    vmem = pl.BlockSpec(memory_space=pltpu.VMEM)
    return pl.pallas_call(
        tok_kernel,
        out_shape=(
            jax.ShapeDtypeStruct((n, rows, width), tokens.dtype),
            jax.ShapeDtypeStruct((n, tail, width), tokens.dtype),
        ),
        in_specs=[vmem],
        out_specs=(vmem, vmem),
        scratch_shapes=[pltpu.SemaphoreType.DMA((n,))] * 4,
        compiler_params=pltpu.CompilerParams(collective_id=1, has_side_effects=True),
    )(tokens)


def state_kernel(src_ref, lam_ref, out_ref, got, fac, send_sem, recv_sem, block_len):
    n = got.shape[0]
    n_core = lax.axis_size("c")
    me = lax.axis_index("p") * n_core + lax.axis_index("c")
    col = lax.axis_index("ch")
    mesh_id = pl.DeviceIdType.MESH
    barrier = pltpu.get_barrier_semaphore()
    for k in range(1, n):
        other = (me + k) % n
        pl.semaphore_signal(
            barrier, 1, device_id=(other // n_core, other % n_core, col), device_id_type=mesh_id
        )
    for j in range(n):
        @pl.when(j >= me)
        def _():
            got[j] = jnp.zeros(got.shape[1:], got.dtype)

        gap = jnp.maximum(me - 1 - j, 0).astype(jnp.float32)
        fac[j] = jnp.exp(-lam_ref[...] * (block_len * gap))
    pl.semaphore_wait(barrier, n - 1)
    copies = []
    for k in range(1, n):
        other = me + k
        copy = pltpu.make_async_remote_copy(
            src_ref=src_ref,
            dst_ref=got.at[me],
            send_sem=send_sem.at[k],
            recv_sem=recv_sem.at[me],
            device_id=(other // n_core, other % n_core, col),
            device_id_type=mesh_id,
        )

        @pl.when(other < n)
        def _():
            copy.start()

        copies.append((other, copy))
    for j in range(n):
        @pl.when(j < me)
        def _():
            pltpu.make_async_copy(src_ref, got.at[j], recv_sem.at[j]).wait()
    acc = jnp.zeros(out_ref.shape, jnp.float32)
    for j in range(n):
        acc = acc + fac[j] * got[j]
    out_ref[...] = acc
    for other, copy in copies:
        @pl.when(other < n)
        def _():
            copy.wait_send()


def gather_earlier(state, lam, n, block_len):
    vmem = pl.BlockSpec(memory_space=pltpu.VMEM)
    return pl.pallas_call(
        functools.partial(state_kernel, block_len=float(block_len)),
        out_shape=jax.ShapeDtypeStruct(state.shape, state.dtype),
        in_specs=[vmem, vmem],
        out_specs=vmem,
        scratch_shapes=[
            pltpu.VMEM((n,) + state.shape, state.dtype),
            pltpu.VMEM((n,) + state.shape, jnp.float32),
            pltpu.SemaphoreType.DMA((n,)),
            pltpu.SemaphoreType.DMA((n,)),
        ],
        compiler_params=pltpu.CompilerParams(collective_id=2, has_side_effects=True),
    )(state, lam)


def local(tokens, w_in, short_filter, decay_rate, residue, skip):
    n_chip = lax.axis_size("p")
    block_len = tokens.shape[0]
    local_width = w_in.shape[2]
    group_count = local_width // GROUP
    chip = lax.axis_index("p")
    core = lax.axis_index("c")
    col = lax.axis_index("ch")

    n_col = lax.axis_size("ch")
    w_parts = jnp.transpose(w_in, (1, 0, 2))
    query, gated = project_and_gate(tokens, w_parts, short_filter)
    x = gated.reshape(block_len, group_count, GROUP)

    pole_weight = residue * jnp.sqrt(2.0 * decay_rate)
    pos = jnp.arange(block_len, dtype=jnp.float32)
    lam = decay_rate[:, None, :]
    a_mat = pole_weight[:, None, :] * jnp.exp(-lam * pos[None, :, None])
    b_mat = jnp.exp(lam * pos[None, :, None])
    toep = jnp.einsum("gtr,gsr->gts", a_mat, b_mat, precision=lax.Precision.HIGH)
    causal = pos[:, None] >= pos[None, :]
    toep = jnp.where(causal[None], toep, 0.0)
    near = dot_split("gts,sgc->tgc", toep, x)

    e_mat = jnp.exp(-lam * (block_len - 1 - pos)[None, :, None])
    s_loc = dot_split("gsr,sgc->grc", e_mat, x)
    n_ctx = n_chip * lax.axis_size("c")
    me = chip * lax.axis_size("c") + core
    s_flat = s_loc.reshape(group_count, -1)
    lam_b = jnp.broadcast_to(decay_rate[..., None], decay_rate.shape + (GROUP,))
    s_in = gather_earlier(s_flat, lam_b.reshape(group_count, -1), n_ctx, block_len)
    s_in = s_in.reshape(s_loc.shape)
    f_mat = pole_weight[:, None, :] * jnp.exp(-lam * (pos + 1.0)[None, :, None])
    far = jnp.einsum("gtr,grc->tgc", f_mat, s_in, precision=HIGH)
    long_out = (near + far).reshape(block_len, local_width)
    out = query * (long_out + skip * gated.astype(jnp.float32))
    return out.astype(jnp.bfloat16)


def solution(mesh):
    n_ctx, n_ch = mesh.devices.shape
    sub = Mesh(mesh.devices.reshape(n_ctx // 2, 2, n_ch), ("p", "c", "ch"))
    ctx = ("p", "c")
    return jax.shard_map(
        local,
        mesh=sub,
        in_specs=(
            P(ctx, "ch"),
            P(ctx, None, "ch"),
            P(None, None, "ch"),
            P("ch", None),
            P("ch", None),
            P("ch"),
        ),
        out_specs=P(ctx, "ch"),
        check_vma=False,
    )
```

```python
import functools

import jax
import jax.numpy as jnp
from jax import lax
from jax.experimental import pallas as pl
from jax.experimental.pallas import tpu as pltpu
from jax.sharding import Mesh
from jax.sharding import PartitionSpec as P

GROUP = 16
HIGH = lax.Precision.HIGHEST


def split_bf16(x):
    hi = x.astype(jnp.bfloat16)
    lo = (x - hi.astype(jnp.float32)).astype(jnp.bfloat16)
    return hi, lo


def dot_split(spec, weight, data):
    hi, lo = split_bf16(weight)
    return jnp.einsum(spec, hi, data, preferred_element_type=jnp.float32) + jnp.einsum(
        spec, lo, data, preferred_element_type=jnp.float32
    )


CYCLES = (
    (0, 1, 3, 2, 4, 5, 7, 6),
    (0, 1, 3, 5, 7, 6, 4, 2),
    (0, 1, 7, 5, 3, 2, 4, 6),
    (0, 1, 7, 6, 4, 5, 3, 2),
    (0, 2, 3, 1, 7, 5, 4, 6),
    (0, 2, 4, 5, 3, 1, 7, 6),
)


def lookup(table, v):
    n = len(table)
    total = 0
    for k, t in enumerate(table):
        if t:
            total = total + t * (1 - ((v - k + n) % n + n - 1) // n)
    return total


def ring_chip(r, n):
    hi = r // (n // 2)
    return 2 * (r + hi * (n - 1 - 2 * r)) + hi


def ring_pos(p, n):
    z, y = p // 2, p % 2
    return z + y * (n - 1 - 2 * z)


def rs_kernel(
    src_ref, w_hbm, taps_ref, q_ref, g_ref,
    tok_buf, prior_buf, w_own, w_other, sbuf, rbuf, proj,
    tsend, trecv, psend, precv, send_sem, recv_sem, wsem,
):
    n, rows, _ = tok_buf.shape
    tail = prior_buf.shape[1]
    ext_len = rows + tail
    half, width = w_own.shape
    n_ring = sbuf.shape[0]
    chunk = width // n_ring
    chip = lax.axis_index("p")
    core = lax.axis_index("c")
    col = lax.axis_index("ch")
    other = 1 - core
    mesh_id = pl.DeviceIdType.MESH
    diag = chip == col
    cyc = CYCLES[0]
    r = lookup([cyc.index(p) for p in range(n)], chip)
    nxt = lookup(cyc, (r + 1) % n)
    prv = lookup(cyc, (r + n - 1) % n)

    barrier = pltpu.get_barrier_semaphore()
    for k in range(n):
        dest = (col, core, (chip + k) % n)
        srce = ((chip + k) % n, core, chip)
        if k == 0:
            @pl.when(jnp.logical_not(diag))
            def _():
                pl.semaphore_signal(barrier, 1, device_id=dest, device_id_type=mesh_id)
                pl.semaphore_signal(barrier, 1, device_id=srce, device_id_type=mesh_id)
        else:
            pl.semaphore_signal(barrier, 1, device_id=dest, device_id_type=mesh_id)
            pl.semaphore_signal(barrier, 1, device_id=srce, device_id_type=mesh_id)
        pl.semaphore_signal(
            barrier, 1, device_id=(col, other, (chip + k) % n), device_id_type=mesh_id
        )
        pl.semaphore_signal(
            barrier, 1, device_id=((chip + k) % n, other, chip), device_id_type=mesh_id
        )
    for nb in (nxt, prv):
        pl.semaphore_signal(barrier, 1, device_id=(nb, core, col), device_id_type=mesh_id)
    pl.semaphore_signal(barrier, 1, device_id=(chip, other, col), device_id_type=mesh_id)
    n_part, part_width = w_hbm.shape[0], w_hbm.shape[2]
    w_loads, w_swaps = [], []
    for j in range(n_part):
        w_cols = pl.ds(j * part_width, part_width)
        w_loads.append(pltpu.make_async_copy(w_hbm.at[j], w_own.at[:, w_cols], wsem.at[0, j]))
        w_loads[-1].start()
    pl.semaphore_wait(barrier, 4 * n + 3 - 2 * diag.astype(jnp.int32))
    for j in range(n_part):
        w_cols = pl.ds(j * part_width, part_width)
        w_swaps.append(
            pltpu.make_async_remote_copy(
                src_ref=w_hbm.at[j], dst_ref=w_other.at[:, w_cols], send_sem=wsem.at[1, j],
                recv_sem=wsem.at[2, j], device_id=(chip, other, col), device_id_type=mesh_id,
            )
        )
        w_swaps[-1].start()

    slot = (chip + core) % n
    tail_rows = src_ref.at[pl.ds(rows - tail, tail)]
    tcopies, pcopies = [], []
    half_rows = rows // 2
    for k in range(n):
        dev = (col, core, (chip + k) % n)
        pair = []
        for h in range(2):
            piece = pl.ds(h * half_rows, half_rows)
            pair.append(
                pltpu.make_async_remote_copy(
                    src_ref=src_ref.at[piece], dst_ref=tok_buf.at[chip, piece],
                    send_sem=tsend.at[k, h], recv_sem=trecv.at[chip], device_id=dev,
                    device_id_type=mesh_id,
                )
            )
        if k == 0:
            own = pltpu.make_async_copy(src_ref, tok_buf.at[chip], trecv.at[chip])

            @pl.when(diag)
            def _():
                own.start()

            @pl.when(jnp.logical_not(diag))
            def _():
                for copy in pair:
                    copy.start()
        else:
            for copy in pair:
                copy.start()
        tcopies.append(pair)
    for k in range(n):
        pcopy = pltpu.make_async_remote_copy(
            src_ref=tail_rows, dst_ref=prior_buf.at[slot], send_sem=psend.at[k],
            recv_sem=precv.at[slot], device_id=(col, other, (chip + k) % n),
            device_id_type=mesh_id,
        )
        pcopy.start()
        pcopies.append(pcopy)

    waited = set()

    def arrive(offset):
        if offset in waited:
            return
        waited.add(offset)
        blk = lookup(cyc, (r + offset) % n)
        pltpu.make_async_copy(src_ref, tok_buf.at[blk], trecv.at[blk]).wait()
        pltpu.make_async_copy(tail_rows, prior_buf.at[blk], precv.at[blk]).wait()

    for j in range(n_part):
        w_loads[j].wait()
        w_swaps[j].wait_recv()
    own_cols = pl.ds(pl.multiple_of(core * half, half), half)
    other_cols = pl.ds(pl.multiple_of((1 - core) * half, half), half)

    def part(blk, cols):
        def proj_rows(ref):
            return jnp.dot(
                ref[blk, :, own_cols], w_own[:, cols], preferred_element_type=jnp.float32
            ) + jnp.dot(ref[blk, :, other_cols], w_other[:, cols], preferred_element_type=jnp.float32)

        return jnp.concatenate([proj_rows(tok_buf), proj_rows(prior_buf)], axis=0)

    copies = [[] for _ in range(n_ring)]
    for s in range(n - 1):
        arrive((n - 1 - s) % n)
        arrive((1 + s) % n)
        for ring in range(n_ring):
            fwd = ring < n_ring // 2
            d, dest = (1, nxt) if fwd else (-1, prv)
            cols = pl.ds(ring * chunk, chunk)
            q = lookup(cyc, (r - d * (1 + s) + 2 * n) % n)
            if s == 0:
                sbuf[ring, 0] = part(q, cols).astype(sbuf.dtype)
            else:
                mine = part(q, cols)
                copies[ring][s - 1].wait_recv()
                sbuf[ring, s] = (rbuf[ring, s - 1].astype(jnp.float32) + mine).astype(sbuf.dtype)
            copy = pltpu.make_async_remote_copy(
                src_ref=sbuf.at[ring, s],
                dst_ref=rbuf.at[ring, s],
                send_sem=send_sem.at[ring, s],
                recv_sem=recv_sem.at[ring, s],
                device_id=(dest, core, col),
                device_id_type=mesh_id,
            )
            copy.start()
            copies[ring].append(copy)
    arrive(0)
    for ring in range(n_ring):
        cols = pl.ds(ring * chunk, chunk)
        mine = part(chip, cols)
        copies[ring][-1].wait_recv()
        total = (rbuf[ring, n - 2].astype(jnp.float32) + mine).astype(jnp.bfloat16)
        total = total.astype(jnp.float32)
        proj[pl.ds(tail, rows), cols] = total[:rows]
        proj[pl.ds(0, tail), cols] = total[rows:]

    @pl.when(jnp.logical_and(chip == 0, core == 0))
    def _():
        proj[0:tail, :] = jnp.zeros((tail, width), jnp.float32)

    third = width // 3
    mixed = []
    for j in range(3):
        cols = pl.ds(j * third, third)
        mixed.append(
            taps_ref[0, j][None, :] * proj[pl.ds(2, rows), cols]
            + taps_ref[1, j][None, :] * proj[pl.ds(1, rows), cols]
            + taps_ref[2, j][None, :] * proj[pl.ds(0, rows), cols]
        )
    q_ref[...] = mixed[0]
    g_ref[...] = (mixed[1] * mixed[2]).astype(g_ref.dtype)
    for ring in range(n_ring):
        for copy in copies[ring]:
            copy.wait_send()
    for k in range(n):
        if k == 0:
            @pl.when(jnp.logical_not(diag))
            def _():
                for copy in tcopies[0]:
                    copy.wait_send()
        else:
            for copy in tcopies[k]:
                copy.wait_send()
        pcopies[k].wait_send()
    for j in range(n_part):
        w_swaps[j].wait_send()


def project_and_gate(tokens, w_own, taps, n_ring=6, tail=2):
    rows, tok_width = tokens.shape
    n = lax.axis_size("p")
    ext_len = rows + tail
    n_part, half, part_width = w_own.shape
    width = n_part * part_width
    third = width // 3
    vmem = pl.BlockSpec(memory_space=pltpu.VMEM)
    return pl.pallas_call(
        rs_kernel,
        out_shape=(
            jax.ShapeDtypeStruct((rows, third), jnp.float32),
            jax.ShapeDtypeStruct((rows, third), jnp.bfloat16),
        ),
        in_specs=[vmem, pl.BlockSpec(memory_space=pl.ANY), vmem],
        out_specs=(vmem, vmem),
        scratch_shapes=[
            pltpu.VMEM((n, rows, tok_width), tokens.dtype),
            pltpu.VMEM((n, tail, tok_width), tokens.dtype),
            pltpu.VMEM((half, width), w_own.dtype),
            pltpu.VMEM((half, width), w_own.dtype),
            pltpu.VMEM((n_ring, n - 1, ext_len, width // n_ring), jnp.bfloat16),
            pltpu.VMEM((n_ring, n - 1, ext_len, width // n_ring), jnp.bfloat16),
            pltpu.VMEM((ext_len, width), jnp.float32),
        ]
        + [pltpu.SemaphoreType.DMA((n, 2)), pltpu.SemaphoreType.DMA((n,))]
        + [pltpu.SemaphoreType.DMA((n,))] * 2
        + [pltpu.SemaphoreType.DMA((n_ring, n - 1))] * 2
        + [pltpu.SemaphoreType.DMA((3, n_part))],
        compiler_params=pltpu.CompilerParams(
            collective_id=0, has_side_effects=True, vmem_limit_bytes=48 * 1024 * 1024
        ),
    )(tokens, w_own, taps)


def tok_kernel(src_ref, out_ref, prior_ref, send_sem, recv_sem, psend_sem, precv_sem):
    n, rows, _ = out_ref.shape
    tail = prior_ref.shape[1]
    chip = lax.axis_index("p")
    core = lax.axis_index("c")
    col = lax.axis_index("ch")
    other = 1 - core
    mesh_id = pl.DeviceIdType.MESH
    diag = chip == col
    barrier = pltpu.get_barrier_semaphore()
    for k in range(n):
        dest = (col, core, (chip + k) % n)
        srce = ((chip + k) % n, core, chip)
        if k == 0:
            @pl.when(jnp.logical_not(diag))
            def _():
                pl.semaphore_signal(barrier, 1, device_id=dest, device_id_type=mesh_id)
                pl.semaphore_signal(barrier, 1, device_id=srce, device_id_type=mesh_id)
        else:
            pl.semaphore_signal(barrier, 1, device_id=dest, device_id_type=mesh_id)
            pl.semaphore_signal(barrier, 1, device_id=srce, device_id_type=mesh_id)
        pl.semaphore_signal(
            barrier, 1, device_id=(col, other, (chip + k) % n), device_id_type=mesh_id
        )
        pl.semaphore_signal(
            barrier, 1, device_id=((chip + k) % n, other, chip), device_id_type=mesh_id
        )
    pl.semaphore_wait(barrier, 4 * n - 2 * diag.astype(jnp.int32))
    slot = (chip + core) % n
    copies = []
    for k in range(n):
        copy = pltpu.make_async_remote_copy(
            src_ref=src_ref,
            dst_ref=out_ref.at[chip],
            send_sem=send_sem.at[k],
            recv_sem=recv_sem.at[chip],
            device_id=(col, core, (chip + k) % n),
            device_id_type=mesh_id,
        )
        if k == 0:
            own = pltpu.make_async_copy(src_ref, out_ref.at[chip], recv_sem.at[chip])

            @pl.when(diag)
            def _():
                own.start()

            @pl.when(jnp.logical_not(diag))
            def _():
                copy.start()
        else:
            copy.start()
        copies.append(copy)
    pcopies = []
    for k in range(n):
        pcopy = pltpu.make_async_remote_copy(
            src_ref=src_ref.at[pl.ds(rows - tail, tail)],
            dst_ref=prior_ref.at[slot],
            send_sem=psend_sem.at[k],
            recv_sem=precv_sem.at[slot],
            device_id=(col, other, (chip + k) % n),
            device_id_type=mesh_id,
        )
        pcopy.start()
        pcopies.append(pcopy)
    for j in range(n):
        pltpu.make_async_copy(src_ref, out_ref.at[j], recv_sem.at[j]).wait()
        pltpu.make_async_copy(
            src_ref.at[pl.ds(rows - tail, tail)], prior_ref.at[j], precv_sem.at[j]
        ).wait()
    for k in range(n):
        if k == 0:
            @pl.when(jnp.logical_not(diag))
            def _():
                copies[0].wait_send()
        else:
            copies[k].wait_send()
        pcopies[k].wait_send()


def spread_tokens(tokens, n, tail=2):
    rows, width = tokens.shape
    vmem = pl.BlockSpec(memory_space=pltpu.VMEM)
    return pl.pallas_call(
        tok_kernel,
        out_shape=(
            jax.ShapeDtypeStruct((n, rows, width), tokens.dtype),
            jax.ShapeDtypeStruct((n, tail, width), tokens.dtype),
        ),
        in_specs=[vmem],
        out_specs=(vmem, vmem),
        scratch_shapes=[pltpu.SemaphoreType.DMA((n,))] * 4,
        compiler_params=pltpu.CompilerParams(collective_id=1, has_side_effects=True),
    )(tokens)


def state_kernel(src_ref, lam_ref, out_ref, got, fac, send_sem, recv_sem, block_len):
    n = got.shape[0]
    n_core = lax.axis_size("c")
    me = lax.axis_index("p") * n_core + lax.axis_index("c")
    col = lax.axis_index("ch")
    mesh_id = pl.DeviceIdType.MESH
    barrier = pltpu.get_barrier_semaphore()
    for k in range(1, n):
        other = (me + k) % n
        pl.semaphore_signal(
            barrier, 1, device_id=(other // n_core, other % n_core, col), device_id_type=mesh_id
        )
    for j in range(n):
        @pl.when(j >= me)
        def _():
            got[j] = jnp.zeros(got.shape[1:], got.dtype)

        gap = jnp.maximum(me - 1 - j, 0).astype(jnp.float32)
        fac[j] = jnp.exp(-lam_ref[...] * (block_len * gap))
    pl.semaphore_wait(barrier, n - 1)
    copies = []
    for k in range(1, n):
        other = me + k
        copy = pltpu.make_async_remote_copy(
            src_ref=src_ref,
            dst_ref=got.at[me],
            send_sem=send_sem.at[k],
            recv_sem=recv_sem.at[me],
            device_id=(other // n_core, other % n_core, col),
            device_id_type=mesh_id,
        )

        @pl.when(other < n)
        def _():
            copy.start()

        copies.append((other, copy))
    for j in range(n):
        @pl.when(j < me)
        def _():
            pltpu.make_async_copy(src_ref, got.at[j], recv_sem.at[j]).wait()
    acc = jnp.zeros(out_ref.shape, jnp.float32)
    for j in range(n):
        acc = acc + fac[j] * got[j]
    out_ref[...] = acc
    for other, copy in copies:
        @pl.when(other < n)
        def _():
            copy.wait_send()


def gather_earlier(state, lam, n, block_len):
    vmem = pl.BlockSpec(memory_space=pltpu.VMEM)
    return pl.pallas_call(
        functools.partial(state_kernel, block_len=float(block_len)),
        out_shape=jax.ShapeDtypeStruct(state.shape, state.dtype),
        in_specs=[vmem, vmem],
        out_specs=vmem,
        scratch_shapes=[
            pltpu.VMEM((n,) + state.shape, state.dtype),
            pltpu.VMEM((n,) + state.shape, jnp.float32),
            pltpu.SemaphoreType.DMA((n,)),
            pltpu.SemaphoreType.DMA((n,)),
        ],
        compiler_params=pltpu.CompilerParams(collective_id=2, has_side_effects=True),
    )(state, lam)


def local(tokens, w_in, short_filter, decay_rate, residue, skip):
    n_chip = lax.axis_size("p")
    block_len = tokens.shape[0]
    local_width = w_in.shape[2]
    group_count = local_width // GROUP
    chip = lax.axis_index("p")
    core = lax.axis_index("c")
    col = lax.axis_index("ch")

    n_col = lax.axis_size("ch")
    w_parts = jnp.transpose(w_in, (1, 0, 2))
    query, gated = project_and_gate(tokens, w_parts, short_filter)
    x = gated.reshape(block_len, group_count, GROUP)

    pole_weight = residue * jnp.sqrt(2.0 * decay_rate)
    pos = jnp.arange(block_len, dtype=jnp.float32)
    lam = decay_rate[:, None, :]
    a_mat = pole_weight[:, None, :] * jnp.exp(-lam * pos[None, :, None])
    b_mat = jnp.exp(lam * pos[None, :, None])
    toep = jnp.einsum("gtr,gsr->gts", a_mat, b_mat, precision=lax.Precision.HIGH)
    causal = pos[:, None] >= pos[None, :]
    toep = jnp.where(causal[None], toep, 0.0)
    near = dot_split("gts,sgc->tgc", toep, x)

    e_mat = jnp.exp(-lam * (block_len - 1 - pos)[None, :, None])
    s_loc = dot_split("gsr,sgc->grc", e_mat, x)
    n_ctx = n_chip * lax.axis_size("c")
    me = chip * lax.axis_size("c") + core
    s_flat = s_loc.reshape(group_count, -1)
    lam_b = jnp.broadcast_to(decay_rate[..., None], decay_rate.shape + (GROUP,))
    s_in = gather_earlier(s_flat, lam_b.reshape(group_count, -1), n_ctx, block_len)
    s_in = s_in.reshape(s_loc.shape)
    f_mat = pole_weight[:, None, :] * jnp.exp(-lam * (pos + 1.0)[None, :, None])
    far = jnp.einsum("gtr,grc->tgc", f_mat, s_in, precision=HIGH)
    long_out = (near + far).reshape(block_len, local_width)
    out = query * (long_out + skip * gated.astype(jnp.float32))
    return out.astype(jnp.bfloat16)


def solution(mesh):
    n_ctx, n_ch = mesh.devices.shape
    sub = Mesh(mesh.devices.reshape(n_ctx // 2, 2, n_ch), ("p", "c", "ch"))
    ctx = ("p", "c")
    return jax.shard_map(
        local,
        mesh=sub,
        in_specs=(
            P(ctx, "ch"),
            P(ctx, None, "ch"),
            P(None, None, "ch"),
            P("ch", None),
            P("ch", None),
            P("ch"),
        ),
        out_specs=P(ctx, "ch"),
        check_vma=False,
    )
```

```python
import functools

import jax
import jax.numpy as jnp
from jax import lax
from jax.experimental import pallas as pl
from jax.experimental.pallas import tpu as pltpu
from jax.sharding import Mesh
from jax.sharding import PartitionSpec as P

GROUP = 16
HIGH = lax.Precision.HIGHEST


def split_bf16(x):
    hi = x.astype(jnp.bfloat16)
    lo = (x - hi.astype(jnp.float32)).astype(jnp.bfloat16)
    return hi, lo


def dot_split(spec, weight, data):
    hi, lo = split_bf16(weight)
    return jnp.einsum(spec, hi, data, preferred_element_type=jnp.float32) + jnp.einsum(
        spec, lo, data, preferred_element_type=jnp.float32
    )


CYCLES = (
    (0, 1, 3, 2, 4, 5, 7, 6),
    (0, 1, 3, 5, 7, 6, 4, 2),
    (0, 1, 7, 5, 3, 2, 4, 6),
    (0, 1, 7, 6, 4, 5, 3, 2),
    (0, 2, 3, 1, 7, 5, 4, 6),
    (0, 2, 4, 5, 3, 1, 7, 6),
)


def lookup(table, v):
    n = len(table)
    total = 0
    for k, t in enumerate(table):
        if t:
            total = total + t * (1 - ((v - k + n) % n + n - 1) // n)
    return total


def ring_chip(r, n):
    hi = r // (n // 2)
    return 2 * (r + hi * (n - 1 - 2 * r)) + hi


def ring_pos(p, n):
    z, y = p // 2, p % 2
    return z + y * (n - 1 - 2 * z)


def rs_kernel(
    src_hbm, w_hbm, taps_hbm, q_ref, g_ref,
    src_ref, taps_ref, tok_buf, prior_buf, w_own, w_other, sbuf, rbuf, proj,
    tsend, trecv, psend, precv, send_sem, recv_sem, wsem, lsem,
):
    n, rows, _ = tok_buf.shape
    tail = prior_buf.shape[1]
    ext_len = rows + tail
    half, width = w_own.shape
    n_ring = sbuf.shape[0]
    chunk = width // n_ring
    chip = lax.axis_index("p")
    core = lax.axis_index("c")
    col = lax.axis_index("ch")
    other = 1 - core
    mesh_id = pl.DeviceIdType.MESH
    diag = chip == col
    cyc = CYCLES[0]
    r = lookup([cyc.index(p) for p in range(n)], chip)
    nxt = lookup(cyc, (r + 1) % n)
    prv = lookup(cyc, (r + n - 1) % n)

    src_load = pltpu.make_async_copy(src_hbm, src_ref, lsem.at[0])
    src_load.start()
    taps_load = pltpu.make_async_copy(taps_hbm, taps_ref, lsem.at[1])
    taps_load.start()
    barrier = pltpu.get_barrier_semaphore()
    for k in range(n):
        dest = (col, core, (chip + k) % n)
        srce = ((chip + k) % n, core, chip)
        if k == 0:
            @pl.when(jnp.logical_not(diag))
            def _():
                pl.semaphore_signal(barrier, 1, device_id=dest, device_id_type=mesh_id)
                pl.semaphore_signal(barrier, 1, device_id=srce, device_id_type=mesh_id)
        else:
            pl.semaphore_signal(barrier, 1, device_id=dest, device_id_type=mesh_id)
            pl.semaphore_signal(barrier, 1, device_id=srce, device_id_type=mesh_id)
        pl.semaphore_signal(
            barrier, 1, device_id=(col, other, (chip + k) % n), device_id_type=mesh_id
        )
        pl.semaphore_signal(
            barrier, 1, device_id=((chip + k) % n, other, chip), device_id_type=mesh_id
        )
    for nb in (nxt, prv):
        pl.semaphore_signal(barrier, 1, device_id=(nb, core, col), device_id_type=mesh_id)
    pl.semaphore_signal(barrier, 1, device_id=(chip, other, col), device_id_type=mesh_id)
    n_part, part_width = w_hbm.shape[0], w_hbm.shape[2]
    w_loads, w_swaps = [], []
    for j in range(n_part):
        w_cols = pl.ds(j * part_width, part_width)
        w_loads.append(pltpu.make_async_copy(w_hbm.at[j], w_own.at[:, w_cols], wsem.at[0, j]))
        w_loads[-1].start()
    pl.semaphore_wait(barrier, 4 * n + 3 - 2 * diag.astype(jnp.int32))
    src_load.wait()
    for j in range(n_part):
        w_cols = pl.ds(j * part_width, part_width)
        w_swaps.append(
            pltpu.make_async_remote_copy(
                src_ref=w_hbm.at[j], dst_ref=w_other.at[:, w_cols], send_sem=wsem.at[1, j],
                recv_sem=wsem.at[2, j], device_id=(chip, other, col), device_id_type=mesh_id,
            )
        )
        w_swaps[-1].start()

    slot = (chip + core) % n
    tail_rows = src_ref.at[pl.ds(rows - tail, tail)]
    tcopies, pcopies = [], []
    for k in range(n):
        dev = (col, core, (chip + k) % n)
        copy = pltpu.make_async_remote_copy(
            src_ref=src_ref, dst_ref=tok_buf.at[chip], send_sem=tsend.at[k],
            recv_sem=trecv.at[chip], device_id=dev, device_id_type=mesh_id,
        )
        if k == 0:
            own = pltpu.make_async_copy(src_ref, tok_buf.at[chip], trecv.at[chip])

            @pl.when(diag)
            def _():
                own.start()

            @pl.when(jnp.logical_not(diag))
            def _():
                copy.start()
        else:
            copy.start()
        tcopies.append(copy)
    for k in range(n):
        pcopy = pltpu.make_async_remote_copy(
            src_ref=tail_rows, dst_ref=prior_buf.at[slot], send_sem=psend.at[k],
            recv_sem=precv.at[slot], device_id=(col, other, (chip + k) % n),
            device_id_type=mesh_id,
        )
        pcopy.start()
        pcopies.append(pcopy)

    waited = set()

    def arrive(offset):
        if offset in waited:
            return
        waited.add(offset)
        blk = lookup(cyc, (r + offset) % n)
        pltpu.make_async_copy(src_ref, tok_buf.at[blk], trecv.at[blk]).wait()
        pltpu.make_async_copy(tail_rows, prior_buf.at[blk], precv.at[blk]).wait()

    for j in range(n_part):
        w_loads[j].wait()
        w_swaps[j].wait_recv()
    own_cols = pl.ds(pl.multiple_of(core * half, half), half)
    other_cols = pl.ds(pl.multiple_of((1 - core) * half, half), half)

    def part(blk, cols):
        def proj_rows(ref):
            return jnp.dot(
                ref[blk, :, own_cols], w_own[:, cols], preferred_element_type=jnp.float32
            ) + jnp.dot(ref[blk, :, other_cols], w_other[:, cols], preferred_element_type=jnp.float32)

        return jnp.concatenate([proj_rows(tok_buf), proj_rows(prior_buf)], axis=0)

    copies = [[] for _ in range(n_ring)]
    for s in range(n - 1):
        arrive((n - 1 - s) % n)
        arrive((1 + s) % n)
        for ring in range(n_ring):
            fwd = ring < n_ring // 2
            d, dest = (1, nxt) if fwd else (-1, prv)
            cols = pl.ds(ring * chunk, chunk)
            q = lookup(cyc, (r - d * (1 + s) + 2 * n) % n)
            if s == 0:
                sbuf[ring, 0] = part(q, cols).astype(sbuf.dtype)
            else:
                mine = part(q, cols)
                copies[ring][s - 1].wait_recv()
                sbuf[ring, s] = (rbuf[ring, s - 1].astype(jnp.float32) + mine).astype(sbuf.dtype)
            copy = pltpu.make_async_remote_copy(
                src_ref=sbuf.at[ring, s],
                dst_ref=rbuf.at[ring, s],
                send_sem=send_sem.at[ring, s],
                recv_sem=recv_sem.at[ring, s],
                device_id=(dest, core, col),
                device_id_type=mesh_id,
            )
            copy.start()
            copies[ring].append(copy)
    arrive(0)
    for ring in range(n_ring):
        cols = pl.ds(ring * chunk, chunk)
        mine = part(chip, cols)
        copies[ring][-1].wait_recv()
        total = (rbuf[ring, n - 2].astype(jnp.float32) + mine).astype(jnp.bfloat16)
        total = total.astype(jnp.float32)
        proj[pl.ds(tail, rows), cols] = total[:rows]
        proj[pl.ds(0, tail), cols] = total[rows:]

    @pl.when(jnp.logical_and(chip == 0, core == 0))
    def _():
        proj[0:tail, :] = jnp.zeros((tail, width), jnp.float32)

    taps_load.wait()

    third = width // 3
    mixed = []
    for j in range(3):
        cols = pl.ds(j * third, third)
        mixed.append(
            taps_ref[0, j][None, :] * proj[pl.ds(2, rows), cols]
            + taps_ref[1, j][None, :] * proj[pl.ds(1, rows), cols]
            + taps_ref[2, j][None, :] * proj[pl.ds(0, rows), cols]
        )
    q_ref[...] = mixed[0]
    g_ref[...] = (mixed[1] * mixed[2]).astype(g_ref.dtype)
    for ring in range(n_ring):
        for copy in copies[ring]:
            copy.wait_send()
    for k in range(n):
        if k == 0:
            @pl.when(jnp.logical_not(diag))
            def _():
                tcopies[0].wait_send()
        else:
            tcopies[k].wait_send()
        pcopies[k].wait_send()
    for j in range(n_part):
        w_swaps[j].wait_send()


def project_and_gate(tokens, w_own, taps, n_ring=6, tail=2):
    rows, tok_width = tokens.shape
    n = lax.axis_size("p")
    ext_len = rows + tail
    n_part, half, part_width = w_own.shape
    width = n_part * part_width
    third = width // 3
    vmem = pl.BlockSpec(memory_space=pltpu.VMEM)
    return pl.pallas_call(
        rs_kernel,
        out_shape=(
            jax.ShapeDtypeStruct((rows, third), jnp.float32),
            jax.ShapeDtypeStruct((rows, third), jnp.bfloat16),
        ),
        in_specs=[pl.BlockSpec(memory_space=pl.ANY)] * 3,
        out_specs=(vmem, vmem),
        scratch_shapes=[
            pltpu.VMEM(tokens.shape, tokens.dtype),
            pltpu.VMEM(taps.shape, taps.dtype),
            pltpu.VMEM((n, rows, tok_width), tokens.dtype),
            pltpu.VMEM((n, tail, tok_width), tokens.dtype),
            pltpu.VMEM((half, width), w_own.dtype),
            pltpu.VMEM((half, width), w_own.dtype),
            pltpu.VMEM((n_ring, n - 1, ext_len, width // n_ring), jnp.bfloat16),
            pltpu.VMEM((n_ring, n - 1, ext_len, width // n_ring), jnp.bfloat16),
            pltpu.VMEM((ext_len, width), jnp.float32),
        ]
        + [pltpu.SemaphoreType.DMA((n,))] * 4
        + [pltpu.SemaphoreType.DMA((n_ring, n - 1))] * 2
        + [pltpu.SemaphoreType.DMA((3, n_part)), pltpu.SemaphoreType.DMA((2,))],
        compiler_params=pltpu.CompilerParams(
            collective_id=0, has_side_effects=True, vmem_limit_bytes=67043328
        ),
    )(tokens, w_own, taps)


def tok_kernel(src_ref, out_ref, prior_ref, send_sem, recv_sem, psend_sem, precv_sem):
    n, rows, _ = out_ref.shape
    tail = prior_ref.shape[1]
    chip = lax.axis_index("p")
    core = lax.axis_index("c")
    col = lax.axis_index("ch")
    other = 1 - core
    mesh_id = pl.DeviceIdType.MESH
    diag = chip == col
    src_load = pltpu.make_async_copy(src_hbm, src_ref, lsem.at[0])
    src_load.start()
    taps_load = pltpu.make_async_copy(taps_hbm, taps_ref, lsem.at[1])
    taps_load.start()
    barrier = pltpu.get_barrier_semaphore()
    for k in range(n):
        dest = (col, core, (chip + k) % n)
        srce = ((chip + k) % n, core, chip)
        if k == 0:
            @pl.when(jnp.logical_not(diag))
            def _():
                pl.semaphore_signal(barrier, 1, device_id=dest, device_id_type=mesh_id)
                pl.semaphore_signal(barrier, 1, device_id=srce, device_id_type=mesh_id)
        else:
            pl.semaphore_signal(barrier, 1, device_id=dest, device_id_type=mesh_id)
            pl.semaphore_signal(barrier, 1, device_id=srce, device_id_type=mesh_id)
        pl.semaphore_signal(
            barrier, 1, device_id=(col, other, (chip + k) % n), device_id_type=mesh_id
        )
        pl.semaphore_signal(
            barrier, 1, device_id=((chip + k) % n, other, chip), device_id_type=mesh_id
        )
    pl.semaphore_wait(barrier, 4 * n - 2 * diag.astype(jnp.int32))
    slot = (chip + core) % n
    copies = []
    for k in range(n):
        copy = pltpu.make_async_remote_copy(
            src_ref=src_ref,
            dst_ref=out_ref.at[chip],
            send_sem=send_sem.at[k],
            recv_sem=recv_sem.at[chip],
            device_id=(col, core, (chip + k) % n),
            device_id_type=mesh_id,
        )
        if k == 0:
            own = pltpu.make_async_copy(src_ref, out_ref.at[chip], recv_sem.at[chip])

            @pl.when(diag)
            def _():
                own.start()

            @pl.when(jnp.logical_not(diag))
            def _():
                copy.start()
        else:
            copy.start()
        copies.append(copy)
    pcopies = []
    for k in range(n):
        pcopy = pltpu.make_async_remote_copy(
            src_ref=src_ref.at[pl.ds(rows - tail, tail)],
            dst_ref=prior_ref.at[slot],
            send_sem=psend_sem.at[k],
            recv_sem=precv_sem.at[slot],
            device_id=(col, other, (chip + k) % n),
            device_id_type=mesh_id,
        )
        pcopy.start()
        pcopies.append(pcopy)
    for j in range(n):
        pltpu.make_async_copy(src_ref, out_ref.at[j], recv_sem.at[j]).wait()
        pltpu.make_async_copy(
            src_ref.at[pl.ds(rows - tail, tail)], prior_ref.at[j], precv_sem.at[j]
        ).wait()
    for k in range(n):
        if k == 0:
            @pl.when(jnp.logical_not(diag))
            def _():
                copies[0].wait_send()
        else:
            copies[k].wait_send()
        pcopies[k].wait_send()


def spread_tokens(tokens, n, tail=2):
    rows, width = tokens.shape
    vmem = pl.BlockSpec(memory_space=pltpu.VMEM)
    return pl.pallas_call(
        tok_kernel,
        out_shape=(
            jax.ShapeDtypeStruct((n, rows, width), tokens.dtype),
            jax.ShapeDtypeStruct((n, tail, width), tokens.dtype),
        ),
        in_specs=[vmem],
        out_specs=(vmem, vmem),
        scratch_shapes=[pltpu.SemaphoreType.DMA((n,))] * 4,
        compiler_params=pltpu.CompilerParams(collective_id=1, has_side_effects=True),
    )(tokens)


def state_kernel(src_ref, lam_ref, out_ref, got, fac, send_sem, recv_sem, block_len):
    n = got.shape[0]
    n_core = lax.axis_size("c")
    me = lax.axis_index("p") * n_core + lax.axis_index("c")
    col = lax.axis_index("ch")
    mesh_id = pl.DeviceIdType.MESH
    barrier = pltpu.get_barrier_semaphore()
    for k in range(1, n):
        other = (me + k) % n
        pl.semaphore_signal(
            barrier, 1, device_id=(other // n_core, other % n_core, col), device_id_type=mesh_id
        )
    for j in range(n):
        @pl.when(j >= me)
        def _():
            got[j] = jnp.zeros(got.shape[1:], got.dtype)

        gap = jnp.maximum(me - 1 - j, 0).astype(jnp.float32)
        fac[j] = jnp.exp(-lam_ref[...] * (block_len * gap))
    pl.semaphore_wait(barrier, n - 1)
    copies = []
    for k in range(1, n):
        other = me + k
        copy = pltpu.make_async_remote_copy(
            src_ref=src_ref,
            dst_ref=got.at[me],
            send_sem=send_sem.at[k],
            recv_sem=recv_sem.at[me],
            device_id=(other // n_core, other % n_core, col),
            device_id_type=mesh_id,
        )

        @pl.when(other < n)
        def _():
            copy.start()

        copies.append((other, copy))
    for j in range(n):
        @pl.when(j < me)
        def _():
            pltpu.make_async_copy(src_ref, got.at[j], recv_sem.at[j]).wait()
    acc = jnp.zeros(out_ref.shape, jnp.float32)
    for j in range(n):
        acc = acc + fac[j] * got[j]
    out_ref[...] = acc
    for other, copy in copies:
        @pl.when(other < n)
        def _():
            copy.wait_send()


def gather_earlier(state, lam, n, block_len):
    vmem = pl.BlockSpec(memory_space=pltpu.VMEM)
    return pl.pallas_call(
        functools.partial(state_kernel, block_len=float(block_len)),
        out_shape=jax.ShapeDtypeStruct(state.shape, state.dtype),
        in_specs=[vmem, vmem],
        out_specs=vmem,
        scratch_shapes=[
            pltpu.VMEM((n,) + state.shape, state.dtype),
            pltpu.VMEM((n,) + state.shape, jnp.float32),
            pltpu.SemaphoreType.DMA((n,)),
            pltpu.SemaphoreType.DMA((n,)),
        ],
        compiler_params=pltpu.CompilerParams(collective_id=2, has_side_effects=True),
    )(state, lam)


def local(tokens, w_in, short_filter, decay_rate, residue, skip):
    n_chip = lax.axis_size("p")
    block_len = tokens.shape[0]
    local_width = w_in.shape[2]
    group_count = local_width // GROUP
    chip = lax.axis_index("p")
    core = lax.axis_index("c")
    col = lax.axis_index("ch")

    n_col = lax.axis_size("ch")
    w_parts = jnp.transpose(w_in, (1, 0, 2))
    query, gated = project_and_gate(tokens, w_parts, short_filter)
    x = gated.reshape(block_len, group_count, GROUP)

    pole_weight = residue * jnp.sqrt(2.0 * decay_rate)
    pos = jnp.arange(block_len, dtype=jnp.float32)
    lam = decay_rate[:, None, :]
    a_mat = pole_weight[:, None, :] * jnp.exp(-lam * pos[None, :, None])
    b_mat = jnp.exp(lam * pos[None, :, None])
    toep = jnp.einsum("gtr,gsr->gts", a_mat, b_mat, precision=lax.Precision.HIGH)
    causal = pos[:, None] >= pos[None, :]
    toep = jnp.where(causal[None], toep, 0.0)
    near = dot_split("gts,sgc->tgc", toep, x)

    e_mat = jnp.exp(-lam * (block_len - 1 - pos)[None, :, None])
    s_loc = dot_split("gsr,sgc->grc", e_mat, x)
    n_ctx = n_chip * lax.axis_size("c")
    me = chip * lax.axis_size("c") + core
    s_flat = s_loc.reshape(group_count, -1)
    lam_b = jnp.broadcast_to(decay_rate[..., None], decay_rate.shape + (GROUP,))
    s_in = gather_earlier(s_flat, lam_b.reshape(group_count, -1), n_ctx, block_len)
    s_in = s_in.reshape(s_loc.shape)
    f_mat = pole_weight[:, None, :] * jnp.exp(-lam * (pos + 1.0)[None, :, None])
    far = jnp.einsum("gtr,grc->tgc", f_mat, s_in, precision=HIGH)
    long_out = (near + far).reshape(block_len, local_width)
    out = query * (long_out + skip * gated.astype(jnp.float32))
    return out.astype(jnp.bfloat16)


def solution(mesh):
    n_ctx, n_ch = mesh.devices.shape
    sub = Mesh(mesh.devices.reshape(n_ctx // 2, 2, n_ch), ("p", "c", "ch"))
    ctx = ("p", "c")
    return jax.shard_map(
        local,
        mesh=sub,
        in_specs=(
            P(ctx, "ch"),
            P(ctx, None, "ch"),
            P(None, None, "ch"),
            P("ch", None),
            P("ch", None),
            P("ch"),
        ),
        out_specs=P(ctx, "ch"),
        check_vma=False,
    )
```

```python
import functools

import jax
import jax.numpy as jnp
from jax import lax
from jax.experimental import pallas as pl
from jax.experimental.pallas import tpu as pltpu
from jax.sharding import Mesh
from jax.sharding import PartitionSpec as P

GROUP = 16
HIGH = lax.Precision.HIGHEST


def split_bf16(x):
    hi = x.astype(jnp.bfloat16)
    lo = (x - hi.astype(jnp.float32)).astype(jnp.bfloat16)
    return hi, lo


def dot_split(spec, weight, data):
    hi, lo = split_bf16(weight)
    return jnp.einsum(spec, hi, data, preferred_element_type=jnp.float32) + jnp.einsum(
        spec, lo, data, preferred_element_type=jnp.float32
    )


CYCLES = (
    (0, 1, 3, 2, 4, 5, 7, 6),
    (0, 1, 3, 5, 7, 6, 4, 2),
    (0, 1, 7, 5, 3, 2, 4, 6),
    (0, 1, 7, 6, 4, 5, 3, 2),
    (0, 2, 3, 1, 7, 5, 4, 6),
    (0, 2, 4, 5, 3, 1, 7, 6),
)


def lookup(table, v):
    n = len(table)
    total = 0
    for k, t in enumerate(table):
        if t:
            total = total + t * (1 - ((v - k + n) % n + n - 1) // n)
    return total


def ring_chip(r, n):
    hi = r // (n // 2)
    return 2 * (r + hi * (n - 1 - 2 * r)) + hi


def ring_pos(p, n):
    z, y = p // 2, p % 2
    return z + y * (n - 1 - 2 * z)


def rs_kernel(
    src_hbm, w_hbm, taps_hbm, q_ref, g_ref,
    src_ref, taps_ref, tok_buf, prior_buf, w_own, w_other, sbuf, rbuf, proj,
    tsend, trecv, psend, precv, send_sem, recv_sem, wsem, lsem,
):
    n, rows, _ = tok_buf.shape
    tail = prior_buf.shape[1]
    ext_len = rows + tail
    half, width = w_own.shape
    n_ring = sbuf.shape[0]
    chunk = width // n_ring
    chip = lax.axis_index("p")
    core = lax.axis_index("c")
    col = lax.axis_index("ch")
    other = 1 - core
    mesh_id = pl.DeviceIdType.MESH
    diag = chip == col
    cyc = CYCLES[0]
    r = lookup([cyc.index(p) for p in range(n)], chip)
    nxt = lookup(cyc, (r + 1) % n)
    prv = lookup(cyc, (r + n - 1) % n)

    src_load = pltpu.make_async_copy(src_hbm, src_ref, lsem.at[0])
    src_load.start()
    taps_load = pltpu.make_async_copy(taps_hbm, taps_ref, lsem.at[1])
    taps_load.start()
    barrier = pltpu.get_barrier_semaphore()
    for k in range(n):
        dest = (col, core, (chip + k) % n)
        srce = ((chip + k) % n, core, chip)
        if k == 0:
            @pl.when(jnp.logical_not(diag))
            def _():
                pl.semaphore_signal(barrier, 1, device_id=dest, device_id_type=mesh_id)
                pl.semaphore_signal(barrier, 1, device_id=srce, device_id_type=mesh_id)
        else:
            pl.semaphore_signal(barrier, 1, device_id=dest, device_id_type=mesh_id)
            pl.semaphore_signal(barrier, 1, device_id=srce, device_id_type=mesh_id)
        pl.semaphore_signal(
            barrier, 1, device_id=(col, other, (chip + k) % n), device_id_type=mesh_id
        )
        pl.semaphore_signal(
            barrier, 1, device_id=((chip + k) % n, other, chip), device_id_type=mesh_id
        )
    for nb in (nxt, prv):
        pl.semaphore_signal(barrier, 1, device_id=(nb, core, col), device_id_type=mesh_id)
    pl.semaphore_signal(barrier, 1, device_id=(chip, other, col), device_id_type=mesh_id)
    n_part, part_width = w_hbm.shape[0], w_hbm.shape[2]
    w_loads, w_swaps = [], []
    for j in range(n_part):
        w_cols = pl.ds(j * part_width, part_width)
        w_loads.append(pltpu.make_async_copy(w_hbm.at[j], w_own.at[:, w_cols], wsem.at[0, j]))
        w_loads[-1].start()
    pl.semaphore_wait(barrier, 4 * n + 3 - 2 * diag.astype(jnp.int32))
    src_load.wait()
    for j in range(n_part):
        w_cols = pl.ds(j * part_width, part_width)
        w_swaps.append(
            pltpu.make_async_remote_copy(
                src_ref=w_hbm.at[j], dst_ref=w_other.at[:, w_cols], send_sem=wsem.at[1, j],
                recv_sem=wsem.at[2, j], device_id=(chip, other, col), device_id_type=mesh_id,
            )
        )
        w_swaps[-1].start()

    slot = (chip + core) % n
    tail_rows = src_ref.at[pl.ds(rows - tail, tail)]
    tcopies, pcopies = [], []
    for k in range(n):
        pcopy = pltpu.make_async_remote_copy(
            src_ref=tail_rows, dst_ref=prior_buf.at[slot], send_sem=psend.at[k],
            recv_sem=precv.at[slot], device_id=(col, other, (chip + k) % n),
            device_id_type=mesh_id,
        )
        pcopy.start()
        pcopies.append(pcopy)
    for k in range(n):
        dev = (col, core, (chip + k) % n)
        copy = pltpu.make_async_remote_copy(
            src_ref=src_ref, dst_ref=tok_buf.at[chip], send_sem=tsend.at[k],
            recv_sem=trecv.at[chip], device_id=dev, device_id_type=mesh_id,
        )
        if k == 0:
            own = pltpu.make_async_copy(src_ref, tok_buf.at[chip], trecv.at[chip])

            @pl.when(diag)
            def _():
                own.start()

            @pl.when(jnp.logical_not(diag))
            def _():
                copy.start()
        else:
            copy.start()
        tcopies.append(copy)

    waited = set()

    def arrive(offset):
        if offset in waited:
            return
        waited.add(offset)
        blk = lookup(cyc, (r + offset) % n)
        pltpu.make_async_copy(src_ref, tok_buf.at[blk], trecv.at[blk]).wait()
        pltpu.make_async_copy(tail_rows, prior_buf.at[blk], precv.at[blk]).wait()

    for j in range(n_part):
        w_loads[j].wait()
        w_swaps[j].wait_recv()
    own_cols = pl.ds(pl.multiple_of(core * half, half), half)
    other_cols = pl.ds(pl.multiple_of((1 - core) * half, half), half)

    def part(blk, cols):
        def proj_rows(ref):
            return jnp.dot(
                ref[blk, :, own_cols], w_own[:, cols], preferred_element_type=jnp.float32
            ) + jnp.dot(ref[blk, :, other_cols], w_other[:, cols], preferred_element_type=jnp.float32)

        return jnp.concatenate([proj_rows(tok_buf), proj_rows(prior_buf)], axis=0)

    copies = [[] for _ in range(n_ring)]
    for s in range(n - 1):
        arrive((n - 1 - s) % n)
        arrive((1 + s) % n)
        for ring in range(n_ring):
            fwd = ring < n_ring // 2
            d, dest = (1, nxt) if fwd else (-1, prv)
            cols = pl.ds(ring * chunk, chunk)
            q = lookup(cyc, (r - d * (1 + s) + 2 * n) % n)
            if s == 0:
                sbuf[ring, 0] = part(q, cols).astype(sbuf.dtype)
            else:
                mine = part(q, cols)
                copies[ring][s - 1].wait_recv()
                sbuf[ring, s] = (rbuf[ring, s - 1].astype(jnp.float32) + mine).astype(sbuf.dtype)
            copy = pltpu.make_async_remote_copy(
                src_ref=sbuf.at[ring, s],
                dst_ref=rbuf.at[ring, s],
                send_sem=send_sem.at[ring, s],
                recv_sem=recv_sem.at[ring, s],
                device_id=(dest, core, col),
                device_id_type=mesh_id,
            )
            copy.start()
            copies[ring].append(copy)
    arrive(0)
    for ring in range(n_ring):
        cols = pl.ds(ring * chunk, chunk)
        mine = part(chip, cols)
        copies[ring][-1].wait_recv()
        total = (rbuf[ring, n - 2].astype(jnp.float32) + mine).astype(jnp.bfloat16)
        total = total.astype(jnp.float32)
        proj[pl.ds(tail, rows), cols] = total[:rows]
        proj[pl.ds(0, tail), cols] = total[rows:]

    @pl.when(jnp.logical_and(chip == 0, core == 0))
    def _():
        proj[0:tail, :] = jnp.zeros((tail, width), jnp.float32)

    taps_load.wait()

    third = width // 3
    mixed = []
    for j in range(3):
        cols = pl.ds(j * third, third)
        mixed.append(
            taps_ref[0, j][None, :] * proj[pl.ds(2, rows), cols]
            + taps_ref[1, j][None, :] * proj[pl.ds(1, rows), cols]
            + taps_ref[2, j][None, :] * proj[pl.ds(0, rows), cols]
        )
    q_ref[...] = mixed[0]
    g_ref[...] = (mixed[1] * mixed[2]).astype(g_ref.dtype)
    for ring in range(n_ring):
        for copy in copies[ring]:
            copy.wait_send()
    for k in range(n):
        if k == 0:
            @pl.when(jnp.logical_not(diag))
            def _():
                tcopies[0].wait_send()
        else:
            tcopies[k].wait_send()
        pcopies[k].wait_send()
    for j in range(n_part):
        w_swaps[j].wait_send()


def project_and_gate(tokens, w_own, taps, n_ring=6, tail=2):
    rows, tok_width = tokens.shape
    n = lax.axis_size("p")
    ext_len = rows + tail
    n_part, half, part_width = w_own.shape
    width = n_part * part_width
    third = width // 3
    vmem = pl.BlockSpec(memory_space=pltpu.VMEM)
    return pl.pallas_call(
        rs_kernel,
        out_shape=(
            jax.ShapeDtypeStruct((rows, third), jnp.float32),
            jax.ShapeDtypeStruct((rows, third), jnp.bfloat16),
        ),
        in_specs=[pl.BlockSpec(memory_space=pl.ANY)] * 3,
        out_specs=(vmem, vmem),
        scratch_shapes=[
            pltpu.VMEM(tokens.shape, tokens.dtype),
            pltpu.VMEM(taps.shape, taps.dtype),
            pltpu.VMEM((n, rows, tok_width), tokens.dtype),
            pltpu.VMEM((n, tail, tok_width), tokens.dtype),
            pltpu.VMEM((half, width), w_own.dtype),
            pltpu.VMEM((half, width), w_own.dtype),
            pltpu.VMEM((n_ring, n - 1, ext_len, width // n_ring), jnp.bfloat16),
            pltpu.VMEM((n_ring, n - 1, ext_len, width // n_ring), jnp.bfloat16),
            pltpu.VMEM((ext_len, width), jnp.float32),
        ]
        + [pltpu.SemaphoreType.DMA((n,))] * 4
        + [pltpu.SemaphoreType.DMA((n_ring, n - 1))] * 2
        + [pltpu.SemaphoreType.DMA((3, n_part)), pltpu.SemaphoreType.DMA((2,))],
        compiler_params=pltpu.CompilerParams(
            collective_id=0, has_side_effects=True, vmem_limit_bytes=67043328
        ),
    )(tokens, w_own, taps)


def tok_kernel(src_ref, out_ref, prior_ref, send_sem, recv_sem, psend_sem, precv_sem):
    n, rows, _ = out_ref.shape
    tail = prior_ref.shape[1]
    chip = lax.axis_index("p")
    core = lax.axis_index("c")
    col = lax.axis_index("ch")
    other = 1 - core
    mesh_id = pl.DeviceIdType.MESH
    diag = chip == col
    src_load = pltpu.make_async_copy(src_hbm, src_ref, lsem.at[0])
    src_load.start()
    taps_load = pltpu.make_async_copy(taps_hbm, taps_ref, lsem.at[1])
    taps_load.start()
    barrier = pltpu.get_barrier_semaphore()
    for k in range(n):
        dest = (col, core, (chip + k) % n)
        srce = ((chip + k) % n, core, chip)
        if k == 0:
            @pl.when(jnp.logical_not(diag))
            def _():
                pl.semaphore_signal(barrier, 1, device_id=dest, device_id_type=mesh_id)
                pl.semaphore_signal(barrier, 1, device_id=srce, device_id_type=mesh_id)
        else:
            pl.semaphore_signal(barrier, 1, device_id=dest, device_id_type=mesh_id)
            pl.semaphore_signal(barrier, 1, device_id=srce, device_id_type=mesh_id)
        pl.semaphore_signal(
            barrier, 1, device_id=(col, other, (chip + k) % n), device_id_type=mesh_id
        )
        pl.semaphore_signal(
            barrier, 1, device_id=((chip + k) % n, other, chip), device_id_type=mesh_id
        )
    pl.semaphore_wait(barrier, 4 * n - 2 * diag.astype(jnp.int32))
    slot = (chip + core) % n
    copies = []
    for k in range(n):
        copy = pltpu.make_async_remote_copy(
            src_ref=src_ref,
            dst_ref=out_ref.at[chip],
            send_sem=send_sem.at[k],
            recv_sem=recv_sem.at[chip],
            device_id=(col, core, (chip + k) % n),
            device_id_type=mesh_id,
        )
        if k == 0:
            own = pltpu.make_async_copy(src_ref, out_ref.at[chip], recv_sem.at[chip])

            @pl.when(diag)
            def _():
                own.start()

            @pl.when(jnp.logical_not(diag))
            def _():
                copy.start()
        else:
            copy.start()
        copies.append(copy)
    pcopies = []
    for k in range(n):
        pcopy = pltpu.make_async_remote_copy(
            src_ref=src_ref.at[pl.ds(rows - tail, tail)],
            dst_ref=prior_ref.at[slot],
            send_sem=psend_sem.at[k],
            recv_sem=precv_sem.at[slot],
            device_id=(col, other, (chip + k) % n),
            device_id_type=mesh_id,
        )
        pcopy.start()
        pcopies.append(pcopy)
    for j in range(n):
        pltpu.make_async_copy(src_ref, out_ref.at[j], recv_sem.at[j]).wait()
        pltpu.make_async_copy(
            src_ref.at[pl.ds(rows - tail, tail)], prior_ref.at[j], precv_sem.at[j]
        ).wait()
    for k in range(n):
        if k == 0:
            @pl.when(jnp.logical_not(diag))
            def _():
                copies[0].wait_send()
        else:
            copies[k].wait_send()
        pcopies[k].wait_send()


def spread_tokens(tokens, n, tail=2):
    rows, width = tokens.shape
    vmem = pl.BlockSpec(memory_space=pltpu.VMEM)
    return pl.pallas_call(
        tok_kernel,
        out_shape=(
            jax.ShapeDtypeStruct((n, rows, width), tokens.dtype),
            jax.ShapeDtypeStruct((n, tail, width), tokens.dtype),
        ),
        in_specs=[vmem],
        out_specs=(vmem, vmem),
        scratch_shapes=[pltpu.SemaphoreType.DMA((n,))] * 4,
        compiler_params=pltpu.CompilerParams(collective_id=1, has_side_effects=True),
    )(tokens)


def state_kernel(src_ref, lam_ref, out_ref, got, fac, send_sem, recv_sem, block_len):
    n = got.shape[0]
    n_core = lax.axis_size("c")
    me = lax.axis_index("p") * n_core + lax.axis_index("c")
    col = lax.axis_index("ch")
    mesh_id = pl.DeviceIdType.MESH
    barrier = pltpu.get_barrier_semaphore()
    for k in range(1, n):
        other = (me + k) % n
        pl.semaphore_signal(
            barrier, 1, device_id=(other // n_core, other % n_core, col), device_id_type=mesh_id
        )
    for j in range(n):
        @pl.when(j >= me)
        def _():
            got[j] = jnp.zeros(got.shape[1:], got.dtype)

        gap = jnp.maximum(me - 1 - j, 0).astype(jnp.float32)
        fac[j] = jnp.exp(-lam_ref[...] * (block_len * gap))
    pl.semaphore_wait(barrier, n - 1)
    copies = []
    for k in range(1, n):
        other = me + k
        copy = pltpu.make_async_remote_copy(
            src_ref=src_ref,
            dst_ref=got.at[me],
            send_sem=send_sem.at[k],
            recv_sem=recv_sem.at[me],
            device_id=(other // n_core, other % n_core, col),
            device_id_type=mesh_id,
        )

        @pl.when(other < n)
        def _():
            copy.start()

        copies.append((other, copy))
    for j in range(n):
        @pl.when(j < me)
        def _():
            pltpu.make_async_copy(src_ref, got.at[j], recv_sem.at[j]).wait()
    acc = jnp.zeros(out_ref.shape, jnp.float32)
    for j in range(n):
        acc = acc + fac[j] * got[j]
    out_ref[...] = acc
    for other, copy in copies:
        @pl.when(other < n)
        def _():
            copy.wait_send()


def gather_earlier(state, lam, n, block_len):
    vmem = pl.BlockSpec(memory_space=pltpu.VMEM)
    return pl.pallas_call(
        functools.partial(state_kernel, block_len=float(block_len)),
        out_shape=jax.ShapeDtypeStruct(state.shape, state.dtype),
        in_specs=[vmem, vmem],
        out_specs=vmem,
        scratch_shapes=[
            pltpu.VMEM((n,) + state.shape, state.dtype),
            pltpu.VMEM((n,) + state.shape, jnp.float32),
            pltpu.SemaphoreType.DMA((n,)),
            pltpu.SemaphoreType.DMA((n,)),
        ],
        compiler_params=pltpu.CompilerParams(collective_id=2, has_side_effects=True),
    )(state, lam)


def local(tokens, w_in, short_filter, decay_rate, residue, skip):
    n_chip = lax.axis_size("p")
    block_len = tokens.shape[0]
    local_width = w_in.shape[2]
    group_count = local_width // GROUP
    chip = lax.axis_index("p")
    core = lax.axis_index("c")
    col = lax.axis_index("ch")

    n_col = lax.axis_size("ch")
    w_parts = jnp.transpose(w_in, (1, 0, 2))
    query, gated = project_and_gate(tokens, w_parts, short_filter)
    x = gated.reshape(block_len, group_count, GROUP)

    pole_weight = residue * jnp.sqrt(2.0 * decay_rate)
    pos = jnp.arange(block_len, dtype=jnp.float32)
    lam = decay_rate[:, None, :]
    a_mat = pole_weight[:, None, :] * jnp.exp(-lam * pos[None, :, None])
    b_mat = jnp.exp(lam * pos[None, :, None])
    toep = jnp.einsum("gtr,gsr->gts", a_mat, b_mat, precision=lax.Precision.HIGH)
    causal = pos[:, None] >= pos[None, :]
    toep = jnp.where(causal[None], toep, 0.0)
    near = dot_split("gts,sgc->tgc", toep, x)

    e_mat = jnp.exp(-lam * (block_len - 1 - pos)[None, :, None])
    s_loc = dot_split("gsr,sgc->grc", e_mat, x)
    n_ctx = n_chip * lax.axis_size("c")
    me = chip * lax.axis_size("c") + core
    s_flat = s_loc.reshape(group_count, -1)
    lam_b = jnp.broadcast_to(decay_rate[..., None], decay_rate.shape + (GROUP,))
    s_in = gather_earlier(s_flat, lam_b.reshape(group_count, -1), n_ctx, block_len)
    s_in = s_in.reshape(s_loc.shape)
    f_mat = pole_weight[:, None, :] * jnp.exp(-lam * (pos + 1.0)[None, :, None])
    far = jnp.einsum("gtr,grc->tgc", f_mat, s_in, precision=HIGH)
    long_out = (near + far).reshape(block_len, local_width)
    out = query * (long_out + skip * gated.astype(jnp.float32))
    return out.astype(jnp.bfloat16)


def solution(mesh):
    n_ctx, n_ch = mesh.devices.shape
    sub = Mesh(mesh.devices.reshape(n_ctx // 2, 2, n_ch), ("p", "c", "ch"))
    ctx = ("p", "c")
    return jax.shard_map(
        local,
        mesh=sub,
        in_specs=(
            P(ctx, "ch"),
            P(ctx, None, "ch"),
            P(None, None, "ch"),
            P("ch", None),
            P("ch", None),
            P("ch"),
        ),
        out_specs=P(ctx, "ch"),
        check_vma=False,
    )
```

```python
import functools

import jax
import jax.numpy as jnp
from jax import lax
from jax.experimental import pallas as pl
from jax.experimental.pallas import tpu as pltpu
from jax.sharding import Mesh
from jax.sharding import PartitionSpec as P

GROUP = 16
HIGH = lax.Precision.HIGHEST


def split_bf16(x):
    hi = x.astype(jnp.bfloat16)
    lo = (x - hi.astype(jnp.float32)).astype(jnp.bfloat16)
    return hi, lo


def dot_split(spec, weight, data):
    hi, lo = split_bf16(weight)
    return jnp.einsum(spec, hi, data, preferred_element_type=jnp.float32) + jnp.einsum(
        spec, lo, data, preferred_element_type=jnp.float32
    )


CYCLES = (
    (0, 1, 3, 2, 4, 5, 7, 6),
    (0, 1, 3, 5, 7, 6, 4, 2),
    (0, 1, 7, 5, 3, 2, 4, 6),
    (0, 1, 7, 6, 4, 5, 3, 2),
    (0, 2, 3, 1, 7, 5, 4, 6),
    (0, 2, 4, 5, 3, 1, 7, 6),
)


def lookup(table, v):
    n = len(table)
    total = 0
    for k, t in enumerate(table):
        if t:
            total = total + t * (1 - ((v - k + n) % n + n - 1) // n)
    return total


def ring_chip(r, n):
    hi = r // (n // 2)
    return 2 * (r + hi * (n - 1 - 2 * r)) + hi


def ring_pos(p, n):
    z, y = p // 2, p % 2
    return z + y * (n - 1 - 2 * z)


def rs_kernel(
    src_hbm, w_hbm, taps_hbm, q_ref, g_ref,
    src_ref, taps_ref, tok_buf, prior_buf, w_own, w_other, sbuf, rbuf, proj,
    tsend, trecv, psend, precv, send_sem, recv_sem, wsem, lsem,
):
    n, rows, _ = tok_buf.shape
    tail = prior_buf.shape[1]
    ext_len = rows + tail
    half, width = w_own.shape
    n_ring = sbuf.shape[0]
    chunk = width // n_ring
    chip = lax.axis_index("p")
    core = lax.axis_index("c")
    col = lax.axis_index("ch")
    other = 1 - core
    mesh_id = pl.DeviceIdType.MESH
    diag = chip == col
    cyc = CYCLES[0]
    r = lookup([cyc.index(p) for p in range(n)], chip)
    nxt = lookup(cyc, (r + 1) % n)
    prv = lookup(cyc, (r + n - 1) % n)

    src_load = pltpu.make_async_copy(src_hbm, src_ref, lsem.at[0])
    src_load.start()
    taps_load = pltpu.make_async_copy(taps_hbm, taps_ref, lsem.at[1])
    taps_load.start()
    barrier = pltpu.get_barrier_semaphore()
    for k in range(n):
        dest = (col, core, (chip + k) % n)
        srce = ((chip + k) % n, core, chip)
        if k == 0:
            @pl.when(jnp.logical_not(diag))
            def _():
                pl.semaphore_signal(barrier, 1, device_id=dest, device_id_type=mesh_id)
                pl.semaphore_signal(barrier, 1, device_id=srce, device_id_type=mesh_id)
        else:
            pl.semaphore_signal(barrier, 1, device_id=dest, device_id_type=mesh_id)
            pl.semaphore_signal(barrier, 1, device_id=srce, device_id_type=mesh_id)
        pl.semaphore_signal(
            barrier, 1, device_id=(col, other, (chip + k) % n), device_id_type=mesh_id
        )
        pl.semaphore_signal(
            barrier, 1, device_id=((chip + k) % n, other, chip), device_id_type=mesh_id
        )
    for nb in (nxt, prv):
        pl.semaphore_signal(barrier, 1, device_id=(nb, core, col), device_id_type=mesh_id)
    pl.semaphore_signal(barrier, 1, device_id=(chip, other, col), device_id_type=mesh_id)
    n_part, part_width = w_hbm.shape[0], w_hbm.shape[2]
    w_loads, w_swaps = [], []
    for j in range(n_part):
        w_cols = pl.ds(j * part_width, part_width)
        w_loads.append(pltpu.make_async_copy(w_hbm.at[j], w_own.at[:, w_cols], wsem.at[0, j]))
        w_loads[-1].start()
    pl.semaphore_wait(barrier, 4 * n + 3 - 2 * diag.astype(jnp.int32))
    src_load.wait()
    slot = (chip + core) % n
    tail_rows = src_ref.at[pl.ds(rows - tail, tail)]
    tcopies, pcopies = [], []
    for k in range(n):
        pcopy = pltpu.make_async_remote_copy(
            src_ref=tail_rows, dst_ref=prior_buf.at[slot], send_sem=psend.at[k],
            recv_sem=precv.at[slot], device_id=(col, other, (chip + k) % n),
            device_id_type=mesh_id,
        )
        pcopy.start()
        pcopies.append(pcopy)
    for k in range(n):
        dev = (col, core, (chip + k) % n)
        copy = pltpu.make_async_remote_copy(
            src_ref=src_ref, dst_ref=tok_buf.at[chip], send_sem=tsend.at[k],
            recv_sem=trecv.at[chip], device_id=dev, device_id_type=mesh_id,
        )
        if k == 0:
            own = pltpu.make_async_copy(src_ref, tok_buf.at[chip], trecv.at[chip])

            @pl.when(diag)
            def _():
                own.start()

            @pl.when(jnp.logical_not(diag))
            def _():
                copy.start()
        else:
            copy.start()
        tcopies.append(copy)

    for j in range(n_part):
        w_cols = pl.ds(j * part_width, part_width)
        w_swaps.append(
            pltpu.make_async_remote_copy(
                src_ref=w_hbm.at[j], dst_ref=w_other.at[:, w_cols], send_sem=wsem.at[1, j],
                recv_sem=wsem.at[2, j], device_id=(chip, other, col), device_id_type=mesh_id,
            )
        )
        w_swaps[-1].start()

    waited = set()

    def arrive(offset):
        if offset in waited:
            return
        waited.add(offset)
        blk = lookup(cyc, (r + offset) % n)
        pltpu.make_async_copy(src_ref, tok_buf.at[blk], trecv.at[blk]).wait()
        pltpu.make_async_copy(tail_rows, prior_buf.at[blk], precv.at[blk]).wait()

    for j in range(n_part):
        w_loads[j].wait()
        w_swaps[j].wait_recv()
    own_cols = pl.ds(pl.multiple_of(core * half, half), half)
    other_cols = pl.ds(pl.multiple_of((1 - core) * half, half), half)

    def part(blk, cols):
        def proj_rows(ref):
            return jnp.dot(
                ref[blk, :, own_cols], w_own[:, cols], preferred_element_type=jnp.float32
            ) + jnp.dot(ref[blk, :, other_cols], w_other[:, cols], preferred_element_type=jnp.float32)

        return jnp.concatenate([proj_rows(tok_buf), proj_rows(prior_buf)], axis=0)

    copies = [[] for _ in range(n_ring)]
    for s in range(n - 1):
        arrive((n - 1 - s) % n)
        arrive((1 + s) % n)
        for ring in range(n_ring):
            fwd = ring < n_ring // 2
            d, dest = (1, nxt) if fwd else (-1, prv)
            cols = pl.ds(ring * chunk, chunk)
            q = lookup(cyc, (r - d * (1 + s) + 2 * n) % n)
            if s == 0:
                sbuf[ring, 0] = part(q, cols).astype(sbuf.dtype)
            else:
                mine = part(q, cols)
                copies[ring][s - 1].wait_recv()
                sbuf[ring, s] = (rbuf[ring, s - 1].astype(jnp.float32) + mine).astype(sbuf.dtype)
            copy = pltpu.make_async_remote_copy(
                src_ref=sbuf.at[ring, s],
                dst_ref=rbuf.at[ring, s],
                send_sem=send_sem.at[ring, s],
                recv_sem=recv_sem.at[ring, s],
                device_id=(dest, core, col),
                device_id_type=mesh_id,
            )
            copy.start()
            copies[ring].append(copy)
    arrive(0)
    for ring in range(n_ring):
        cols = pl.ds(ring * chunk, chunk)
        mine = part(chip, cols)
        copies[ring][-1].wait_recv()
        total = (rbuf[ring, n - 2].astype(jnp.float32) + mine).astype(jnp.bfloat16)
        total = total.astype(jnp.float32)
        proj[pl.ds(tail, rows), cols] = total[:rows]
        proj[pl.ds(0, tail), cols] = total[rows:]

    @pl.when(jnp.logical_and(chip == 0, core == 0))
    def _():
        proj[0:tail, :] = jnp.zeros((tail, width), jnp.float32)

    taps_load.wait()

    third = width // 3
    mixed = []
    for j in range(3):
        cols = pl.ds(j * third, third)
        mixed.append(
            taps_ref[0, j][None, :] * proj[pl.ds(2, rows), cols]
            + taps_ref[1, j][None, :] * proj[pl.ds(1, rows), cols]
            + taps_ref[2, j][None, :] * proj[pl.ds(0, rows), cols]
        )
    q_ref[...] = mixed[0]
    g_ref[...] = (mixed[1] * mixed[2]).astype(g_ref.dtype)
    for ring in range(n_ring):
        for copy in copies[ring]:
            copy.wait_send()
    for k in range(n):
        if k == 0:
            @pl.when(jnp.logical_not(diag))
            def _():
                tcopies[0].wait_send()
        else:
            tcopies[k].wait_send()
        pcopies[k].wait_send()
    for j in range(n_part):
        w_swaps[j].wait_send()


def project_and_gate(tokens, w_own, taps, n_ring=6, tail=2):
    rows, tok_width = tokens.shape
    n = lax.axis_size("p")
    ext_len = rows + tail
    n_part, half, part_width = w_own.shape
    width = n_part * part_width
    third = width // 3
    vmem = pl.BlockSpec(memory_space=pltpu.VMEM)
    return pl.pallas_call(
        rs_kernel,
        out_shape=(
            jax.ShapeDtypeStruct((rows, third), jnp.float32),
            jax.ShapeDtypeStruct((rows, third), jnp.bfloat16),
        ),
        in_specs=[pl.BlockSpec(memory_space=pl.ANY)] * 3,
        out_specs=(vmem, vmem),
        scratch_shapes=[
            pltpu.VMEM(tokens.shape, tokens.dtype),
            pltpu.VMEM(taps.shape, taps.dtype),
            pltpu.VMEM((n, rows, tok_width), tokens.dtype),
            pltpu.VMEM((n, tail, tok_width), tokens.dtype),
            pltpu.VMEM((half, width), w_own.dtype),
            pltpu.VMEM((half, width), w_own.dtype),
            pltpu.VMEM((n_ring, n - 1, ext_len, width // n_ring), jnp.bfloat16),
            pltpu.VMEM((n_ring, n - 1, ext_len, width // n_ring), jnp.bfloat16),
            pltpu.VMEM((ext_len, width), jnp.float32),
        ]
        + [pltpu.SemaphoreType.DMA((n,))] * 4
        + [pltpu.SemaphoreType.DMA((n_ring, n - 1))] * 2
        + [pltpu.SemaphoreType.DMA((3, n_part)), pltpu.SemaphoreType.DMA((2,))],
        compiler_params=pltpu.CompilerParams(
            collective_id=0, has_side_effects=True, vmem_limit_bytes=67043328
        ),
    )(tokens, w_own, taps)


def tok_kernel(src_ref, out_ref, prior_ref, send_sem, recv_sem, psend_sem, precv_sem):
    n, rows, _ = out_ref.shape
    tail = prior_ref.shape[1]
    chip = lax.axis_index("p")
    core = lax.axis_index("c")
    col = lax.axis_index("ch")
    other = 1 - core
    mesh_id = pl.DeviceIdType.MESH
    diag = chip == col
    src_load = pltpu.make_async_copy(src_hbm, src_ref, lsem.at[0])
    src_load.start()
    taps_load = pltpu.make_async_copy(taps_hbm, taps_ref, lsem.at[1])
    taps_load.start()
    barrier = pltpu.get_barrier_semaphore()
    for k in range(n):
        dest = (col, core, (chip + k) % n)
        srce = ((chip + k) % n, core, chip)
        if k == 0:
            @pl.when(jnp.logical_not(diag))
            def _():
                pl.semaphore_signal(barrier, 1, device_id=dest, device_id_type=mesh_id)
                pl.semaphore_signal(barrier, 1, device_id=srce, device_id_type=mesh_id)
        else:
            pl.semaphore_signal(barrier, 1, device_id=dest, device_id_type=mesh_id)
            pl.semaphore_signal(barrier, 1, device_id=srce, device_id_type=mesh_id)
        pl.semaphore_signal(
            barrier, 1, device_id=(col, other, (chip + k) % n), device_id_type=mesh_id
        )
        pl.semaphore_signal(
            barrier, 1, device_id=((chip + k) % n, other, chip), device_id_type=mesh_id
        )
    pl.semaphore_wait(barrier, 4 * n - 2 * diag.astype(jnp.int32))
    slot = (chip + core) % n
    copies = []
    for k in range(n):
        copy = pltpu.make_async_remote_copy(
            src_ref=src_ref,
            dst_ref=out_ref.at[chip],
            send_sem=send_sem.at[k],
            recv_sem=recv_sem.at[chip],
            device_id=(col, core, (chip + k) % n),
            device_id_type=mesh_id,
        )
        if k == 0:
            own = pltpu.make_async_copy(src_ref, out_ref.at[chip], recv_sem.at[chip])

            @pl.when(diag)
            def _():
                own.start()

            @pl.when(jnp.logical_not(diag))
            def _():
                copy.start()
        else:
            copy.start()
        copies.append(copy)
    pcopies = []
    for k in range(n):
        pcopy = pltpu.make_async_remote_copy(
            src_ref=src_ref.at[pl.ds(rows - tail, tail)],
            dst_ref=prior_ref.at[slot],
            send_sem=psend_sem.at[k],
            recv_sem=precv_sem.at[slot],
            device_id=(col, other, (chip + k) % n),
            device_id_type=mesh_id,
        )
        pcopy.start()
        pcopies.append(pcopy)
    for j in range(n):
        pltpu.make_async_copy(src_ref, out_ref.at[j], recv_sem.at[j]).wait()
        pltpu.make_async_copy(
            src_ref.at[pl.ds(rows - tail, tail)], prior_ref.at[j], precv_sem.at[j]
        ).wait()
    for k in range(n):
        if k == 0:
            @pl.when(jnp.logical_not(diag))
            def _():
                copies[0].wait_send()
        else:
            copies[k].wait_send()
        pcopies[k].wait_send()


def spread_tokens(tokens, n, tail=2):
    rows, width = tokens.shape
    vmem = pl.BlockSpec(memory_space=pltpu.VMEM)
    return pl.pallas_call(
        tok_kernel,
        out_shape=(
            jax.ShapeDtypeStruct((n, rows, width), tokens.dtype),
            jax.ShapeDtypeStruct((n, tail, width), tokens.dtype),
        ),
        in_specs=[vmem],
        out_specs=(vmem, vmem),
        scratch_shapes=[pltpu.SemaphoreType.DMA((n,))] * 4,
        compiler_params=pltpu.CompilerParams(collective_id=1, has_side_effects=True),
    )(tokens)


def state_kernel(src_ref, lam_ref, out_ref, got, fac, send_sem, recv_sem, block_len):
    n = got.shape[0]
    n_core = lax.axis_size("c")
    me = lax.axis_index("p") * n_core + lax.axis_index("c")
    col = lax.axis_index("ch")
    mesh_id = pl.DeviceIdType.MESH
    barrier = pltpu.get_barrier_semaphore()
    for k in range(1, n):
        other = (me + k) % n
        pl.semaphore_signal(
            barrier, 1, device_id=(other // n_core, other % n_core, col), device_id_type=mesh_id
        )
    for j in range(n):
        @pl.when(j >= me)
        def _():
            got[j] = jnp.zeros(got.shape[1:], got.dtype)

        gap = jnp.maximum(me - 1 - j, 0).astype(jnp.float32)
        fac[j] = jnp.exp(-lam_ref[...] * (block_len * gap))
    pl.semaphore_wait(barrier, n - 1)
    copies = []
    for k in range(1, n):
        other = me + k
        copy = pltpu.make_async_remote_copy(
            src_ref=src_ref,
            dst_ref=got.at[me],
            send_sem=send_sem.at[k],
            recv_sem=recv_sem.at[me],
            device_id=(other // n_core, other % n_core, col),
            device_id_type=mesh_id,
        )

        @pl.when(other < n)
        def _():
            copy.start()

        copies.append((other, copy))
    for j in range(n):
        @pl.when(j < me)
        def _():
            pltpu.make_async_copy(src_ref, got.at[j], recv_sem.at[j]).wait()
    acc = jnp.zeros(out_ref.shape, jnp.float32)
    for j in range(n):
        acc = acc + fac[j] * got[j]
    out_ref[...] = acc
    for other, copy in copies:
        @pl.when(other < n)
        def _():
            copy.wait_send()


def gather_earlier(state, lam, n, block_len):
    vmem = pl.BlockSpec(memory_space=pltpu.VMEM)
    return pl.pallas_call(
        functools.partial(state_kernel, block_len=float(block_len)),
        out_shape=jax.ShapeDtypeStruct(state.shape, state.dtype),
        in_specs=[vmem, vmem],
        out_specs=vmem,
        scratch_shapes=[
            pltpu.VMEM((n,) + state.shape, state.dtype),
            pltpu.VMEM((n,) + state.shape, jnp.float32),
            pltpu.SemaphoreType.DMA((n,)),
            pltpu.SemaphoreType.DMA((n,)),
        ],
        compiler_params=pltpu.CompilerParams(collective_id=2, has_side_effects=True),
    )(state, lam)


def local(tokens, w_in, short_filter, decay_rate, residue, skip):
    n_chip = lax.axis_size("p")
    block_len = tokens.shape[0]
    local_width = w_in.shape[2]
    group_count = local_width // GROUP
    chip = lax.axis_index("p")
    core = lax.axis_index("c")
    col = lax.axis_index("ch")

    n_col = lax.axis_size("ch")
    w_parts = jnp.transpose(w_in, (1, 0, 2))
    query, gated = project_and_gate(tokens, w_parts, short_filter)
    x = gated.reshape(block_len, group_count, GROUP)

    pole_weight = residue * jnp.sqrt(2.0 * decay_rate)
    pos = jnp.arange(block_len, dtype=jnp.float32)
    lam = decay_rate[:, None, :]
    a_mat = pole_weight[:, None, :] * jnp.exp(-lam * pos[None, :, None])
    b_mat = jnp.exp(lam * pos[None, :, None])
    toep = jnp.einsum("gtr,gsr->gts", a_mat, b_mat, precision=lax.Precision.HIGH)
    causal = pos[:, None] >= pos[None, :]
    toep = jnp.where(causal[None], toep, 0.0)
    near = dot_split("gts,sgc->tgc", toep, x)

    e_mat = jnp.exp(-lam * (block_len - 1 - pos)[None, :, None])
    s_loc = dot_split("gsr,sgc->grc", e_mat, x)
    n_ctx = n_chip * lax.axis_size("c")
    me = chip * lax.axis_size("c") + core
    s_flat = s_loc.reshape(group_count, -1)
    lam_b = jnp.broadcast_to(decay_rate[..., None], decay_rate.shape + (GROUP,))
    s_in = gather_earlier(s_flat, lam_b.reshape(group_count, -1), n_ctx, block_len)
    s_in = s_in.reshape(s_loc.shape)
    f_mat = pole_weight[:, None, :] * jnp.exp(-lam * (pos + 1.0)[None, :, None])
    far = jnp.einsum("gtr,grc->tgc", f_mat, s_in, precision=HIGH)
    long_out = (near + far).reshape(block_len, local_width)
    out = query * (long_out + skip * gated.astype(jnp.float32))
    return out.astype(jnp.bfloat16)


def solution(mesh):
    n_ctx, n_ch = mesh.devices.shape
    sub = Mesh(mesh.devices.reshape(n_ctx // 2, 2, n_ch), ("p", "c", "ch"))
    ctx = ("p", "c")
    return jax.shard_map(
        local,
        mesh=sub,
        in_specs=(
            P(ctx, "ch"),
            P(ctx, None, "ch"),
            P(None, None, "ch"),
            P("ch", None),
            P("ch", None),
            P("ch"),
        ),
        out_specs=P(ctx, "ch"),
        check_vma=False,
    )
```

```python
import functools

import jax
import jax.numpy as jnp
from jax import lax
from jax.experimental import pallas as pl
from jax.experimental.pallas import tpu as pltpu
from jax.sharding import Mesh
from jax.sharding import PartitionSpec as P

GROUP = 16
HIGH = lax.Precision.HIGHEST


def split_bf16(x):
    hi = x.astype(jnp.bfloat16)
    lo = (x - hi.astype(jnp.float32)).astype(jnp.bfloat16)
    return hi, lo


def dot_split(spec, weight, data):
    hi, lo = split_bf16(weight)
    return jnp.einsum(spec, hi, data, preferred_element_type=jnp.float32) + jnp.einsum(
        spec, lo, data, preferred_element_type=jnp.float32
    )


CYCLES = (
    (0, 1, 3, 2, 4, 5, 7, 6),
    (0, 1, 3, 5, 7, 6, 4, 2),
    (0, 1, 7, 5, 3, 2, 4, 6),
    (0, 1, 7, 6, 4, 5, 3, 2),
    (0, 2, 3, 1, 7, 5, 4, 6),
    (0, 2, 4, 5, 3, 1, 7, 6),
)


def lookup(table, v):
    n = len(table)
    total = 0
    for k, t in enumerate(table):
        if t:
            total = total + t * (1 - ((v - k + n) % n + n - 1) // n)
    return total


def ring_chip(r, n):
    hi = r // (n // 2)
    return 2 * (r + hi * (n - 1 - 2 * r)) + hi


def ring_pos(p, n):
    z, y = p // 2, p % 2
    return z + y * (n - 1 - 2 * z)


def rs_kernel(
    src_hbm, w_hbm, taps_hbm, q_ref, g_ref,
    src_ref, taps_ref, tok_buf, prior_buf, w_own, w_other, sbuf, rbuf, proj,
    tsend, trecv, psend, precv, send_sem, recv_sem, wsem, lsem,
):
    n, rows, _ = tok_buf.shape
    tail = prior_buf.shape[1]
    ext_len = rows + tail
    half, width = w_own.shape
    n_ring = sbuf.shape[0]
    chunk = width // n_ring
    chip = lax.axis_index("p")
    core = lax.axis_index("c")
    col = lax.axis_index("ch")
    other = 1 - core
    mesh_id = pl.DeviceIdType.MESH
    diag = chip == col
    cyc = CYCLES[0]
    r = lookup([cyc.index(p) for p in range(n)], chip)
    nxt = lookup(cyc, (r + 1) % n)
    prv = lookup(cyc, (r + n - 1) % n)

    src_load = pltpu.make_async_copy(src_hbm, src_ref, lsem.at[0])
    src_load.start()
    taps_load = pltpu.make_async_copy(taps_hbm, taps_ref, lsem.at[1])
    taps_load.start()
    barrier = pltpu.get_barrier_semaphore()
    for k in range(n):
        dest = (col, core, (chip + k) % n)
        srce = ((chip + k) % n, core, chip)
        if k == 0:
            @pl.when(jnp.logical_not(diag))
            def _():
                pl.semaphore_signal(barrier, 1, device_id=dest, device_id_type=mesh_id)
                pl.semaphore_signal(barrier, 1, device_id=srce, device_id_type=mesh_id)
        else:
            pl.semaphore_signal(barrier, 1, device_id=dest, device_id_type=mesh_id)
            pl.semaphore_signal(barrier, 1, device_id=srce, device_id_type=mesh_id)
        pl.semaphore_signal(
            barrier, 1, device_id=(col, other, (chip + k) % n), device_id_type=mesh_id
        )
        pl.semaphore_signal(
            barrier, 1, device_id=((chip + k) % n, other, chip), device_id_type=mesh_id
        )
    for nb in (nxt, prv):
        pl.semaphore_signal(barrier, 1, device_id=(nb, core, col), device_id_type=mesh_id)
    pl.semaphore_signal(barrier, 1, device_id=(chip, other, col), device_id_type=mesh_id)
    n_part, part_width = w_hbm.shape[0], w_hbm.shape[2]
    w_loads, w_swaps = [], []
    for j in range(n_part):
        w_cols = pl.ds(j * part_width, part_width)
        w_loads.append(pltpu.make_async_copy(w_hbm.at[j], w_own.at[:, w_cols], wsem.at[0, j]))
        w_loads[-1].start()
    pl.semaphore_wait(barrier, 4 * n + 3 - 2 * diag.astype(jnp.int32))
    src_load.wait()
    slot = (chip + core) % n
    tail_rows = src_ref.at[pl.ds(rows - tail, tail)]
    tcopies, pcopies = [], []
    for k in range(n):
        pcopy = pltpu.make_async_remote_copy(
            src_ref=tail_rows, dst_ref=prior_buf.at[slot], send_sem=psend.at[k],
            recv_sem=precv.at[slot], device_id=(col, other, (chip + k) % n),
            device_id_type=mesh_id,
        )
        pcopy.start()
        pcopies.append(pcopy)
    n_x = n // 2
    far_first = [(dy, dx) for dy in (1, 0) for dx in (2, 1, 3, 0)]
    for k, (dy, dx) in enumerate(far_first):
        dev = (col, core, ((col // n_x + dy) % 2) * n_x + (col % n_x + dx) % n_x)
        copy = pltpu.make_async_remote_copy(
            src_ref=src_ref, dst_ref=tok_buf.at[chip], send_sem=tsend.at[k],
            recv_sem=trecv.at[chip], device_id=dev, device_id_type=mesh_id,
        )
        if k == n - 1:
            own = pltpu.make_async_copy(src_ref, tok_buf.at[chip], trecv.at[chip])

            @pl.when(diag)
            def _():
                own.start()

            @pl.when(jnp.logical_not(diag))
            def _():
                copy.start()
        else:
            copy.start()
        tcopies.append(copy)

    for j in range(n_part):
        w_cols = pl.ds(j * part_width, part_width)
        w_swaps.append(
            pltpu.make_async_remote_copy(
                src_ref=w_hbm.at[j], dst_ref=w_other.at[:, w_cols], send_sem=wsem.at[1, j],
                recv_sem=wsem.at[2, j], device_id=(chip, other, col), device_id_type=mesh_id,
            )
        )
        w_swaps[-1].start()

    waited = set()

    def arrive(offset):
        if offset in waited:
            return
        waited.add(offset)
        blk = lookup(cyc, (r + offset) % n)
        pltpu.make_async_copy(src_ref, tok_buf.at[blk], trecv.at[blk]).wait()
        pltpu.make_async_copy(tail_rows, prior_buf.at[blk], precv.at[blk]).wait()

    for j in range(n_part):
        w_loads[j].wait()
        w_swaps[j].wait_recv()
    own_cols = pl.ds(pl.multiple_of(core * half, half), half)
    other_cols = pl.ds(pl.multiple_of((1 - core) * half, half), half)

    def part(blk, cols):
        def proj_rows(ref):
            return jnp.dot(
                ref[blk, :, own_cols], w_own[:, cols], preferred_element_type=jnp.float32
            ) + jnp.dot(ref[blk, :, other_cols], w_other[:, cols], preferred_element_type=jnp.float32)

        return jnp.concatenate([proj_rows(tok_buf), proj_rows(prior_buf)], axis=0)

    copies = [[] for _ in range(n_ring)]
    for s in range(n - 1):
        arrive((n - 1 - s) % n)
        arrive((1 + s) % n)
        for ring in range(n_ring):
            fwd = ring < n_ring // 2
            d, dest = (1, nxt) if fwd else (-1, prv)
            cols = pl.ds(ring * chunk, chunk)
            q = lookup(cyc, (r - d * (1 + s) + 2 * n) % n)
            if s == 0:
                sbuf[ring, 0] = part(q, cols).astype(sbuf.dtype)
            else:
                mine = part(q, cols)
                copies[ring][s - 1].wait_recv()
                sbuf[ring, s] = (rbuf[ring, s - 1].astype(jnp.float32) + mine).astype(sbuf.dtype)
            copy = pltpu.make_async_remote_copy(
                src_ref=sbuf.at[ring, s],
                dst_ref=rbuf.at[ring, s],
                send_sem=send_sem.at[ring, s],
                recv_sem=recv_sem.at[ring, s],
                device_id=(dest, core, col),
                device_id_type=mesh_id,
            )
            copy.start()
            copies[ring].append(copy)
    arrive(0)
    for ring in range(n_ring):
        cols = pl.ds(ring * chunk, chunk)
        mine = part(chip, cols)
        copies[ring][-1].wait_recv()
        total = (rbuf[ring, n - 2].astype(jnp.float32) + mine).astype(jnp.bfloat16)
        total = total.astype(jnp.float32)
        proj[pl.ds(tail, rows), cols] = total[:rows]
        proj[pl.ds(0, tail), cols] = total[rows:]

    @pl.when(jnp.logical_and(chip == 0, core == 0))
    def _():
        proj[0:tail, :] = jnp.zeros((tail, width), jnp.float32)

    taps_load.wait()

    third = width // 3
    mixed = []
    for j in range(3):
        cols = pl.ds(j * third, third)
        mixed.append(
            taps_ref[0, j][None, :] * proj[pl.ds(2, rows), cols]
            + taps_ref[1, j][None, :] * proj[pl.ds(1, rows), cols]
            + taps_ref[2, j][None, :] * proj[pl.ds(0, rows), cols]
        )
    q_ref[...] = mixed[0]
    g_ref[...] = (mixed[1] * mixed[2]).astype(g_ref.dtype)
    for ring in range(n_ring):
        for copy in copies[ring]:
            copy.wait_send()
    for k in range(n):
        if k == n - 1:
            @pl.when(jnp.logical_not(diag))
            def _():
                tcopies[k].wait_send()
        else:
            tcopies[k].wait_send()
        pcopies[k].wait_send()
    for j in range(n_part):
        w_swaps[j].wait_send()


def project_and_gate(tokens, w_own, taps, n_ring=6, tail=2):
    rows, tok_width = tokens.shape
    n = lax.axis_size("p")
    ext_len = rows + tail
    n_part, half, part_width = w_own.shape
    width = n_part * part_width
    third = width // 3
    vmem = pl.BlockSpec(memory_space=pltpu.VMEM)
    return pl.pallas_call(
        rs_kernel,
        out_shape=(
            jax.ShapeDtypeStruct((rows, third), jnp.float32),
            jax.ShapeDtypeStruct((rows, third), jnp.bfloat16),
        ),
        in_specs=[pl.BlockSpec(memory_space=pl.ANY)] * 3,
        out_specs=(vmem, vmem),
        scratch_shapes=[
            pltpu.VMEM(tokens.shape, tokens.dtype),
            pltpu.VMEM(taps.shape, taps.dtype),
            pltpu.VMEM((n, rows, tok_width), tokens.dtype),
            pltpu.VMEM((n, tail, tok_width), tokens.dtype),
            pltpu.VMEM((half, width), w_own.dtype),
            pltpu.VMEM((half, width), w_own.dtype),
            pltpu.VMEM((n_ring, n - 1, ext_len, width // n_ring), jnp.bfloat16),
            pltpu.VMEM((n_ring, n - 1, ext_len, width // n_ring), jnp.bfloat16),
            pltpu.VMEM((ext_len, width), jnp.float32),
        ]
        + [pltpu.SemaphoreType.DMA((n,))] * 4
        + [pltpu.SemaphoreType.DMA((n_ring, n - 1))] * 2
        + [pltpu.SemaphoreType.DMA((3, n_part)), pltpu.SemaphoreType.DMA((2,))],
        compiler_params=pltpu.CompilerParams(
            collective_id=0, has_side_effects=True, vmem_limit_bytes=67043328
        ),
    )(tokens, w_own, taps)


def tok_kernel(src_ref, out_ref, prior_ref, send_sem, recv_sem, psend_sem, precv_sem):
    n, rows, _ = out_ref.shape
    tail = prior_ref.shape[1]
    chip = lax.axis_index("p")
    core = lax.axis_index("c")
    col = lax.axis_index("ch")
    other = 1 - core
    mesh_id = pl.DeviceIdType.MESH
    diag = chip == col
    src_load = pltpu.make_async_copy(src_hbm, src_ref, lsem.at[0])
    src_load.start()
    taps_load = pltpu.make_async_copy(taps_hbm, taps_ref, lsem.at[1])
    taps_load.start()
    barrier = pltpu.get_barrier_semaphore()
    for k in range(n):
        dest = (col, core, (chip + k) % n)
        srce = ((chip + k) % n, core, chip)
        if k == 0:
            @pl.when(jnp.logical_not(diag))
            def _():
                pl.semaphore_signal(barrier, 1, device_id=dest, device_id_type=mesh_id)
                pl.semaphore_signal(barrier, 1, device_id=srce, device_id_type=mesh_id)
        else:
            pl.semaphore_signal(barrier, 1, device_id=dest, device_id_type=mesh_id)
            pl.semaphore_signal(barrier, 1, device_id=srce, device_id_type=mesh_id)
        pl.semaphore_signal(
            barrier, 1, device_id=(col, other, (chip + k) % n), device_id_type=mesh_id
        )
        pl.semaphore_signal(
            barrier, 1, device_id=((chip + k) % n, other, chip), device_id_type=mesh_id
        )
    pl.semaphore_wait(barrier, 4 * n - 2 * diag.astype(jnp.int32))
    slot = (chip + core) % n
    copies = []
    for k in range(n):
        copy = pltpu.make_async_remote_copy(
            src_ref=src_ref,
            dst_ref=out_ref.at[chip],
            send_sem=send_sem.at[k],
            recv_sem=recv_sem.at[chip],
            device_id=(col, core, (chip + k) % n),
            device_id_type=mesh_id,
        )
        if k == 0:
            own = pltpu.make_async_copy(src_ref, out_ref.at[chip], recv_sem.at[chip])

            @pl.when(diag)
            def _():
                own.start()

            @pl.when(jnp.logical_not(diag))
            def _():
                copy.start()
        else:
            copy.start()
        copies.append(copy)
    pcopies = []
    for k in range(n):
        pcopy = pltpu.make_async_remote_copy(
            src_ref=src_ref.at[pl.ds(rows - tail, tail)],
            dst_ref=prior_ref.at[slot],
            send_sem=psend_sem.at[k],
            recv_sem=precv_sem.at[slot],
            device_id=(col, other, (chip + k) % n),
            device_id_type=mesh_id,
        )
        pcopy.start()
        pcopies.append(pcopy)
    for j in range(n):
        pltpu.make_async_copy(src_ref, out_ref.at[j], recv_sem.at[j]).wait()
        pltpu.make_async_copy(
            src_ref.at[pl.ds(rows - tail, tail)], prior_ref.at[j], precv_sem.at[j]
        ).wait()
    for k in range(n):
        if k == 0:
            @pl.when(jnp.logical_not(diag))
            def _():
                copies[0].wait_send()
        else:
            copies[k].wait_send()
        pcopies[k].wait_send()


def spread_tokens(tokens, n, tail=2):
    rows, width = tokens.shape
    vmem = pl.BlockSpec(memory_space=pltpu.VMEM)
    return pl.pallas_call(
        tok_kernel,
        out_shape=(
            jax.ShapeDtypeStruct((n, rows, width), tokens.dtype),
            jax.ShapeDtypeStruct((n, tail, width), tokens.dtype),
        ),
        in_specs=[vmem],
        out_specs=(vmem, vmem),
        scratch_shapes=[pltpu.SemaphoreType.DMA((n,))] * 4,
        compiler_params=pltpu.CompilerParams(collective_id=1, has_side_effects=True),
    )(tokens)


def state_kernel(src_ref, lam_ref, out_ref, got, fac, send_sem, recv_sem, block_len):
    n = got.shape[0]
    n_core = lax.axis_size("c")
    me = lax.axis_index("p") * n_core + lax.axis_index("c")
    col = lax.axis_index("ch")
    mesh_id = pl.DeviceIdType.MESH
    barrier = pltpu.get_barrier_semaphore()
    for k in range(1, n):
        other = (me + k) % n
        pl.semaphore_signal(
            barrier, 1, device_id=(other // n_core, other % n_core, col), device_id_type=mesh_id
        )
    for j in range(n):
        @pl.when(j >= me)
        def _():
            got[j] = jnp.zeros(got.shape[1:], got.dtype)

        gap = jnp.maximum(me - 1 - j, 0).astype(jnp.float32)
        fac[j] = jnp.exp(-lam_ref[...] * (block_len * gap))
    pl.semaphore_wait(barrier, n - 1)
    copies = []
    for k in range(1, n):
        other = me + k
        copy = pltpu.make_async_remote_copy(
            src_ref=src_ref,
            dst_ref=got.at[me],
            send_sem=send_sem.at[k],
            recv_sem=recv_sem.at[me],
            device_id=(other // n_core, other % n_core, col),
            device_id_type=mesh_id,
        )

        @pl.when(other < n)
        def _():
            copy.start()

        copies.append((other, copy))
    for j in range(n):
        @pl.when(j < me)
        def _():
            pltpu.make_async_copy(src_ref, got.at[j], recv_sem.at[j]).wait()
    acc = jnp.zeros(out_ref.shape, jnp.float32)
    for j in range(n):
        acc = acc + fac[j] * got[j]
    out_ref[...] = acc
    for other, copy in copies:
        @pl.when(other < n)
        def _():
            copy.wait_send()


def gather_earlier(state, lam, n, block_len):
    vmem = pl.BlockSpec(memory_space=pltpu.VMEM)
    return pl.pallas_call(
        functools.partial(state_kernel, block_len=float(block_len)),
        out_shape=jax.ShapeDtypeStruct(state.shape, state.dtype),
        in_specs=[vmem, vmem],
        out_specs=vmem,
        scratch_shapes=[
            pltpu.VMEM((n,) + state.shape, state.dtype),
            pltpu.VMEM((n,) + state.shape, jnp.float32),
            pltpu.SemaphoreType.DMA((n,)),
            pltpu.SemaphoreType.DMA((n,)),
        ],
        compiler_params=pltpu.CompilerParams(collective_id=2, has_side_effects=True),
    )(state, lam)


def local(tokens, w_in, short_filter, decay_rate, residue, skip):
    n_chip = lax.axis_size("p")
    block_len = tokens.shape[0]
    local_width = w_in.shape[2]
    group_count = local_width // GROUP
    chip = lax.axis_index("p")
    core = lax.axis_index("c")
    col = lax.axis_index("ch")

    n_col = lax.axis_size("ch")
    w_parts = jnp.transpose(w_in, (1, 0, 2))
    query, gated = project_and_gate(tokens, w_parts, short_filter)
    x = gated.reshape(block_len, group_count, GROUP)

    pole_weight = residue * jnp.sqrt(2.0 * decay_rate)
    pos = jnp.arange(block_len, dtype=jnp.float32)
    lam = decay_rate[:, None, :]
    a_mat = pole_weight[:, None, :] * jnp.exp(-lam * pos[None, :, None])
    b_mat = jnp.exp(lam * pos[None, :, None])
    toep = jnp.einsum("gtr,gsr->gts", a_mat, b_mat, precision=lax.Precision.HIGH)
    causal = pos[:, None] >= pos[None, :]
    toep = jnp.where(causal[None], toep, 0.0)
    near = dot_split("gts,sgc->tgc", toep, x)

    e_mat = jnp.exp(-lam * (block_len - 1 - pos)[None, :, None])
    s_loc = dot_split("gsr,sgc->grc", e_mat, x)
    n_ctx = n_chip * lax.axis_size("c")
    me = chip * lax.axis_size("c") + core
    s_flat = s_loc.reshape(group_count, -1)
    lam_b = jnp.broadcast_to(decay_rate[..., None], decay_rate.shape + (GROUP,))
    s_in = gather_earlier(s_flat, lam_b.reshape(group_count, -1), n_ctx, block_len)
    s_in = s_in.reshape(s_loc.shape)
    f_mat = pole_weight[:, None, :] * jnp.exp(-lam * (pos + 1.0)[None, :, None])
    far = jnp.einsum("gtr,grc->tgc", f_mat, s_in, precision=HIGH)
    long_out = (near + far).reshape(block_len, local_width)
    out = query * (long_out + skip * gated.astype(jnp.float32))
    return out.astype(jnp.bfloat16)


def solution(mesh):
    n_ctx, n_ch = mesh.devices.shape
    sub = Mesh(mesh.devices.reshape(n_ctx // 2, 2, n_ch), ("p", "c", "ch"))
    ctx = ("p", "c")
    return jax.shard_map(
        local,
        mesh=sub,
        in_specs=(
            P(ctx, "ch"),
            P(ctx, None, "ch"),
            P(None, None, "ch"),
            P("ch", None),
            P("ch", None),
            P("ch"),
        ),
        out_specs=P(ctx, "ch"),
        check_vma=False,
    )
```

```python
import functools

import jax
import jax.numpy as jnp
from jax import lax
from jax.experimental import pallas as pl
from jax.experimental.pallas import tpu as pltpu
from jax.sharding import Mesh
from jax.sharding import PartitionSpec as P

GROUP = 16
HIGH = lax.Precision.HIGHEST


def split_bf16(x):
    hi = x.astype(jnp.bfloat16)
    lo = (x - hi.astype(jnp.float32)).astype(jnp.bfloat16)
    return hi, lo


def dot_split(spec, weight, data):
    hi, lo = split_bf16(weight)
    return jnp.einsum(spec, hi, data, preferred_element_type=jnp.float32) + jnp.einsum(
        spec, lo, data, preferred_element_type=jnp.float32
    )


CYCLES = (
    (0, 1, 3, 2, 4, 5, 7, 6),
    (0, 1, 3, 5, 7, 6, 4, 2),
    (0, 1, 7, 5, 3, 2, 4, 6),
    (0, 1, 7, 6, 4, 5, 3, 2),
    (0, 2, 3, 1, 7, 5, 4, 6),
    (0, 2, 4, 5, 3, 1, 7, 6),
)


def lookup(table, v):
    n = len(table)
    total = 0
    for k, t in enumerate(table):
        if t:
            total = total + t * (1 - ((v - k + n) % n + n - 1) // n)
    return total


def ring_chip(r, n):
    hi = r // (n // 2)
    return 2 * (r + hi * (n - 1 - 2 * r)) + hi


def ring_pos(p, n):
    z, y = p // 2, p % 2
    return z + y * (n - 1 - 2 * z)


def rs_kernel(
    src_hbm, w_hbm, taps_hbm, q_ref, g_ref,
    src_ref, taps_ref, tok_buf, prior_buf, w_own, w_other, sbuf, rbuf, proj,
    tsend, trecv, psend, precv, send_sem, recv_sem, wsem, lsem,
):
    n, rows, _ = tok_buf.shape
    tail = prior_buf.shape[1]
    ext_len = rows + tail
    half, width = w_own.shape
    n_ring = sbuf.shape[0]
    chunk = width // n_ring
    chip = lax.axis_index("p")
    core = lax.axis_index("c")
    col = lax.axis_index("ch")
    other = 1 - core
    mesh_id = pl.DeviceIdType.MESH
    diag = chip == col
    cyc = CYCLES[0]
    r = lookup([cyc.index(p) for p in range(n)], chip)
    nxt = lookup(cyc, (r + 1) % n)
    prv = lookup(cyc, (r + n - 1) % n)

    src_load = pltpu.make_async_copy(src_hbm, src_ref, lsem.at[0])
    src_load.start()
    taps_load = pltpu.make_async_copy(taps_hbm, taps_ref, lsem.at[1])
    taps_load.start()
    barrier = pltpu.get_barrier_semaphore()
    for k in range(n):
        dest = (col, core, (chip + k) % n)
        srce = ((chip + k) % n, core, chip)
        if k == 0:
            @pl.when(jnp.logical_not(diag))
            def _():
                pl.semaphore_signal(barrier, 1, device_id=dest, device_id_type=mesh_id)
                pl.semaphore_signal(barrier, 1, device_id=srce, device_id_type=mesh_id)
        else:
            pl.semaphore_signal(barrier, 1, device_id=dest, device_id_type=mesh_id)
            pl.semaphore_signal(barrier, 1, device_id=srce, device_id_type=mesh_id)
        pl.semaphore_signal(
            barrier, 1, device_id=(col, other, (chip + k) % n), device_id_type=mesh_id
        )
        pl.semaphore_signal(
            barrier, 1, device_id=((chip + k) % n, other, chip), device_id_type=mesh_id
        )
    for nb in (nxt, prv):
        pl.semaphore_signal(barrier, 1, device_id=(nb, core, col), device_id_type=mesh_id)
    pl.semaphore_signal(barrier, 1, device_id=(chip, other, col), device_id_type=mesh_id)
    n_part, part_width = w_hbm.shape[0], w_hbm.shape[2]
    w_loads, w_swaps = [], []
    for j in range(n_part):
        w_cols = pl.ds(j * part_width, part_width)
        w_loads.append(pltpu.make_async_copy(w_hbm.at[j], w_own.at[:, w_cols], wsem.at[0, j]))
        w_loads[-1].start()
    pl.semaphore_wait(barrier, 4 * n + 3 - 2 * diag.astype(jnp.int32))
    src_load.wait()
    slot = (chip + core) % n
    tail_rows = src_ref.at[pl.ds(rows - tail, tail)]
    tcopies, pcopies = [], []
    for k in range(n):
        pcopy = pltpu.make_async_remote_copy(
            src_ref=tail_rows, dst_ref=prior_buf.at[slot], send_sem=psend.at[k],
            recv_sem=precv.at[slot], device_id=(col, other, (chip + k) % n),
            device_id_type=mesh_id,
        )
        pcopy.start()
        pcopies.append(pcopy)
    n_x = n // 2
    near_first = [(dy, dx) for dy in (0, 1) for dx in (0, 1, 3, 2)]
    for k, (dy, dx) in enumerate(near_first):
        dev = (col, core, ((col // n_x + dy) % 2) * n_x + (col % n_x + dx) % n_x)
        copy = pltpu.make_async_remote_copy(
            src_ref=src_ref, dst_ref=tok_buf.at[chip], send_sem=tsend.at[k],
            recv_sem=trecv.at[chip], device_id=dev, device_id_type=mesh_id,
        )
        if k == 0:
            own = pltpu.make_async_copy(src_ref, tok_buf.at[chip], trecv.at[chip])

            @pl.when(diag)
            def _():
                own.start()

            @pl.when(jnp.logical_not(diag))
            def _():
                copy.start()
        else:
            copy.start()
        tcopies.append(copy)

    for j in range(n_part):
        w_cols = pl.ds(j * part_width, part_width)
        w_swaps.append(
            pltpu.make_async_remote_copy(
                src_ref=w_hbm.at[j], dst_ref=w_other.at[:, w_cols], send_sem=wsem.at[1, j],
                recv_sem=wsem.at[2, j], device_id=(chip, other, col), device_id_type=mesh_id,
            )
        )
        w_swaps[-1].start()

    waited = set()

    def arrive(offset):
        if offset in waited:
            return
        waited.add(offset)
        blk = lookup(cyc, (r + offset) % n)
        pltpu.make_async_copy(src_ref, tok_buf.at[blk], trecv.at[blk]).wait()
        pltpu.make_async_copy(tail_rows, prior_buf.at[blk], precv.at[blk]).wait()

    for j in range(n_part):
        w_loads[j].wait()
        w_swaps[j].wait_recv()
    own_cols = pl.ds(pl.multiple_of(core * half, half), half)
    other_cols = pl.ds(pl.multiple_of((1 - core) * half, half), half)

    def part(blk, cols):
        def proj_rows(ref):
            return jnp.dot(
                ref[blk, :, own_cols], w_own[:, cols], preferred_element_type=jnp.float32
            ) + jnp.dot(ref[blk, :, other_cols], w_other[:, cols], preferred_element_type=jnp.float32)

        return jnp.concatenate([proj_rows(tok_buf), proj_rows(prior_buf)], axis=0)

    copies = [[] for _ in range(n_ring)]
    for s in range(n - 1):
        arrive((n - 1 - s) % n)
        arrive((1 + s) % n)
        for ring in range(n_ring):
            fwd = ring < n_ring // 2
            d, dest = (1, nxt) if fwd else (-1, prv)
            cols = pl.ds(ring * chunk, chunk)
            q = lookup(cyc, (r - d * (1 + s) + 2 * n) % n)
            if s == 0:
                sbuf[ring, 0] = part(q, cols).astype(sbuf.dtype)
            else:
                mine = part(q, cols)
                copies[ring][s - 1].wait_recv()
                sbuf[ring, s] = (rbuf[ring, s - 1].astype(jnp.float32) + mine).astype(sbuf.dtype)
            copy = pltpu.make_async_remote_copy(
                src_ref=sbuf.at[ring, s],
                dst_ref=rbuf.at[ring, s],
                send_sem=send_sem.at[ring, s],
                recv_sem=recv_sem.at[ring, s],
                device_id=(dest, core, col),
                device_id_type=mesh_id,
            )
            copy.start()
            copies[ring].append(copy)
    arrive(0)
    for ring in range(n_ring):
        cols = pl.ds(ring * chunk, chunk)
        mine = part(chip, cols)
        copies[ring][-1].wait_recv()
        total = (rbuf[ring, n - 2].astype(jnp.float32) + mine).astype(jnp.bfloat16)
        total = total.astype(jnp.float32)
        proj[pl.ds(tail, rows), cols] = total[:rows]
        proj[pl.ds(0, tail), cols] = total[rows:]

    @pl.when(jnp.logical_and(chip == 0, core == 0))
    def _():
        proj[0:tail, :] = jnp.zeros((tail, width), jnp.float32)

    taps_load.wait()

    third = width // 3
    mixed = []
    for j in range(3):
        cols = pl.ds(j * third, third)
        mixed.append(
            taps_ref[0, j][None, :] * proj[pl.ds(2, rows), cols]
            + taps_ref[1, j][None, :] * proj[pl.ds(1, rows), cols]
            + taps_ref[2, j][None, :] * proj[pl.ds(0, rows), cols]
        )
    q_ref[...] = mixed[0]
    g_ref[...] = (mixed[1] * mixed[2]).astype(g_ref.dtype)
    for ring in range(n_ring):
        for copy in copies[ring]:
            copy.wait_send()
    for k in range(n):
        if k == 0:
            @pl.when(jnp.logical_not(diag))
            def _():
                tcopies[k].wait_send()
        else:
            tcopies[k].wait_send()
        pcopies[k].wait_send()
    for j in range(n_part):
        w_swaps[j].wait_send()


def project_and_gate(tokens, w_own, taps, n_ring=6, tail=2):
    rows, tok_width = tokens.shape
    n = lax.axis_size("p")
    ext_len = rows + tail
    n_part, half, part_width = w_own.shape
    width = n_part * part_width
    third = width // 3
    vmem = pl.BlockSpec(memory_space=pltpu.VMEM)
    return pl.pallas_call(
        rs_kernel,
        out_shape=(
            jax.ShapeDtypeStruct((rows, third), jnp.float32),
            jax.ShapeDtypeStruct((rows, third), jnp.bfloat16),
        ),
        in_specs=[pl.BlockSpec(memory_space=pl.ANY)] * 3,
        out_specs=(vmem, vmem),
        scratch_shapes=[
            pltpu.VMEM(tokens.shape, tokens.dtype),
            pltpu.VMEM(taps.shape, taps.dtype),
            pltpu.VMEM((n, rows, tok_width), tokens.dtype),
            pltpu.VMEM((n, tail, tok_width), tokens.dtype),
            pltpu.VMEM((half, width), w_own.dtype),
            pltpu.VMEM((half, width), w_own.dtype),
            pltpu.VMEM((n_ring, n - 1, ext_len, width // n_ring), jnp.bfloat16),
            pltpu.VMEM((n_ring, n - 1, ext_len, width // n_ring), jnp.bfloat16),
            pltpu.VMEM((ext_len, width), jnp.float32),
        ]
        + [pltpu.SemaphoreType.DMA((n,))] * 4
        + [pltpu.SemaphoreType.DMA((n_ring, n - 1))] * 2
        + [pltpu.SemaphoreType.DMA((3, n_part)), pltpu.SemaphoreType.DMA((2,))],
        compiler_params=pltpu.CompilerParams(
            collective_id=0, has_side_effects=True, vmem_limit_bytes=67043328
        ),
    )(tokens, w_own, taps)


def tok_kernel(src_ref, out_ref, prior_ref, send_sem, recv_sem, psend_sem, precv_sem):
    n, rows, _ = out_ref.shape
    tail = prior_ref.shape[1]
    chip = lax.axis_index("p")
    core = lax.axis_index("c")
    col = lax.axis_index("ch")
    other = 1 - core
    mesh_id = pl.DeviceIdType.MESH
    diag = chip == col
    src_load = pltpu.make_async_copy(src_hbm, src_ref, lsem.at[0])
    src_load.start()
    taps_load = pltpu.make_async_copy(taps_hbm, taps_ref, lsem.at[1])
    taps_load.start()
    barrier = pltpu.get_barrier_semaphore()
    for k in range(n):
        dest = (col, core, (chip + k) % n)
        srce = ((chip + k) % n, core, chip)
        if k == 0:
            @pl.when(jnp.logical_not(diag))
            def _():
                pl.semaphore_signal(barrier, 1, device_id=dest, device_id_type=mesh_id)
                pl.semaphore_signal(barrier, 1, device_id=srce, device_id_type=mesh_id)
        else:
            pl.semaphore_signal(barrier, 1, device_id=dest, device_id_type=mesh_id)
            pl.semaphore_signal(barrier, 1, device_id=srce, device_id_type=mesh_id)
        pl.semaphore_signal(
            barrier, 1, device_id=(col, other, (chip + k) % n), device_id_type=mesh_id
        )
        pl.semaphore_signal(
            barrier, 1, device_id=((chip + k) % n, other, chip), device_id_type=mesh_id
        )
    pl.semaphore_wait(barrier, 4 * n - 2 * diag.astype(jnp.int32))
    slot = (chip + core) % n
    copies = []
    for k in range(n):
        copy = pltpu.make_async_remote_copy(
            src_ref=src_ref,
            dst_ref=out_ref.at[chip],
            send_sem=send_sem.at[k],
            recv_sem=recv_sem.at[chip],
            device_id=(col, core, (chip + k) % n),
            device_id_type=mesh_id,
        )
        if k == 0:
            own = pltpu.make_async_copy(src_ref, out_ref.at[chip], recv_sem.at[chip])

            @pl.when(diag)
            def _():
                own.start()

            @pl.when(jnp.logical_not(diag))
            def _():
                copy.start()
        else:
            copy.start()
        copies.append(copy)
    pcopies = []
    for k in range(n):
        pcopy = pltpu.make_async_remote_copy(
            src_ref=src_ref.at[pl.ds(rows - tail, tail)],
            dst_ref=prior_ref.at[slot],
            send_sem=psend_sem.at[k],
            recv_sem=precv_sem.at[slot],
            device_id=(col, other, (chip + k) % n),
            device_id_type=mesh_id,
        )
        pcopy.start()
        pcopies.append(pcopy)
    for j in range(n):
        pltpu.make_async_copy(src_ref, out_ref.at[j], recv_sem.at[j]).wait()
        pltpu.make_async_copy(
            src_ref.at[pl.ds(rows - tail, tail)], prior_ref.at[j], precv_sem.at[j]
        ).wait()
    for k in range(n):
        if k == 0:
            @pl.when(jnp.logical_not(diag))
            def _():
                copies[0].wait_send()
        else:
            copies[k].wait_send()
        pcopies[k].wait_send()


def spread_tokens(tokens, n, tail=2):
    rows, width = tokens.shape
    vmem = pl.BlockSpec(memory_space=pltpu.VMEM)
    return pl.pallas_call(
        tok_kernel,
        out_shape=(
            jax.ShapeDtypeStruct((n, rows, width), tokens.dtype),
            jax.ShapeDtypeStruct((n, tail, width), tokens.dtype),
        ),
        in_specs=[vmem],
        out_specs=(vmem, vmem),
        scratch_shapes=[pltpu.SemaphoreType.DMA((n,))] * 4,
        compiler_params=pltpu.CompilerParams(collective_id=1, has_side_effects=True),
    )(tokens)


def state_kernel(src_ref, lam_ref, out_ref, got, fac, send_sem, recv_sem, block_len):
    n = got.shape[0]
    n_core = lax.axis_size("c")
    me = lax.axis_index("p") * n_core + lax.axis_index("c")
    col = lax.axis_index("ch")
    mesh_id = pl.DeviceIdType.MESH
    barrier = pltpu.get_barrier_semaphore()
    for k in range(1, n):
        other = (me + k) % n
        pl.semaphore_signal(
            barrier, 1, device_id=(other // n_core, other % n_core, col), device_id_type=mesh_id
        )
    for j in range(n):
        @pl.when(j >= me)
        def _():
            got[j] = jnp.zeros(got.shape[1:], got.dtype)

        gap = jnp.maximum(me - 1 - j, 0).astype(jnp.float32)
        fac[j] = jnp.exp(-lam_ref[...] * (block_len * gap))
    pl.semaphore_wait(barrier, n - 1)
    copies = []
    for k in range(1, n):
        other = me + k
        copy = pltpu.make_async_remote_copy(
            src_ref=src_ref,
            dst_ref=got.at[me],
            send_sem=send_sem.at[k],
            recv_sem=recv_sem.at[me],
            device_id=(other // n_core, other % n_core, col),
            device_id_type=mesh_id,
        )

        @pl.when(other < n)
        def _():
            copy.start()

        copies.append((other, copy))
    for j in range(n):
        @pl.when(j < me)
        def _():
            pltpu.make_async_copy(src_ref, got.at[j], recv_sem.at[j]).wait()
    acc = jnp.zeros(out_ref.shape, jnp.float32)
    for j in range(n):
        acc = acc + fac[j] * got[j]
    out_ref[...] = acc
    for other, copy in copies:
        @pl.when(other < n)
        def _():
            copy.wait_send()


def gather_earlier(state, lam, n, block_len):
    vmem = pl.BlockSpec(memory_space=pltpu.VMEM)
    return pl.pallas_call(
        functools.partial(state_kernel, block_len=float(block_len)),
        out_shape=jax.ShapeDtypeStruct(state.shape, state.dtype),
        in_specs=[vmem, vmem],
        out_specs=vmem,
        scratch_shapes=[
            pltpu.VMEM((n,) + state.shape, state.dtype),
            pltpu.VMEM((n,) + state.shape, jnp.float32),
            pltpu.SemaphoreType.DMA((n,)),
            pltpu.SemaphoreType.DMA((n,)),
        ],
        compiler_params=pltpu.CompilerParams(collective_id=2, has_side_effects=True),
    )(state, lam)


def local(tokens, w_in, short_filter, decay_rate, residue, skip):
    n_chip = lax.axis_size("p")
    block_len = tokens.shape[0]
    local_width = w_in.shape[2]
    group_count = local_width // GROUP
    chip = lax.axis_index("p")
    core = lax.axis_index("c")
    col = lax.axis_index("ch")

    n_col = lax.axis_size("ch")
    w_parts = jnp.transpose(w_in, (1, 0, 2))
    query, gated = project_and_gate(tokens, w_parts, short_filter)
    x = gated.reshape(block_len, group_count, GROUP)

    pole_weight = residue * jnp.sqrt(2.0 * decay_rate)
    pos = jnp.arange(block_len, dtype=jnp.float32)
    lam = decay_rate[:, None, :]
    a_mat = pole_weight[:, None, :] * jnp.exp(-lam * pos[None, :, None])
    b_mat = jnp.exp(lam * pos[None, :, None])
    toep = jnp.einsum("gtr,gsr->gts", a_mat, b_mat, precision=lax.Precision.HIGH)
    causal = pos[:, None] >= pos[None, :]
    toep = jnp.where(causal[None], toep, 0.0)
    near = dot_split("gts,sgc->tgc", toep, x)

    e_mat = jnp.exp(-lam * (block_len - 1 - pos)[None, :, None])
    s_loc = dot_split("gsr,sgc->grc", e_mat, x)
    n_ctx = n_chip * lax.axis_size("c")
    me = chip * lax.axis_size("c") + core
    s_flat = s_loc.reshape(group_count, -1)
    lam_b = jnp.broadcast_to(decay_rate[..., None], decay_rate.shape + (GROUP,))
    s_in = gather_earlier(s_flat, lam_b.reshape(group_count, -1), n_ctx, block_len)
    s_in = s_in.reshape(s_loc.shape)
    f_mat = pole_weight[:, None, :] * jnp.exp(-lam * (pos + 1.0)[None, :, None])
    far = jnp.einsum("gtr,grc->tgc", f_mat, s_in, precision=HIGH)
    long_out = (near + far).reshape(block_len, local_width)
    out = query * (long_out + skip * gated.astype(jnp.float32))
    return out.astype(jnp.bfloat16)


def solution(mesh):
    n_ctx, n_ch = mesh.devices.shape
    sub = Mesh(mesh.devices.reshape(n_ctx // 2, 2, n_ch), ("p", "c", "ch"))
    ctx = ("p", "c")
    return jax.shard_map(
        local,
        mesh=sub,
        in_specs=(
            P(ctx, "ch"),
            P(ctx, None, "ch"),
            P(None, None, "ch"),
            P("ch", None),
            P("ch", None),
            P("ch"),
        ),
        out_specs=P(ctx, "ch"),
        check_vma=False,
    )
```

```python
import functools

import jax
import jax.numpy as jnp
from jax import lax
from jax.experimental import pallas as pl
from jax.experimental.pallas import tpu as pltpu
from jax.sharding import Mesh
from jax.sharding import PartitionSpec as P

GROUP = 16
HIGH = lax.Precision.HIGHEST


def split_bf16(x):
    hi = x.astype(jnp.bfloat16)
    lo = (x - hi.astype(jnp.float32)).astype(jnp.bfloat16)
    return hi, lo


def dot_split(spec, weight, data):
    hi, lo = split_bf16(weight)
    return jnp.einsum(spec, hi, data, preferred_element_type=jnp.float32) + jnp.einsum(
        spec, lo, data, preferred_element_type=jnp.float32
    )


CYCLES = (
    (0, 1, 3, 2, 4, 5, 7, 6),
    (0, 1, 3, 5, 7, 6, 4, 2),
    (0, 1, 7, 5, 3, 2, 4, 6),
    (0, 1, 7, 6, 4, 5, 3, 2),
    (0, 2, 3, 1, 7, 5, 4, 6),
    (0, 2, 4, 5, 3, 1, 7, 6),
)


def lookup(table, v):
    n = len(table)
    total = 0
    for k, t in enumerate(table):
        if t:
            total = total + t * (1 - ((v - k + n) % n + n - 1) // n)
    return total


def ring_chip(r, n):
    hi = r // (n // 2)
    return 2 * (r + hi * (n - 1 - 2 * r)) + hi


def ring_pos(p, n):
    z, y = p // 2, p % 2
    return z + y * (n - 1 - 2 * z)


def rs_kernel(
    src_hbm, w_hbm, taps_hbm, q_ref, g_ref,
    src_ref, taps_ref, tok_buf, prior_buf, w_own, w_other, sbuf, rbuf, proj,
    tsend, trecv, psend, precv, send_sem, recv_sem, wsem, lsem,
):
    n, rows, _ = tok_buf.shape
    tail = prior_buf.shape[1]
    ext_len = rows + tail
    half, width = w_own.shape
    n_ring = sbuf.shape[0]
    chunk = width // n_ring
    chip = lax.axis_index("p")
    core = lax.axis_index("c")
    col = lax.axis_index("ch")
    other = 1 - core
    mesh_id = pl.DeviceIdType.MESH
    diag = chip == col
    cyc = CYCLES[0]
    r = lookup([cyc.index(p) for p in range(n)], chip)
    nxt = lookup(cyc, (r + 1) % n)
    prv = lookup(cyc, (r + n - 1) % n)

    src_load = pltpu.make_async_copy(src_hbm, src_ref, lsem.at[0])
    src_load.start()
    taps_load = pltpu.make_async_copy(taps_hbm, taps_ref, lsem.at[1])
    taps_load.start()
    barrier = pltpu.get_barrier_semaphore()
    for k in range(n):
        dest = (col, core, (chip + k) % n)
        srce = ((chip + k) % n, core, chip)
        if k == 0:
            @pl.when(jnp.logical_not(diag))
            def _():
                pl.semaphore_signal(barrier, 1, device_id=dest, device_id_type=mesh_id)
                pl.semaphore_signal(barrier, 1, device_id=srce, device_id_type=mesh_id)
        else:
            pl.semaphore_signal(barrier, 1, device_id=dest, device_id_type=mesh_id)
            pl.semaphore_signal(barrier, 1, device_id=srce, device_id_type=mesh_id)
        pl.semaphore_signal(
            barrier, 1, device_id=(col, other, (chip + k) % n), device_id_type=mesh_id
        )
        pl.semaphore_signal(
            barrier, 1, device_id=((chip + k) % n, other, chip), device_id_type=mesh_id
        )
    for nb in (nxt, prv):
        pl.semaphore_signal(barrier, 1, device_id=(nb, core, col), device_id_type=mesh_id)
    pl.semaphore_signal(barrier, 1, device_id=(chip, other, col), device_id_type=mesh_id)
    n_part, part_width = w_hbm.shape[0], w_hbm.shape[2]
    w_loads, w_swaps = [], []
    for j in range(n_part):
        w_cols = pl.ds(j * part_width, part_width)
        w_loads.append(pltpu.make_async_copy(w_hbm.at[j], w_own.at[:, w_cols], wsem.at[0, j]))
        w_loads[-1].start()
    pl.semaphore_wait(barrier, 4 * n + 3 - 2 * diag.astype(jnp.int32))
    src_load.wait()
    slot = (chip + core) % n
    tail_rows = src_ref.at[pl.ds(rows - tail, tail)]
    tcopies, pcopies = [], []
    for k in range(n):
        pcopy = pltpu.make_async_remote_copy(
            src_ref=tail_rows, dst_ref=prior_buf.at[slot], send_sem=psend.at[k],
            recv_sem=precv.at[slot], device_id=(col, other, (chip + k) % n),
            device_id_type=mesh_id,
        )
        pcopy.start()
        pcopies.append(pcopy)
    for k in range(n):
        dev = (col, core, (chip + k) % n)
        copy = pltpu.make_async_remote_copy(
            src_ref=src_ref, dst_ref=tok_buf.at[chip], send_sem=tsend.at[k],
            recv_sem=trecv.at[chip], device_id=dev, device_id_type=mesh_id,
        )
        if k == 0:
            own = pltpu.make_async_copy(src_ref, tok_buf.at[chip], trecv.at[chip])

            @pl.when(diag)
            def _():
                own.start()

            @pl.when(jnp.logical_not(diag))
            def _():
                copy.start()
        else:
            copy.start()
        tcopies.append(copy)

    for j in range(n_part):
        w_cols = pl.ds(j * part_width, part_width)
        w_swaps.append(
            pltpu.make_async_remote_copy(
                src_ref=w_hbm.at[j], dst_ref=w_other.at[:, w_cols], send_sem=wsem.at[1, j],
                recv_sem=wsem.at[2, j], device_id=(chip, other, col), device_id_type=mesh_id,
            )
        )
        w_swaps[-1].start()

    waited = set()

    def arrive(offset):
        if offset in waited:
            return
        waited.add(offset)
        blk = lookup(cyc, (r + offset) % n)
        pltpu.make_async_copy(src_ref, tok_buf.at[blk], trecv.at[blk]).wait()
        pltpu.make_async_copy(tail_rows, prior_buf.at[blk], precv.at[blk]).wait()

    for j in range(n_part):
        w_loads[j].wait()
        w_swaps[j].wait_recv()
    own_cols = pl.ds(pl.multiple_of(core * half, half), half)
    other_cols = pl.ds(pl.multiple_of((1 - core) * half, half), half)

    def part(blk, cols):
        def proj_rows(ref):
            return jnp.dot(
                ref[blk, :, own_cols], w_own[:, cols], preferred_element_type=jnp.float32
            ) + jnp.dot(ref[blk, :, other_cols], w_other[:, cols], preferred_element_type=jnp.float32)

        return jnp.concatenate([proj_rows(tok_buf), proj_rows(prior_buf)], axis=0)

    copies = [[] for _ in range(n_ring)]
    order = [h * (n_ring // 2) + k for k in range(n_ring // 2) for h in range(2)]
    for s in range(n - 1):
        arrive((n - 1 - s) % n)
        arrive((1 + s) % n)
        for ring in order:
            fwd = ring < n_ring // 2
            d, dest = (1, nxt) if fwd else (-1, prv)
            cols = pl.ds(ring * chunk, chunk)
            q = lookup(cyc, (r - d * (1 + s) + 2 * n) % n)
            if s == 0:
                sbuf[ring, 0] = part(q, cols).astype(sbuf.dtype)
            else:
                mine = part(q, cols)
                copies[ring][s - 1].wait_recv()
                sbuf[ring, s] = (rbuf[ring, s - 1].astype(jnp.float32) + mine).astype(sbuf.dtype)
            copy = pltpu.make_async_remote_copy(
                src_ref=sbuf.at[ring, s],
                dst_ref=rbuf.at[ring, s],
                send_sem=send_sem.at[ring, s],
                recv_sem=recv_sem.at[ring, s],
                device_id=(dest, core, col),
                device_id_type=mesh_id,
            )
            copy.start()
            copies[ring].append(copy)
    arrive(0)
    for ring in range(n_ring):
        cols = pl.ds(ring * chunk, chunk)
        mine = part(chip, cols)
        copies[ring][-1].wait_recv()
        total = (rbuf[ring, n - 2].astype(jnp.float32) + mine).astype(jnp.bfloat16)
        total = total.astype(jnp.float32)
        proj[pl.ds(tail, rows), cols] = total[:rows]
        proj[pl.ds(0, tail), cols] = total[rows:]

    @pl.when(jnp.logical_and(chip == 0, core == 0))
    def _():
        proj[0:tail, :] = jnp.zeros((tail, width), jnp.float32)

    taps_load.wait()

    third = width // 3
    mixed = []
    for j in range(3):
        cols = pl.ds(j * third, third)
        mixed.append(
            taps_ref[0, j][None, :] * proj[pl.ds(2, rows), cols]
            + taps_ref[1, j][None, :] * proj[pl.ds(1, rows), cols]
            + taps_ref[2, j][None, :] * proj[pl.ds(0, rows), cols]
        )
    q_ref[...] = mixed[0]
    g_ref[...] = (mixed[1] * mixed[2]).astype(g_ref.dtype)
    for ring in range(n_ring):
        for copy in copies[ring]:
            copy.wait_send()
    for k in range(n):
        if k == 0:
            @pl.when(jnp.logical_not(diag))
            def _():
                tcopies[0].wait_send()
        else:
            tcopies[k].wait_send()
        pcopies[k].wait_send()
    for j in range(n_part):
        w_swaps[j].wait_send()


def project_and_gate(tokens, w_own, taps, n_ring=6, tail=2):
    rows, tok_width = tokens.shape
    n = lax.axis_size("p")
    ext_len = rows + tail
    n_part, half, part_width = w_own.shape
    width = n_part * part_width
    third = width // 3
    vmem = pl.BlockSpec(memory_space=pltpu.VMEM)
    return pl.pallas_call(
        rs_kernel,
        out_shape=(
            jax.ShapeDtypeStruct((rows, third), jnp.float32),
            jax.ShapeDtypeStruct((rows, third), jnp.bfloat16),
        ),
        in_specs=[pl.BlockSpec(memory_space=pl.ANY)] * 3,
        out_specs=(vmem, vmem),
        scratch_shapes=[
            pltpu.VMEM(tokens.shape, tokens.dtype),
            pltpu.VMEM(taps.shape, taps.dtype),
            pltpu.VMEM((n, rows, tok_width), tokens.dtype),
            pltpu.VMEM((n, tail, tok_width), tokens.dtype),
            pltpu.VMEM((half, width), w_own.dtype),
            pltpu.VMEM((half, width), w_own.dtype),
            pltpu.VMEM((n_ring, n - 1, ext_len, width // n_ring), jnp.bfloat16),
            pltpu.VMEM((n_ring, n - 1, ext_len, width // n_ring), jnp.bfloat16),
            pltpu.VMEM((ext_len, width), jnp.float32),
        ]
        + [pltpu.SemaphoreType.DMA((n,))] * 4
        + [pltpu.SemaphoreType.DMA((n_ring, n - 1))] * 2
        + [pltpu.SemaphoreType.DMA((3, n_part)), pltpu.SemaphoreType.DMA((2,))],
        compiler_params=pltpu.CompilerParams(
            collective_id=0, has_side_effects=True, vmem_limit_bytes=67043328
        ),
    )(tokens, w_own, taps)


def tok_kernel(src_ref, out_ref, prior_ref, send_sem, recv_sem, psend_sem, precv_sem):
    n, rows, _ = out_ref.shape
    tail = prior_ref.shape[1]
    chip = lax.axis_index("p")
    core = lax.axis_index("c")
    col = lax.axis_index("ch")
    other = 1 - core
    mesh_id = pl.DeviceIdType.MESH
    diag = chip == col
    src_load = pltpu.make_async_copy(src_hbm, src_ref, lsem.at[0])
    src_load.start()
    taps_load = pltpu.make_async_copy(taps_hbm, taps_ref, lsem.at[1])
    taps_load.start()
    barrier = pltpu.get_barrier_semaphore()
    for k in range(n):
        dest = (col, core, (chip + k) % n)
        srce = ((chip + k) % n, core, chip)
        if k == 0:
            @pl.when(jnp.logical_not(diag))
            def _():
                pl.semaphore_signal(barrier, 1, device_id=dest, device_id_type=mesh_id)
                pl.semaphore_signal(barrier, 1, device_id=srce, device_id_type=mesh_id)
        else:
            pl.semaphore_signal(barrier, 1, device_id=dest, device_id_type=mesh_id)
            pl.semaphore_signal(barrier, 1, device_id=srce, device_id_type=mesh_id)
        pl.semaphore_signal(
            barrier, 1, device_id=(col, other, (chip + k) % n), device_id_type=mesh_id
        )
        pl.semaphore_signal(
            barrier, 1, device_id=((chip + k) % n, other, chip), device_id_type=mesh_id
        )
    pl.semaphore_wait(barrier, 4 * n - 2 * diag.astype(jnp.int32))
    slot = (chip + core) % n
    copies = []
    for k in range(n):
        copy = pltpu.make_async_remote_copy(
            src_ref=src_ref,
            dst_ref=out_ref.at[chip],
            send_sem=send_sem.at[k],
            recv_sem=recv_sem.at[chip],
            device_id=(col, core, (chip + k) % n),
            device_id_type=mesh_id,
        )
        if k == 0:
            own = pltpu.make_async_copy(src_ref, out_ref.at[chip], recv_sem.at[chip])

            @pl.when(diag)
            def _():
                own.start()

            @pl.when(jnp.logical_not(diag))
            def _():
                copy.start()
        else:
            copy.start()
        copies.append(copy)
    pcopies = []
    for k in range(n):
        pcopy = pltpu.make_async_remote_copy(
            src_ref=src_ref.at[pl.ds(rows - tail, tail)],
            dst_ref=prior_ref.at[slot],
            send_sem=psend_sem.at[k],
            recv_sem=precv_sem.at[slot],
            device_id=(col, other, (chip + k) % n),
            device_id_type=mesh_id,
        )
        pcopy.start()
        pcopies.append(pcopy)
    for j in range(n):
        pltpu.make_async_copy(src_ref, out_ref.at[j], recv_sem.at[j]).wait()
        pltpu.make_async_copy(
            src_ref.at[pl.ds(rows - tail, tail)], prior_ref.at[j], precv_sem.at[j]
        ).wait()
    for k in range(n):
        if k == 0:
            @pl.when(jnp.logical_not(diag))
            def _():
                copies[0].wait_send()
        else:
            copies[k].wait_send()
        pcopies[k].wait_send()


def spread_tokens(tokens, n, tail=2):
    rows, width = tokens.shape
    vmem = pl.BlockSpec(memory_space=pltpu.VMEM)
    return pl.pallas_call(
        tok_kernel,
        out_shape=(
            jax.ShapeDtypeStruct((n, rows, width), tokens.dtype),
            jax.ShapeDtypeStruct((n, tail, width), tokens.dtype),
        ),
        in_specs=[vmem],
        out_specs=(vmem, vmem),
        scratch_shapes=[pltpu.SemaphoreType.DMA((n,))] * 4,
        compiler_params=pltpu.CompilerParams(collective_id=1, has_side_effects=True),
    )(tokens)


def state_kernel(src_ref, lam_ref, out_ref, got, fac, send_sem, recv_sem, block_len):
    n = got.shape[0]
    n_core = lax.axis_size("c")
    me = lax.axis_index("p") * n_core + lax.axis_index("c")
    col = lax.axis_index("ch")
    mesh_id = pl.DeviceIdType.MESH
    barrier = pltpu.get_barrier_semaphore()
    for k in range(1, n):
        other = (me + k) % n
        pl.semaphore_signal(
            barrier, 1, device_id=(other // n_core, other % n_core, col), device_id_type=mesh_id
        )
    for j in range(n):
        @pl.when(j >= me)
        def _():
            got[j] = jnp.zeros(got.shape[1:], got.dtype)

        gap = jnp.maximum(me - 1 - j, 0).astype(jnp.float32)
        fac[j] = jnp.exp(-lam_ref[...] * (block_len * gap))
    pl.semaphore_wait(barrier, n - 1)
    copies = []
    for k in range(1, n):
        other = me + k
        copy = pltpu.make_async_remote_copy(
            src_ref=src_ref,
            dst_ref=got.at[me],
            send_sem=send_sem.at[k],
            recv_sem=recv_sem.at[me],
            device_id=(other // n_core, other % n_core, col),
            device_id_type=mesh_id,
        )

        @pl.when(other < n)
        def _():
            copy.start()

        copies.append((other, copy))
    for j in range(n):
        @pl.when(j < me)
        def _():
            pltpu.make_async_copy(src_ref, got.at[j], recv_sem.at[j]).wait()
    acc = jnp.zeros(out_ref.shape, jnp.float32)
    for j in range(n):
        acc = acc + fac[j] * got[j]
    out_ref[...] = acc
    for other, copy in copies:
        @pl.when(other < n)
        def _():
            copy.wait_send()


def gather_earlier(state, lam, n, block_len):
    vmem = pl.BlockSpec(memory_space=pltpu.VMEM)
    return pl.pallas_call(
        functools.partial(state_kernel, block_len=float(block_len)),
        out_shape=jax.ShapeDtypeStruct(state.shape, state.dtype),
        in_specs=[vmem, vmem],
        out_specs=vmem,
        scratch_shapes=[
            pltpu.VMEM((n,) + state.shape, state.dtype),
            pltpu.VMEM((n,) + state.shape, jnp.float32),
            pltpu.SemaphoreType.DMA((n,)),
            pltpu.SemaphoreType.DMA((n,)),
        ],
        compiler_params=pltpu.CompilerParams(collective_id=2, has_side_effects=True),
    )(state, lam)


def local(tokens, w_in, short_filter, decay_rate, residue, skip):
    n_chip = lax.axis_size("p")
    block_len = tokens.shape[0]
    local_width = w_in.shape[2]
    group_count = local_width // GROUP
    chip = lax.axis_index("p")
    core = lax.axis_index("c")
    col = lax.axis_index("ch")

    n_col = lax.axis_size("ch")
    w_parts = jnp.transpose(w_in, (1, 0, 2))
    query, gated = project_and_gate(tokens, w_parts, short_filter)
    x = gated.reshape(block_len, group_count, GROUP)

    pole_weight = residue * jnp.sqrt(2.0 * decay_rate)
    pos = jnp.arange(block_len, dtype=jnp.float32)
    lam = decay_rate[:, None, :]
    a_mat = pole_weight[:, None, :] * jnp.exp(-lam * pos[None, :, None])
    b_mat = jnp.exp(lam * pos[None, :, None])
    toep = jnp.einsum("gtr,gsr->gts", a_mat, b_mat, precision=lax.Precision.HIGH)
    causal = pos[:, None] >= pos[None, :]
    toep = jnp.where(causal[None], toep, 0.0)
    near = dot_split("gts,sgc->tgc", toep, x)

    e_mat = jnp.exp(-lam * (block_len - 1 - pos)[None, :, None])
    s_loc = dot_split("gsr,sgc->grc", e_mat, x)
    n_ctx = n_chip * lax.axis_size("c")
    me = chip * lax.axis_size("c") + core
    s_flat = s_loc.reshape(group_count, -1)
    lam_b = jnp.broadcast_to(decay_rate[..., None], decay_rate.shape + (GROUP,))
    s_in = gather_earlier(s_flat, lam_b.reshape(group_count, -1), n_ctx, block_len)
    s_in = s_in.reshape(s_loc.shape)
    f_mat = pole_weight[:, None, :] * jnp.exp(-lam * (pos + 1.0)[None, :, None])
    far = jnp.einsum("gtr,grc->tgc", f_mat, s_in, precision=HIGH)
    long_out = (near + far).reshape(block_len, local_width)
    out = query * (long_out + skip * gated.astype(jnp.float32))
    return out.astype(jnp.bfloat16)


def solution(mesh):
    n_ctx, n_ch = mesh.devices.shape
    sub = Mesh(mesh.devices.reshape(n_ctx // 2, 2, n_ch), ("p", "c", "ch"))
    ctx = ("p", "c")
    return jax.shard_map(
        local,
        mesh=sub,
        in_specs=(
            P(ctx, "ch"),
            P(ctx, None, "ch"),
            P(None, None, "ch"),
            P("ch", None),
            P("ch", None),
            P("ch"),
        ),
        out_specs=P(ctx, "ch"),
        check_vma=False,
    )
```

```python
import functools

import jax
import jax.numpy as jnp
from jax import lax
from jax.experimental import pallas as pl
from jax.experimental.pallas import tpu as pltpu
from jax.sharding import Mesh
from jax.sharding import PartitionSpec as P

GROUP = 16
HIGH = lax.Precision.HIGHEST


def split_bf16(x):
    hi = x.astype(jnp.bfloat16)
    lo = (x - hi.astype(jnp.float32)).astype(jnp.bfloat16)
    return hi, lo


def dot_split(spec, weight, data):
    hi, lo = split_bf16(weight)
    return jnp.einsum(spec, hi, data, preferred_element_type=jnp.float32) + jnp.einsum(
        spec, lo, data, preferred_element_type=jnp.float32
    )


CYCLES = (
    (0, 1, 3, 2, 4, 5, 7, 6),
    (0, 1, 3, 5, 7, 6, 4, 2),
    (0, 1, 7, 5, 3, 2, 4, 6),
    (0, 1, 7, 6, 4, 5, 3, 2),
    (0, 2, 3, 1, 7, 5, 4, 6),
    (0, 2, 4, 5, 3, 1, 7, 6),
)


def lookup(table, v):
    n = len(table)
    total = 0
    for k, t in enumerate(table):
        if t:
            total = total + t * (1 - ((v - k + n) % n + n - 1) // n)
    return total


def ring_chip(r, n):
    hi = r // (n // 2)
    return 2 * (r + hi * (n - 1 - 2 * r)) + hi


def ring_pos(p, n):
    z, y = p // 2, p % 2
    return z + y * (n - 1 - 2 * z)


def rs_kernel(
    src_hbm, w_hbm, taps_hbm, q_ref, g_ref,
    src_ref, taps_ref, tok_buf, prior_buf, w_own, w_other, sbuf, rbuf, proj,
    tsend, trecv, psend, precv, send_sem, recv_sem, wsem, lsem,
):
    n, rows, _ = tok_buf.shape
    tail = prior_buf.shape[1]
    ext_len = rows + tail
    half, width = w_own.shape
    n_ring = sbuf.shape[0]
    chunk = width // n_ring
    chip = lax.axis_index("p")
    core = lax.axis_index("c")
    col = lax.axis_index("ch")
    other = 1 - core
    mesh_id = pl.DeviceIdType.MESH
    diag = chip == col
    cyc = CYCLES[0]
    r = lookup([cyc.index(p) for p in range(n)], chip)
    nxt = lookup(cyc, (r + 1) % n)
    prv = lookup(cyc, (r + n - 1) % n)

    src_load = pltpu.make_async_copy(src_hbm, src_ref, lsem.at[0])
    src_load.start()
    taps_load = pltpu.make_async_copy(taps_hbm, taps_ref, lsem.at[1])
    taps_load.start()
    barrier = pltpu.get_barrier_semaphore()
    for k in range(n):
        dest = (col, core, (chip + k) % n)
        srce = ((chip + k) % n, core, chip)
        if k == 0:
            @pl.when(jnp.logical_not(diag))
            def _():
                pl.semaphore_signal(barrier, 1, device_id=dest, device_id_type=mesh_id)
                pl.semaphore_signal(barrier, 1, device_id=srce, device_id_type=mesh_id)
        else:
            pl.semaphore_signal(barrier, 1, device_id=dest, device_id_type=mesh_id)
            pl.semaphore_signal(barrier, 1, device_id=srce, device_id_type=mesh_id)
        pl.semaphore_signal(
            barrier, 1, device_id=(col, other, (chip + k) % n), device_id_type=mesh_id
        )
        pl.semaphore_signal(
            barrier, 1, device_id=((chip + k) % n, other, chip), device_id_type=mesh_id
        )
    for nb in (nxt, prv):
        pl.semaphore_signal(barrier, 1, device_id=(nb, core, col), device_id_type=mesh_id)
    pl.semaphore_signal(barrier, 1, device_id=(chip, other, col), device_id_type=mesh_id)
    n_part, part_width = w_hbm.shape[0], w_hbm.shape[2]
    w_loads, w_swaps = [], []
    for j in range(n_part):
        w_cols = pl.ds(j * part_width, part_width)
        w_loads.append(pltpu.make_async_copy(w_hbm.at[j], w_own.at[:, w_cols], wsem.at[0, j]))
        w_loads[-1].start()
    pl.semaphore_wait(barrier, 4 * n + 3 - 2 * diag.astype(jnp.int32))
    src_load.wait()
    slot = (chip + core) % n
    tail_rows = src_ref.at[pl.ds(rows - tail, tail)]
    tcopies, pcopies = [], []
    for k in range(n):
        pcopy = pltpu.make_async_remote_copy(
            src_ref=tail_rows, dst_ref=prior_buf.at[slot], send_sem=psend.at[k],
            recv_sem=precv.at[slot], device_id=(col, other, (chip + k) % n),
            device_id_type=mesh_id,
        )
        pcopy.start()
        pcopies.append(pcopy)
    for k in range(n):
        dev = (col, core, (chip + k) % n)
        copy = pltpu.make_async_remote_copy(
            src_ref=src_ref, dst_ref=tok_buf.at[chip], send_sem=tsend.at[k],
            recv_sem=trecv.at[chip], device_id=dev, device_id_type=mesh_id,
        )
        if k == 0:
            own = pltpu.make_async_copy(src_ref, tok_buf.at[chip], trecv.at[chip])

            @pl.when(diag)
            def _():
                own.start()

            @pl.when(jnp.logical_not(diag))
            def _():
                copy.start()
        else:
            copy.start()
        tcopies.append(copy)

    for j in range(n_part):
        w_cols = pl.ds(j * part_width, part_width)
        w_swaps.append(
            pltpu.make_async_remote_copy(
                src_ref=w_hbm.at[j], dst_ref=w_other.at[:, w_cols], send_sem=wsem.at[1, j],
                recv_sem=wsem.at[2, j], device_id=(chip, other, col), device_id_type=mesh_id,
            )
        )
        w_swaps[-1].start()

    waited = set()

    def arrive(offset):
        if offset in waited:
            return
        waited.add(offset)
        blk = lookup(cyc, (r + offset) % n)
        pltpu.make_async_copy(src_ref, tok_buf.at[blk], trecv.at[blk]).wait()
        pltpu.make_async_copy(tail_rows, prior_buf.at[blk], precv.at[blk]).wait()

    for j in range(n_part):
        w_loads[j].wait()
        w_swaps[j].wait_recv()
    own_cols = pl.ds(pl.multiple_of(core * half, half), half)
    other_cols = pl.ds(pl.multiple_of((1 - core) * half, half), half)

    def part(blk, cols):
        def proj_rows(ref):
            return jnp.dot(
                ref[blk, :, own_cols], w_own[:, cols], preferred_element_type=jnp.float32
            ) + jnp.dot(ref[blk, :, other_cols], w_other[:, cols], preferred_element_type=jnp.float32)

        return jnp.concatenate([proj_rows(tok_buf), proj_rows(prior_buf)], axis=0)

    copies = [[] for _ in range(n_ring)]
    order = [h * (n_ring // 2) + k for k in range(n_ring // 2) for h in range(2)]
    for s in range(n - 1):
        for ring in order:
            fwd = ring < n_ring // 2
            arrive((n - 1 - s) % n if fwd else (1 + s) % n)
            d, dest = (1, nxt) if fwd else (-1, prv)
            cols = pl.ds(ring * chunk, chunk)
            q = lookup(cyc, (r - d * (1 + s) + 2 * n) % n)
            if s == 0:
                sbuf[ring, 0] = part(q, cols).astype(sbuf.dtype)
            else:
                mine = part(q, cols)
                copies[ring][s - 1].wait_recv()
                sbuf[ring, s] = (rbuf[ring, s - 1].astype(jnp.float32) + mine).astype(sbuf.dtype)
            copy = pltpu.make_async_remote_copy(
                src_ref=sbuf.at[ring, s],
                dst_ref=rbuf.at[ring, s],
                send_sem=send_sem.at[ring, s],
                recv_sem=recv_sem.at[ring, s],
                device_id=(dest, core, col),
                device_id_type=mesh_id,
            )
            copy.start()
            copies[ring].append(copy)
    arrive(0)
    for ring in range(n_ring):
        cols = pl.ds(ring * chunk, chunk)
        mine = part(chip, cols)
        copies[ring][-1].wait_recv()
        total = (rbuf[ring, n - 2].astype(jnp.float32) + mine).astype(jnp.bfloat16)
        total = total.astype(jnp.float32)
        proj[pl.ds(tail, rows), cols] = total[:rows]
        proj[pl.ds(0, tail), cols] = total[rows:]

    @pl.when(jnp.logical_and(chip == 0, core == 0))
    def _():
        proj[0:tail, :] = jnp.zeros((tail, width), jnp.float32)

    taps_load.wait()

    third = width // 3
    mixed = []
    for j in range(3):
        cols = pl.ds(j * third, third)
        mixed.append(
            taps_ref[0, j][None, :] * proj[pl.ds(2, rows), cols]
            + taps_ref[1, j][None, :] * proj[pl.ds(1, rows), cols]
            + taps_ref[2, j][None, :] * proj[pl.ds(0, rows), cols]
        )
    q_ref[...] = mixed[0]
    g_ref[...] = (mixed[1] * mixed[2]).astype(g_ref.dtype)
    for ring in range(n_ring):
        for copy in copies[ring]:
            copy.wait_send()
    for k in range(n):
        if k == 0:
            @pl.when(jnp.logical_not(diag))
            def _():
                tcopies[0].wait_send()
        else:
            tcopies[k].wait_send()
        pcopies[k].wait_send()
    for j in range(n_part):
        w_swaps[j].wait_send()


def project_and_gate(tokens, w_own, taps, n_ring=6, tail=2):
    rows, tok_width = tokens.shape
    n = lax.axis_size("p")
    ext_len = rows + tail
    n_part, half, part_width = w_own.shape
    width = n_part * part_width
    third = width // 3
    vmem = pl.BlockSpec(memory_space=pltpu.VMEM)
    return pl.pallas_call(
        rs_kernel,
        out_shape=(
            jax.ShapeDtypeStruct((rows, third), jnp.float32),
            jax.ShapeDtypeStruct((rows, third), jnp.bfloat16),
        ),
        in_specs=[pl.BlockSpec(memory_space=pl.ANY)] * 3,
        out_specs=(vmem, vmem),
        scratch_shapes=[
            pltpu.VMEM(tokens.shape, tokens.dtype),
            pltpu.VMEM(taps.shape, taps.dtype),
            pltpu.VMEM((n, rows, tok_width), tokens.dtype),
            pltpu.VMEM((n, tail, tok_width), tokens.dtype),
            pltpu.VMEM((half, width), w_own.dtype),
            pltpu.VMEM((half, width), w_own.dtype),
            pltpu.VMEM((n_ring, n - 1, ext_len, width // n_ring), jnp.bfloat16),
            pltpu.VMEM((n_ring, n - 1, ext_len, width // n_ring), jnp.bfloat16),
            pltpu.VMEM((ext_len, width), jnp.float32),
        ]
        + [pltpu.SemaphoreType.DMA((n,))] * 4
        + [pltpu.SemaphoreType.DMA((n_ring, n - 1))] * 2
        + [pltpu.SemaphoreType.DMA((3, n_part)), pltpu.SemaphoreType.DMA((2,))],
        compiler_params=pltpu.CompilerParams(
            collective_id=0, has_side_effects=True, vmem_limit_bytes=67043328
        ),
    )(tokens, w_own, taps)


def tok_kernel(src_ref, out_ref, prior_ref, send_sem, recv_sem, psend_sem, precv_sem):
    n, rows, _ = out_ref.shape
    tail = prior_ref.shape[1]
    chip = lax.axis_index("p")
    core = lax.axis_index("c")
    col = lax.axis_index("ch")
    other = 1 - core
    mesh_id = pl.DeviceIdType.MESH
    diag = chip == col
    src_load = pltpu.make_async_copy(src_hbm, src_ref, lsem.at[0])
    src_load.start()
    taps_load = pltpu.make_async_copy(taps_hbm, taps_ref, lsem.at[1])
    taps_load.start()
    barrier = pltpu.get_barrier_semaphore()
    for k in range(n):
        dest = (col, core, (chip + k) % n)
        srce = ((chip + k) % n, core, chip)
        if k == 0:
            @pl.when(jnp.logical_not(diag))
            def _():
                pl.semaphore_signal(barrier, 1, device_id=dest, device_id_type=mesh_id)
                pl.semaphore_signal(barrier, 1, device_id=srce, device_id_type=mesh_id)
        else:
            pl.semaphore_signal(barrier, 1, device_id=dest, device_id_type=mesh_id)
            pl.semaphore_signal(barrier, 1, device_id=srce, device_id_type=mesh_id)
        pl.semaphore_signal(
            barrier, 1, device_id=(col, other, (chip + k) % n), device_id_type=mesh_id
        )
        pl.semaphore_signal(
            barrier, 1, device_id=((chip + k) % n, other, chip), device_id_type=mesh_id
        )
    pl.semaphore_wait(barrier, 4 * n - 2 * diag.astype(jnp.int32))
    slot = (chip + core) % n
    copies = []
    for k in range(n):
        copy = pltpu.make_async_remote_copy(
            src_ref=src_ref,
            dst_ref=out_ref.at[chip],
            send_sem=send_sem.at[k],
            recv_sem=recv_sem.at[chip],
            device_id=(col, core, (chip + k) % n),
            device_id_type=mesh_id,
        )
        if k == 0:
            own = pltpu.make_async_copy(src_ref, out_ref.at[chip], recv_sem.at[chip])

            @pl.when(diag)
            def _():
                own.start()

            @pl.when(jnp.logical_not(diag))
            def _():
                copy.start()
        else:
            copy.start()
        copies.append(copy)
    pcopies = []
    for k in range(n):
        pcopy = pltpu.make_async_remote_copy(
            src_ref=src_ref.at[pl.ds(rows - tail, tail)],
            dst_ref=prior_ref.at[slot],
            send_sem=psend_sem.at[k],
            recv_sem=precv_sem.at[slot],
            device_id=(col, other, (chip + k) % n),
            device_id_type=mesh_id,
        )
        pcopy.start()
        pcopies.append(pcopy)
    for j in range(n):
        pltpu.make_async_copy(src_ref, out_ref.at[j], recv_sem.at[j]).wait()
        pltpu.make_async_copy(
            src_ref.at[pl.ds(rows - tail, tail)], prior_ref.at[j], precv_sem.at[j]
        ).wait()
    for k in range(n):
        if k == 0:
            @pl.when(jnp.logical_not(diag))
            def _():
                copies[0].wait_send()
        else:
            copies[k].wait_send()
        pcopies[k].wait_send()


def spread_tokens(tokens, n, tail=2):
    rows, width = tokens.shape
    vmem = pl.BlockSpec(memory_space=pltpu.VMEM)
    return pl.pallas_call(
        tok_kernel,
        out_shape=(
            jax.ShapeDtypeStruct((n, rows, width), tokens.dtype),
            jax.ShapeDtypeStruct((n, tail, width), tokens.dtype),
        ),
        in_specs=[vmem],
        out_specs=(vmem, vmem),
        scratch_shapes=[pltpu.SemaphoreType.DMA((n,))] * 4,
        compiler_params=pltpu.CompilerParams(collective_id=1, has_side_effects=True),
    )(tokens)


def state_kernel(src_ref, lam_ref, out_ref, got, fac, send_sem, recv_sem, block_len):
    n = got.shape[0]
    n_core = lax.axis_size("c")
    me = lax.axis_index("p") * n_core + lax.axis_index("c")
    col = lax.axis_index("ch")
    mesh_id = pl.DeviceIdType.MESH
    barrier = pltpu.get_barrier_semaphore()
    for k in range(1, n):
        other = (me + k) % n
        pl.semaphore_signal(
            barrier, 1, device_id=(other // n_core, other % n_core, col), device_id_type=mesh_id
        )
    for j in range(n):
        @pl.when(j >= me)
        def _():
            got[j] = jnp.zeros(got.shape[1:], got.dtype)

        gap = jnp.maximum(me - 1 - j, 0).astype(jnp.float32)
        fac[j] = jnp.exp(-lam_ref[...] * (block_len * gap))
    pl.semaphore_wait(barrier, n - 1)
    copies = []
    for k in range(1, n):
        other = me + k
        copy = pltpu.make_async_remote_copy(
            src_ref=src_ref,
            dst_ref=got.at[me],
            send_sem=send_sem.at[k],
            recv_sem=recv_sem.at[me],
            device_id=(other // n_core, other % n_core, col),
            device_id_type=mesh_id,
        )

        @pl.when(other < n)
        def _():
            copy.start()

        copies.append((other, copy))
    for j in range(n):
        @pl.when(j < me)
        def _():
            pltpu.make_async_copy(src_ref, got.at[j], recv_sem.at[j]).wait()
    acc = jnp.zeros(out_ref.shape, jnp.float32)
    for j in range(n):
        acc = acc + fac[j] * got[j]
    out_ref[...] = acc
    for other, copy in copies:
        @pl.when(other < n)
        def _():
            copy.wait_send()


def gather_earlier(state, lam, n, block_len):
    vmem = pl.BlockSpec(memory_space=pltpu.VMEM)
    return pl.pallas_call(
        functools.partial(state_kernel, block_len=float(block_len)),
        out_shape=jax.ShapeDtypeStruct(state.shape, state.dtype),
        in_specs=[vmem, vmem],
        out_specs=vmem,
        scratch_shapes=[
            pltpu.VMEM((n,) + state.shape, state.dtype),
            pltpu.VMEM((n,) + state.shape, jnp.float32),
            pltpu.SemaphoreType.DMA((n,)),
            pltpu.SemaphoreType.DMA((n,)),
        ],
        compiler_params=pltpu.CompilerParams(collective_id=2, has_side_effects=True),
    )(state, lam)


def local(tokens, w_in, short_filter, decay_rate, residue, skip):
    n_chip = lax.axis_size("p")
    block_len = tokens.shape[0]
    local_width = w_in.shape[2]
    group_count = local_width // GROUP
    chip = lax.axis_index("p")
    core = lax.axis_index("c")
    col = lax.axis_index("ch")

    n_col = lax.axis_size("ch")
    w_parts = jnp.transpose(w_in, (1, 0, 2))
    query, gated = project_and_gate(tokens, w_parts, short_filter)
    x = gated.reshape(block_len, group_count, GROUP)

    pole_weight = residue * jnp.sqrt(2.0 * decay_rate)
    pos = jnp.arange(block_len, dtype=jnp.float32)
    lam = decay_rate[:, None, :]
    a_mat = pole_weight[:, None, :] * jnp.exp(-lam * pos[None, :, None])
    b_mat = jnp.exp(lam * pos[None, :, None])
    toep = jnp.einsum("gtr,gsr->gts", a_mat, b_mat, precision=lax.Precision.HIGH)
    causal = pos[:, None] >= pos[None, :]
    toep = jnp.where(causal[None], toep, 0.0)
    near = dot_split("gts,sgc->tgc", toep, x)

    e_mat = jnp.exp(-lam * (block_len - 1 - pos)[None, :, None])
    s_loc = dot_split("gsr,sgc->grc", e_mat, x)
    n_ctx = n_chip * lax.axis_size("c")
    me = chip * lax.axis_size("c") + core
    s_flat = s_loc.reshape(group_count, -1)
    lam_b = jnp.broadcast_to(decay_rate[..., None], decay_rate.shape + (GROUP,))
    s_in = gather_earlier(s_flat, lam_b.reshape(group_count, -1), n_ctx, block_len)
    s_in = s_in.reshape(s_loc.shape)
    f_mat = pole_weight[:, None, :] * jnp.exp(-lam * (pos + 1.0)[None, :, None])
    far = jnp.einsum("gtr,grc->tgc", f_mat, s_in, precision=HIGH)
    long_out = (near + far).reshape(block_len, local_width)
    out = query * (long_out + skip * gated.astype(jnp.float32))
    return out.astype(jnp.bfloat16)


def solution(mesh):
    n_ctx, n_ch = mesh.devices.shape
    sub = Mesh(mesh.devices.reshape(n_ctx // 2, 2, n_ch), ("p", "c", "ch"))
    ctx = ("p", "c")
    return jax.shard_map(
        local,
        mesh=sub,
        in_specs=(
            P(ctx, "ch"),
            P(ctx, None, "ch"),
            P(None, None, "ch"),
            P("ch", None),
            P("ch", None),
            P("ch"),
        ),
        out_specs=P(ctx, "ch"),
        check_vma=False,
    )
```
